256 devices in a mesh: leaf: 64 (over z, x, core), col: 4 (over y).
Axes of the slice: x: 4, y: 4, z: 8, core: 2. Of those that a mesh axis runs over, the one named last changes fastest.
Arguments:
- points: float32 [65536, 128], P(('leaf', 'col')), may hold values from -6 to 6
- coefs: float32 [65536, 512], P(('leaf', 'col')), may hold values from -6 to 6
- targets: float32 [65536, 512], P(('leaf', 'col')), may hold values from -6 to 6
- ridge: float32 [1], replicated, may hold values from 0.5 to 2
- tile_mask: int32 [64, 5], P('leaf'), may hold values from 0 to 1, as said below
- cluster_perm: int32 [64, 1024], P('leaf'), may hold values from 0 to 1023, each once within a row
- leaf_map: int32 [64], replicated, may hold values from 0 to 63, as said below
- leaf_inverse: float32 [64, 1024, 1024], P('leaf'), may hold values from -0.25 to 1.3
- leaf_basis: float32 [64, 1024, 256], P('leaf'), may hold values from -0.1875 to 0.1875
- node_inverse: float32 [64, 336, 1024], P('leaf'), may hold values from -0.25 to 1.3
- node_transfer: float32 [64, 336, 256], P('leaf'), may hold values from -0.1875 to 0.1875
Outputs:
- residual: float32 [65536, 512], P(('leaf', 'col'))
- new_coef: float32 [65536, 512], P(('leaf', 'col'))
The draws below stay inside these ranges and needn't reach their ends.
Inputs may be any that keep to these rules, and one draw needn't show every extreme that they name: `tile_mask`: entry k of row i is 1 when block i has a nonzero tile with block i + k - 2; entry 2 is always 1, entries naming a block outside 0 .. 63 are 0, and some row lists all 5 tiles. `cluster_perm`: each row is a permutation of 0 .. 1023. `leaf_map`: a permutation of 0 .. 63 that sends the tree leaves 4 n .. 4 n + 3 to the blocks 4 n .. 4 n + 3.
All inputs are finite; a program needn't handle non-finite values.
Results may differ from the reference program's by a relative error of at most 0.0003.
Values sent between devices are 32-bit elements; how exact they have to be, the bound alone decides.
No kernel may reach another device: no remote copies, remote signals or barrier semaphores. Data moves between devices by JAX's collectives and lax.ppermute only.
A program may use at most 128 MiB of HBM per device.

```python
import math
import jax
import jax.numpy as jnp
from jax import lax

F = 128
R = 512
LEAF = 1024
RANK = 256
WIN = 2
LEAVES = 64
NPTS = 65536
SLICE_ROWS = 336


def slice_layout(remaining, rank_size):
    layout = []
    covered = 1
    while remaining > 1:
        children = 4 if remaining % 4 == 0 else remaining
        covered = covered * children
        remaining = remaining // children
        layout.append((covered, children * rank_size // covered))
    return layout


def diagonal_heavy(key, count, order_size):
    first_key, second_key = jax.random.split(key)
    identity = jnp.eye(order_size, dtype=jnp.float32)
    diagonal = jax.random.uniform(first_key, (count, order_size), jnp.float32, 0.6, 1.2)
    spread = jnp.clip(jax.random.normal(second_key, (count, order_size, order_size), jnp.float32), -4.0, 4.0)
    scaled = spread * (0.3 * order_size ** (-0.5))
    return scaled * (1.0 - identity) + diagonal[:, :, None] * identity


def draw_leaf_inverse(key, part):
    return diagonal_heavy(jax.random.fold_in(key, 11), LEAVES, LEAF)


def draw_node_inverse(key, part):
    first_key, second_key = jax.random.split(jax.random.fold_in(key, 23))
    order_size = 4 * RANK
    targets_list = []
    for covered, slice_count in slice_layout(LEAVES, RANK):
        device = jnp.arange(LEAVES, dtype=jnp.int32)[:, None]
        local = jnp.arange(slice_count, dtype=jnp.int32)[None, :]
        targets_list.append(device % covered * slice_count + local)
    target = jnp.concatenate(targets_list, axis=1)
    slice_total = target.shape[1]
    diagonal = jax.random.uniform(first_key, (LEAVES, slice_total), jnp.float32, 0.6, 1.2)
    spread = jnp.clip(jax.random.normal(second_key, (LEAVES, slice_total, order_size), jnp.float32), -4.0, 4.0)
    columns = jnp.arange(order_size, dtype=jnp.int32)[None, None, :]
    on_diagonal = columns == target[:, :, None]
    return jnp.where(on_diagonal, diagonal[:, :, None], spread * (0.3 * order_size ** (-0.5)))


def draw_tile_mask(key, part):
    first_key, second_key, third_key = jax.random.split(jax.random.fold_in(key, 5), 3)
    density = jax.random.randint(first_key, (LEAVES, 1), 1, 5)
    coins = jax.random.randint(second_key, (LEAVES, 2 * WIN + 1), 0, 4)
    full_row = jax.random.randint(third_key, (), WIN, LEAVES - WIN)
    rows = jnp.arange(LEAVES, dtype=jnp.int32)[:, None]
    slots = jnp.arange(2 * WIN + 1, dtype=jnp.int32)[None, :]
    target_block = rows + slots - WIN
    inside = (target_block >= 0) & (target_block < LEAVES)
    chosen = (coins < density) | (slots == WIN) | (rows == full_row)
    return (chosen & inside).astype(jnp.int32)


def draw_leaf_map(key, part):
    group_keys = jax.random.split(jax.random.fold_in(key, 7), LEAVES // 4)
    shuffles = jax.vmap(lambda group_key: jax.random.permutation(group_key, 4).astype(jnp.int32))(group_keys)
    offsets = 4 * jnp.arange(LEAVES // 4, dtype=jnp.int32)[:, None]
    return (shuffles + offsets).reshape(LEAVES).astype(jnp.int32)


def level_of(stream_key, dims, cuts, smallest, top_value):
    loudness, own = 1.0, jax.random.fold_in(stream_key, 6)
    for axis_at, shards_of in cuts:
        draws = jnp.exp(jax.random.uniform(jax.random.fold_in(own, axis_at), (shards_of,), jnp.float32, smallest / len(cuts), top_value / len(cuts)))
        loudness = loudness * jnp.repeat(draws, dims[axis_at] // shards_of).reshape([-1 if axis == axis_at else 1 for axis in range(len(dims))])
    return loudness


def scatter_about(own_key, extent, width, bound, shards=(), held_as=jnp.bfloat16):
    array = width * jax.random.normal(own_key, extent, jnp.float32)
    if shards:
        array = array * level_of(own_key, extent, shards, -0.22, 0.18)
    return jnp.clip(array, -bound, bound).astype(held_as)


def setup_inputs(seed: int = 0) -> dict:
    streams_of = jax.random.split(jax.random.key(seed), 12)
    points = scatter_about(streams_of[0], (NPTS, F), 1.0, 6.0, ((0, 256),), jnp.float32)
    coefs = scatter_about(streams_of[1], (NPTS, R), 1.0, 6.0, ((0, 256),), jnp.float32)
    targets = scatter_about(streams_of[2], (NPTS, R), 1.0, 6.0, ((0, 256),), jnp.float32)
    ridge = jnp.clip(jnp.exp(jax.random.uniform(streams_of[3], (1,), jnp.float32, math.log(0.5), math.log(2.0))), 0.5, 2.0)
    tile_mask = draw_tile_mask(jax.random.fold_in(streams_of[11], 71), 0)
    cluster_perm = jax.vmap(lambda own: jax.random.permutation(own, LEAF))(jax.random.split(streams_of[5], LEAVES)).reshape((LEAVES, LEAF)).astype(jnp.int32)
    leaf_map = draw_leaf_map(jax.random.fold_in(streams_of[11], 71), 0)
    leaf_inverse = draw_leaf_inverse(jax.random.fold_in(streams_of[11], 71), 0)
    leaf_basis = scatter_about(streams_of[8], (LEAVES, LEAF, RANK), (4 * RANK) ** -0.5, 0.1875, ((0, 64),), jnp.float32)
    node_inverse = draw_node_inverse(jax.random.fold_in(streams_of[11], 71), 0)
    node_transfer = scatter_about(streams_of[10], (LEAVES, SLICE_ROWS, RANK), (4 * RANK) ** -0.5, 0.1875, ((0, 64),), jnp.float32)
    return {"points": points, "coefs": coefs, "targets": targets, "ridge": ridge, "tile_mask": tile_mask, "cluster_perm": cluster_perm, "leaf_map": leaf_map, "leaf_inverse": leaf_inverse, "leaf_basis": leaf_basis, "node_inverse": node_inverse, "node_transfer": node_transfer}


highest = lax.Precision.HIGHEST


def kernel_tile(row_points, row_squares, column_points, column_squares):
    inner_products = jnp.einsum("pf,qf->pq", row_points, column_points, precision=highest)
    distance = row_squares[:, None] + column_squares[None, :] - 2.0 * inner_products
    return jnp.exp(distance * (-2.0 / row_points.shape[1]))


def tree_levels(remaining, rank_size):
    levels = []
    covered = 1
    height = 1
    offset = 0
    while remaining > 1:
        children = 4 if remaining % 4 == 0 else remaining
        covered = covered * children
        remaining = remaining // children
        slice_count = children * rank_size // covered
        levels.append((height, children, covered, offset, slice_count))
        offset = offset + slice_count
        height = height + 1
    return levels


def reference(points, coefs, targets, ridge, tile_mask, cluster_perm, leaf_map, leaf_inverse, leaf_basis, node_inverse, node_transfer):
    perm_index = cluster_perm[:, :, None]
    ordered_x = jnp.take_along_axis(points.reshape(LEAVES, LEAF, F), perm_index, axis=1)
    ordered_a = jnp.take_along_axis(coefs.reshape(LEAVES, LEAF, R), perm_index, axis=1)
    ordered_y = jnp.take_along_axis(targets.reshape(LEAVES, LEAF, R), perm_index, axis=1)
    squares = jnp.sum(ordered_x * ordered_x, axis=2)

    def block_residual(block):
        tile_total = jnp.zeros((LEAF, R), jnp.float32)
        for band_slot in range(2 * WIN + 1):
            other = jnp.clip(block + band_slot - WIN, 0, LEAVES - 1).astype(jnp.int32)
            kernel = kernel_tile(ordered_x[block], squares[block], ordered_x[other], squares[other])
            term = jnp.dot(kernel, ordered_a[other], precision=highest)
            tile_total = tile_total + jnp.where(tile_mask[block, band_slot] > 0, term, jnp.zeros_like(term))
        return ordered_y[block] - ridge[0] * ordered_a[block] - tile_total

    residual_c = lax.map(block_residual, jnp.arange(LEAVES, dtype=jnp.int32))
    solved = jnp.einsum("bpq,bqc->bpc", leaf_inverse, residual_c, precision=highest)
    reduced = jnp.einsum("bpr,bpc->brc", leaf_basis, solved, precision=highest)
    current = reduced[leaf_map]
    stored = []
    slice_total = node_inverse.shape[1]
    levels = tree_levels(LEAVES, RANK)
    for height, children, covered, offset, slice_count in levels:
        node_count = current.shape[0] // children
        node_rows = children * RANK
        stacked = current.reshape(node_count, node_rows, R)
        node_inv = node_inverse.reshape(node_count, covered, slice_total, 4 * RANK)[:, :, offset:offset + slice_count, :node_rows].reshape(node_count, node_rows, node_rows)
        transfer_rows = node_transfer.reshape(node_count, covered, slice_total, RANK)[:, :, offset:offset + slice_count, :].reshape(node_count, node_rows, RANK)
        weights = jnp.einsum("nab,nbc->nac", node_inv, stacked, precision=highest)
        stored.append((weights, node_inv, transfer_rows))
        current = jnp.einsum("nar,nac->nrc", transfer_rows, weights, precision=highest)
    values = stored[-1][0]
    for position in range(len(levels) - 2, -1, -1):
        weights, node_inv, transfer_rows = stored[position]
        pieces = values.reshape(weights.shape[0], RANK, R)
        lifted = jnp.einsum("nar,nrc->nac", transfer_rows, pieces, precision=highest)
        values = weights - jnp.einsum("nab,nbc->nac", node_inv, lifted, precision=highest)
    leaf_pieces = values.reshape(LEAVES, RANK, R)
    inverse_map = jnp.zeros((LEAVES,), jnp.int32).at[leaf_map].set(jnp.arange(LEAVES, dtype=jnp.int32))
    pieces = leaf_pieces[inverse_map]
    lifted = jnp.einsum("bpr,brc->bpc", leaf_basis, pieces, precision=highest)
    correction = jnp.einsum("bpq,bqc->bpc", leaf_inverse, lifted, precision=highest)
    fresh = ordered_a + (solved - correction)

    def invert_row(row_perm):
        return jnp.zeros((LEAF,), jnp.int32).at[row_perm].set(jnp.arange(LEAF, dtype=jnp.int32))

    back_index = jax.vmap(invert_row)(cluster_perm)[:, :, None]
    residual = jnp.take_along_axis(residual_c, back_index, axis=1).reshape(NPTS, R)
    new_coef = jnp.take_along_axis(fresh, back_index, axis=1).reshape(NPTS, R)
    return residual, new_coef
```

```python
import jax
import jax.numpy as jnp
from jax import lax
from jax.experimental import pallas as pl
from jax.experimental.pallas import tpu as pltpu
from jax.sharding import PartitionSpec as P

HIGH = lax.Precision.HIGH
HIGHEST = lax.Precision.HIGHEST
Q = 256
RANK = 256
LEAVES = 64


def leaf_at(z, x_hi, kappa):
    x = 2 * x_hi + ((kappa >> 1) ^ x_hi)
    return z * 8 + x * 2 + (kappa & 1)


G4 = [[4 * n + k for k in range(4)] for n in range(16)]
GK = [[leaf_at(z, xh, k) for k in range(4)] for z in range(8) for xh in range(2)]


def facing(i, flip_x, flip_z):
    z, x, core = i // 8, i // 2 % 4, i % 2
    return (z ^ flip_z) * 8 + (3 - x if flip_x else x) * 2 + core


def leaf_route(value, target):
    return lax.ppermute(value, "leaf", [(i, target(i)) for i in range(LEAVES)])


def siblings(value):
    return [value] + [
        leaf_route(value, lambda i, d=d: facing(i, d & 1, d >> 1)) for d in (1, 2, 3)
    ]


def z_from(value, even, odd):
    route = []
    for i in range(LEAVES):
        step = odd if i // 8 % 2 else even
        route.append(((i + 8 * step) % LEAVES, i))
    return lax.ppermute(value, "leaf", route)


def leaf_xor(value, bit):
    return lax.ppermute(value, "leaf", [(i, i ^ bit) for i in range(LEAVES)])


def leaf_from(value, step):
    return lax.ppermute(value, "leaf", [((i + step) % LEAVES, i) for i in range(LEAVES)])


def col_shift(value, step):
    return lax.ppermute(value, "col", [(i, (i + step) % 4) for i in range(4)])


def mm(a, b, dims, precision=HIGH):
    return lax.dot_general(
        a, b, (dims, ((), ())), precision=precision, preferred_element_type=jnp.float32
    )


def halves(value):
    top = lax.reduce_precision(value, 8, 7)
    return top.astype(jnp.bfloat16), (value - top).astype(jnp.bfloat16)


def gather4(value, groups):
    return lax.all_gather(value, "leaf", axis=0, axis_index_groups=groups)


def pair(mine, other, bit):
    return jnp.where(bit == 0, mine, other), jnp.where(bit == 0, other, mine)


def group_rows(value, x_lo, core):
    mine = jnp.stack(pair(value, leaf_xor(value, 2), x_lo))
    low, high = pair(mine, leaf_xor(mine, 1), core)
    return jnp.stack([low[0], high[0], low[1], high[1]])


def dot(a, b, dims=((1,), (0,))):
    return lax.dot_general(a, b, (dims, ((), ())), preferred_element_type=jnp.float32)


def split(value):
    top = value.astype(jnp.bfloat16)
    return top, (value - top.astype(jnp.float32)).astype(jnp.bfloat16)


def tile_sum(x, blocks, weights, tops, lows):
    squares = jnp.sum(x * x, axis=1, keepdims=True)
    ones = jnp.ones((8, 128), jnp.float32)
    total = None
    for k, (block, weight) in enumerate(zip(blocks, weights)):
        y = block[...]
        inner = lax.dot_general(
            x, y, (((1,), (1,)), ((), ())), precision=HIGHEST, preferred_element_type=jnp.float32
        )
        other = lax.dot_general(
            ones,
            y * y,
            (((1,), (1,)), ((), ())),
            precision=HIGHEST,
            preferred_element_type=jnp.float32,
        )[:1]
        distance = squares + other - 2.0 * inner
        top, low = split(jnp.exp(distance * (-2.0 / 128.0)) * weight)
        term = dot(top, tops[k]) + dot(top, lows[k]) + dot(low, tops[k])
        total = term if total is None else total + term
    return total


def near_kernel(mask, side, x0, x1, x2, x3, bx, ay, by, out, rows, tops, lows):
    i = pl.program_id(0)

    @pl.when(i == 0)
    def _():
        for k, ref in enumerate((x0, x1, x2, x3)):
            rows[k] = ref[...]
        for k, ref in enumerate((ay, by)):
            tops[k], lows[k] = split(ref[...])

    weights = (mask[0, 2].astype(jnp.float32), mask[0, 3 - 2 * side[0]].astype(jnp.float32))
    out[...] = tile_sum(rows[i], (x0, bx), weights, tops, lows)


def far_kernel(
    mask, side, ridge, x0, x1, x2, x3, bx, cx, dx, by, cy, dy, near, own_y, own_a, lead,
    out, led, rows, tops, lows,
):
    i = pl.program_id(0)

    @pl.when(i == 0)
    def _():
        for k, ref in enumerate((x0, x1, x2, x3)):
            rows[k] = ref[...]
        for k, ref in enumerate((by, cy, dy)):
            tops[k], lows[k] = split(ref[...])

    weights = (
        mask[0, 0].astype(jnp.float32),
        mask[0, 4].astype(jnp.float32),
        mask[0, 1 + 2 * side[0]].astype(jnp.float32),
    )
    total = near[...] + tile_sum(rows[i], (bx, cx, dx), weights, tops, lows)
    own = own_y[...] - ridge[0] * own_a[...]
    part = jnp.where(i == 0, own - total, -total)
    out[...] = part
    top, low = split(part)
    a, b = split(lead[...])
    product = dot(a, top) + dot(a, low) + dot(b, top)
    for k in range(4):
        piece = product[:, k * 128 : (k + 1) * 128]
        led[k] = jnp.where(i == 0, piece, led[k] + piece)


SMALL = pl.BlockSpec(memory_space=pltpu.SMEM)


def whole(*shape):
    return pl.BlockSpec(shape, lambda i: (0,) * len(shape))


def near_call(mask, side, xs, bx, ay, by):
    return pl.pallas_call(
        near_kernel,
        grid=(4,),
        in_specs=[SMALL, SMALL] + [whole(Q, 128)] * 5 + [whole(Q, 512)] * 2,
        out_specs=pl.BlockSpec((Q, 512), lambda i: (i, 0)),
        out_shape=jax.ShapeDtypeStruct((1024, 512), jnp.float32),
        scratch_shapes=[
            pltpu.VMEM((4, Q, 128), jnp.float32),
            pltpu.VMEM((2, Q, 512), jnp.bfloat16),
            pltpu.VMEM((2, Q, 512), jnp.bfloat16),
        ],
        name="near",
    )(mask, side, *xs, bx, ay, by)


def far_call(mask, side, ridge, xs, others_x, others_a, near, own_y, own_a, lead):
    return pl.pallas_call(
        far_kernel,
        grid=(4,),
        in_specs=[SMALL, SMALL, SMALL]
        + [whole(Q, 128)] * 7
        + [whole(Q, 512)] * 3
        + [pl.BlockSpec((Q, 512), lambda i: (i, 0))]
        + [whole(Q, 512)] * 2
        + [pl.BlockSpec((RANK, Q), lambda i: (0, i))],
        out_specs=[pl.BlockSpec((Q, 512), lambda i: (i, 0)), whole(4, RANK, 128)],
        out_shape=[
            jax.ShapeDtypeStruct((1024, 512), jnp.float32),
            jax.ShapeDtypeStruct((4, RANK, 128), jnp.float32),
        ],
        scratch_shapes=[
            pltpu.VMEM((4, Q, 128), jnp.float32),
            pltpu.VMEM((3, Q, 512), jnp.bfloat16),
            pltpu.VMEM((3, Q, 512), jnp.bfloat16),
        ],
        name="far",
    )(mask, side, ridge, *xs, *others_x, *others_a, near, own_y, own_a, lead)


def local(
    points,
    coefs,
    targets,
    ridge,
    tile_mask,
    cluster_perm,
    leaf_map,
    leaf_inverse,
    leaf_basis,
    node_inverse,
    node_transfer,
):
    col = lax.axis_index("col")
    leaf = lax.axis_index("leaf")
    core = leaf % 2
    x_lo = leaf // 2 % 2
    group_base = leaf // 4 * 4

    child = leaf // 4 % 4
    parent = leaf // 16

    xs = [points] + [col_shift(points, d) for d in (1, 2, 3)]
    left_x, right_x = leaf_from(points, -2), leaf_from(points, 2)
    left_a, right_a = leaf_from(coefs, -2), leaf_from(coefs, 2)
    partner_x, partner_a = leaf_xor(points, 1), leaf_xor(coefs, 1)
    relay_x = leaf_xor(jnp.where(core == 0, right_x, left_x), 1)
    relay_a = leaf_xor(jnp.where(core == 0, right_a, left_a), 1)

    held = lax.optimization_barrier((node_transfer[0, :320], node_inverse[0, 256:336], relay_a))
    transfers = group_rows(held[0], x_lo, core)
    inverses = group_rows(held[1], x_lo, core)

    solve = leaf_inverse[0]
    basis = leaf_basis[0]
    order = cluster_perm[0]
    at = jnp.arange(1024, dtype=jnp.int32)
    turned = (col - at // Q) % 4 * Q + at % Q
    pick_turned = (order[:, None] == turned[None, :]).astype(jnp.bfloat16)
    pick = (order[:, None] == at[None, :]).astype(jnp.bfloat16)

    def select(value, picks, dims):
        a, b = halves(value)
        return mm(a, picks, dims, None) + mm(b, picks, dims, None)

    lead = select(mm(basis, solve, ((0,), (0,))), pick_turned, ((1,), (0,)))
    slots = lax.dynamic_slice_in_dim(leaf_map, group_base, 4, 0) - group_base
    four = jnp.arange(4, dtype=jnp.int32)
    slot_of = jnp.sum(four[:, None] * (slots[:, None] == four[None, :]), axis=0)
    m1 = node_inverse[0, :256]
    e1 = node_transfer[0, :256]
    m1_blocks = m1.reshape(RANK, 4, RANK)[:, slot_of]

    side = core.astype(jnp.int32).reshape(1)
    near = near_call(tile_mask, side, xs, partner_x, coefs, partner_a)
    partial, led = far_call(
        tile_mask,
        side,
        ridge,
        xs,
        (left_x, right_x, relay_x),
        (left_a, right_a, relay_a),
        near,
        targets,
        coefs,
        lead,
    )
    led = lax.all_to_all(led, "col", 0, 0, tiled=True)
    reduced = led.sum(0)

    part, late_basis, _ = lax.optimization_barrier((partial, basis, reduced))
    tail = select(mm(solve, late_basis, ((1,), (0,))), pick, ((0,), (0,)))
    mine = lax.dynamic_slice_in_dim(part, col * 128, 128, 1)
    for d in (1, 2, 3):
        sent = lax.dynamic_slice_in_dim(part, (col + d) % 4 * 128, 128, 1)
        mine = mine + jnp.roll(col_shift(sent, d), d * Q, axis=0)
    pieces = [mine[:Q]] + [col_shift(mine[k * Q : (k + 1) * Q], -k) for k in (1, 2, 3)]
    wide = jnp.concatenate(pieces + pieces[:3], axis=1)
    residual = lax.dynamic_slice_in_dim(wide, (4 - col) % 4 * 128, 512, 1)
    ordered = select(mine, pick_turned, ((0,), (1,)))
    solved = mm(ordered, solve, ((1,), (1,)))
    solved = select(solved, pick, ((1,), (0,))).T

    stacked = gather4(reduced, G4)
    w1 = sum(mm(m1_blocks[:, b], stacked[b], ((1,), (0,))) for b in range(4))
    p1 = mm(w1, e1, ((0,), (0,)))
    p1 = lax.all_to_all(p1, "leaf", 0, 0, axis_index_groups=GK, tiled=True)
    r1 = p1.reshape(4, 32, RANK).sum(0)
    turn = jnp.arange(4, dtype=jnp.int32) ^ child
    m2 = inverses[:, :64].reshape(RANK, 4, RANK)[:, turn]
    e2 = transfers[:, 256:320].reshape(RANK, RANK)
    e2_turned = e2.reshape(RANK, 4, 64)[:, turn]
    near_m = jnp.where(leaf // 8 % 2 == 0, jnp.array([0, 3, 1, 2]), jnp.array([0, 1, 3, 2]))
    m3 = inverses[:, 64:80].reshape(64, 4, RANK)[:, (parent + near_m) % 4]
    f1 = mm(m1, transfers[:, :256].reshape(1024, RANK), ((1,), (0,)))

    def blocks(values, matrix):
        return sum(mm(values[n], matrix[:, n], ((1,), (1,))) for n in range(4))

    w2 = blocks(siblings(r1), m2)
    r2 = sum(siblings(mm(w2, e2, ((1,), (0,)))))
    r2s = [r2, z_from(r2, -1, 1), z_from(r2, 2, -2), z_from(r2, -3, 3)]
    g2 = siblings(blocks(r2s, m3))
    lifted = blocks(g2, e2_turned)
    g1 = w2 - blocks(siblings(lifted), m2)
    g1 = gather4(g1, GK).reshape(128, RANK)
    v1 = w1 - mm(f1, g1, ((1,), (1,)))
    v1s = gather4(v1, G4)
    slot = jnp.sum(four * (slots == leaf - group_base))
    g = lax.dynamic_index_in_dim(v1s, slot, 0, keepdims=False)

    delta = solved - mm(tail, g, ((0,), (0,)))
    delta = lax.all_to_all(delta, "col", 0, 1, tiled=True)
    return residual, coefs + delta


def solution(mesh):
    return jax.shard_map(
        local,
        mesh=mesh,
        in_specs=(
            P(("leaf", "col"), None),
            P(("leaf", "col"), None),
            P(("leaf", "col"), None),
            P(),
            P("leaf", None),
            P("leaf", None),
            P(),
            P("leaf", None, None),
            P("leaf", None, None),
            P("leaf", None, None),
            P("leaf", None, None),
        ),
        out_specs=(P(("leaf", "col"), None), P(("leaf", "col"), None)),
        check_vma=False,
    )
```

```python
import jax
import jax.numpy as jnp
from jax import lax
from jax.experimental import pallas as pl
from jax.experimental.pallas import tpu as pltpu
from jax.sharding import PartitionSpec as P


HIGH = lax.Precision.HIGH
HIGHEST = lax.Precision.HIGHEST
F32 = jnp.float32
BF16 = jnp.bfloat16
Q = 256
RANK = 256
LEAVES = 64


def leaf_at(z, x_hi, kappa):
    x = 2 * x_hi + ((kappa >> 1) ^ x_hi)
    return z * 8 + x * 2 + (kappa & 1)


G4 = [[4 * n + k for k in range(4)] for n in range(16)]
GK = [[leaf_at(z, xh, k) for k in range(4)] for z in range(8) for xh in range(2)]


def facing(i, flip_x, flip_z):
    z, x, core = i // 8, i // 2 % 4, i % 2
    return (z ^ flip_z) * 8 + (3 - x if flip_x else x) * 2 + core


def leaf_route(value, target):
    return lax.ppermute(value, "leaf", [(i, target(i)) for i in range(LEAVES)])


def leaf_xor(value, bit):
    return leaf_route(value, lambda i: i ^ bit)


def leaf_from(value, step):
    return leaf_route(value, lambda i: (i - step) % LEAVES)


def siblings(value):
    return [value] + [
        leaf_route(value, lambda i, d=d: facing(i, d & 1, d >> 1)) for d in (1, 2, 3)
    ]


def z_from(value, even, odd):
    route = []
    for i in range(LEAVES):
        step = odd if i // 8 % 2 else even
        route.append(((i + 8 * step) % LEAVES, i))
    return lax.ppermute(value, "leaf", route)


def col_shift(value, step):
    return lax.ppermute(value, "col", [(i, (i + step) % 4) for i in range(4)])


def gather4(value, groups):
    return lax.all_gather(value, "leaf", axis=0, axis_index_groups=groups)


def group(value):
    across = leaf_xor(value, 2)
    return [value, leaf_xor(value, 1), across, leaf_xor(across, 1)]


def mm(a, b, dims, precision=HIGH):
    return lax.dot_general(a, b, (dims, ((), ())), precision=precision, preferred_element_type=F32)


def halves(value):
    top = lax.reduce_precision(value, 8, 7)
    return top.astype(BF16), (value - top).astype(BF16)


def select(value, picks, dims):
    a, b = halves(value)
    return mm(a, picks, dims, None) + mm(b, picks, dims, None)


NN = ((1,), (0,))
NT = ((1,), (1,))


def dot(a, b, dims=NN):
    return lax.dot_general(a, b, (dims, ((), ())), preferred_element_type=F32)


def split(value):
    top = value.astype(BF16)
    return top, (value - top.astype(F32)).astype(BF16)


def dot3(a, b, dims=NN):
    at, al = split(a)
    bt, bl = split(b)
    return dot(at, bt, dims) + (dot(at, bl, dims) + dot(al, bt, dims))


SMEM = pl.BlockSpec(memory_space=pltpu.SMEM)


def whole(*shape):
    return pl.BlockSpec(shape, lambda *i: (0,) * len(shape))


def like(*shape, dtype=F32):
    return jax.ShapeDtypeStruct(shape, dtype)


CHUNK = 512


def tile_setup(place, xs, ys, avals, rows, squares, tops, lows):
    for k, ref in enumerate(xs):
        rows[(place[2] + 4 - k) % 4] = ref[...]
    for k, (y, a) in enumerate(zip(ys, avals)):
        total = jnp.sum(y[...] * y[...], axis=1, keepdims=True)
        squares[k] = jnp.transpose(jnp.broadcast_to(total, (Q, 128)))[:8]
        tops[k], lows[k] = split(a[...])


def tile_sum(x, ys, weights, squares, tops, lows):
    own = jnp.sum(x * x, axis=1, keepdims=True)
    total = None
    for k, (y, weight) in enumerate(zip(ys, weights)):
        inner = lax.dot_general(
            x, y[...], (NT, ((), ())), precision=HIGHEST, preferred_element_type=F32
        )
        distance = own + squares[k][:1] - 2.0 * inner
        top, low = split(jnp.exp(distance * (-2.0 / 128.0)) * weight)
        term = dot(top, tops[k]) + dot(top, lows[k]) + dot(low, tops[k])
        total = term if total is None else total + term
    return total


def near_kernel(place, mask, x0, x1, x2, x3, bx, ay, by, out, rows, squares, tops, lows):
    i = pl.program_id(0)
    ys = (x0, bx)

    @pl.when(i == 0)
    def _():
        tile_setup(place, (x0, x1, x2, x3), ys, (ay, by), rows, squares, tops, lows)

    weights = (mask[0, 2].astype(F32), mask[0, 3 - 2 * place[0]].astype(F32))
    x = rows[pl.ds(2 * i, 2)].reshape(CHUNK, 128)
    out[...] = tile_sum(x, ys, weights, squares, tops, lows)


def far_kernel(
    place, mask, ridge, x0, x1, x2, x3, bx, cx, dx, by, cy, dy, near, own_y, own_a, lead,
    out, led, rows, squares, tops, lows,
):
    i = pl.program_id(0)
    ys = (bx, cx, dx)

    @pl.when(i == 0)
    def _():
        tile_setup(place, (x0, x1, x2, x3), ys, (by, cy, dy), rows, squares, tops, lows)

    weights = (
        mask[0, 0].astype(F32),
        mask[0, 4].astype(F32),
        mask[0, 1 + 2 * place[0]].astype(F32),
    )
    x = rows[pl.ds(2 * i, 2)].reshape(CHUNK, 128)
    total = near[...] + tile_sum(x, ys, weights, squares, tops, lows)
    own = own_y[...] - ridge[0] * own_a[...]
    part = jnp.concatenate(
        [
            jnp.where(place[2] == 2 * i + h, own, 0.0) - total[h * Q : (h + 1) * Q]
            for h in range(2)
        ],
        axis=0,
    )
    product = dot3(lead[...], part)
    for k in range(4):
        out[k] = part[:, k * 128 : (k + 1) * 128]
        piece = product[:, k * 128 : (k + 1) * 128]
        led[k] = jnp.where(i == 0, piece, led[k] + piece)


def tile_scratch(count):
    return [
        pltpu.VMEM((4, Q, 128), F32),
        pltpu.VMEM((count, 8, Q), F32),
        pltpu.VMEM((count, Q, 512), BF16),
        pltpu.VMEM((count, Q, 512), BF16),
    ]


def near_call(place, mask, xs, bx, ay, by):
    return pl.pallas_call(
        near_kernel,
        grid=(2,),
        in_specs=[SMEM, SMEM] + [whole(Q, 128)] * 5 + [whole(Q, 512)] * 2,
        out_specs=pl.BlockSpec((CHUNK, 512), lambda i: (i, 0)),
        out_shape=like(1024, 512),
        scratch_shapes=tile_scratch(2),
        name="near",
    )(place, mask, *xs, bx, ay, by)


def far_call(place, mask, ridge, xs, others_x, others_a, near, own_y, own_a, lead):
    return pl.pallas_call(
        far_kernel,
        grid=(2,),
        in_specs=[SMEM, SMEM, SMEM]
        + [whole(Q, 128)] * 7
        + [whole(Q, 512)] * 3
        + [pl.BlockSpec((CHUNK, 512), lambda i: (i, 0))]
        + [whole(Q, 512)] * 2
        + [pl.BlockSpec((RANK, CHUNK), lambda i: (0, i))],
        out_specs=[pl.BlockSpec((4, CHUNK, 128), lambda i: (0, i, 0)), whole(4, RANK, 128)],
        out_shape=[like(4, 1024, 128), like(4, RANK, 128)],
        scratch_shapes=tile_scratch(3),
        name="far",
    )(place, mask, ridge, *xs, *others_x, *others_a, near, own_y, own_a, lead)


def nodes_kernel(place, n0, n1, n2, n3, t0, t1, t2, t3, e1, m2, e2, m3):
    q = place[3] % 4
    child = place[3] // 4 % 4
    parent = place[3] // 16
    odd = place[3] // 8 % 2
    for d, (inverse, transfer) in enumerate(zip((n0, n1, n2, n3), (t0, t1, t2, t3))):
        at = q ^ d
        e1[pl.ds(pl.multiple_of(at * 256, 256), 256), :] = transfer[:256, :]
        e2[pl.ds(pl.multiple_of(at * 64, 64), 64), :] = transfer[256:320, :]
        for k in range(4):
            source = pl.ds(pl.multiple_of((child ^ k) * 256, 256), 256)
            m2[pl.ds(pl.multiple_of(at * 64, 64), 64), k * 256 : (k + 1) * 256] = inverse[
                :64, source
            ]
            step = (0, 3, 1, 2)[k] + odd * (0, -2, 2, 0)[k]
            source = pl.ds(pl.multiple_of((parent + step) % 4 * 256, 256), 256)
            m3[pl.ds(pl.multiple_of(at * 16, 16), 16), k * 256 : (k + 1) * 256] = inverse[
                64:80, source
            ]


def nodes_call(place, inverses, transfers):
    return pl.pallas_call(
        nodes_kernel,
        in_specs=[SMEM] + [whole(80, 1024)] * 4 + [whole(320, 256)] * 4,
        out_specs=[whole(1024, 256), whole(256, 1024), whole(256, 256), whole(64, 1024)],
        out_shape=[like(1024, 256), like(256, 1024), like(256, 256), like(64, 1024)],
        grid=(1,),
        name="nodes",
    )(place, *inverses, *transfers)


def level1_kernel(place, leaf_map, stacked, m1, e1, w1, p1):
    base = place[3] // 4 * 4
    total = None
    for k in range(4):
        term = dot3(m1[0, :, k * 256 : (k + 1) * 256], stacked[leaf_map[base + k] - base])
        total = term if total is None else total + term
    w1[...] = total
    p1[...] = dot3(jnp.transpose(total), e1[0])


def level1_call(place, leaf_map, stacked, node_inverse, node_transfer):
    return pl.pallas_call(
        level1_kernel,
        grid=(1,),
        in_specs=[SMEM, SMEM, whole(4, 256, 128), whole(1, 256, 1024), whole(1, 256, 256)],
        out_specs=[whole(256, 128), whole(128, 256)],
        out_shape=[like(256, 128), like(128, 256)],
        name="level1",
    )(place, leaf_map, stacked, node_inverse, node_transfer)


def row_blocks(parts, matrix):
    total = None
    for k, part in enumerate(parts):
        term = dot3(part[...], matrix[:, k * 256 : (k + 1) * 256], NT)
        total = term if total is None else total + term
    return total


def level2_kernel(r0, r1, r2, r3, m2, e2, w2, p2):
    total = row_blocks((r0, r1, r2, r3), m2)
    w2[...] = total
    p2[...] = dot3(total, e2[...])


def level2_call(parts, m2, e2):
    return pl.pallas_call(
        level2_kernel,
        out_shape=[like(32, 256), like(32, 256)],
        name="level2",
    )(*parts, m2, e2)


def root_kernel(r0, r1, r2, r3, m3, g2):
    g2[...] = row_blocks((r0, r1, r2, r3), m3)


def root_call(parts, m3):
    return pl.pallas_call(root_kernel, out_shape=like(32, 64), name="root")(*parts, m3)


def lift_kernel(place, g0, g1, g2, g3, e2, lifted):
    child = place[3] // 4 % 4
    parts = [g0[...], g1[...], g2[...], g3[...]]
    blocks = []
    for k in range(4):
        block = parts[3]
        for d in range(3):
            block = jnp.where((child ^ d) == k, parts[d], block)
        blocks.append(block)
    lifted[...] = dot3(jnp.concatenate(blocks, axis=1), e2[...], NT)


def lift_call(place, parts, e2):
    return pl.pallas_call(
        lift_kernel,
        grid=(1,),
        in_specs=[SMEM] + [whole(32, 64)] * 4 + [whole(256, 256)],
        out_specs=whole(32, 256),
        out_shape=like(32, 256),
        name="lift",
    )(place, *parts, e2)


def down2_kernel(w2, l0, l1, l2, l3, m2, g1):
    g1[...] = w2[...] - row_blocks((l0, l1, l2, l3), m2)


def down2_call(w2, parts, m2):
    return pl.pallas_call(down2_kernel, out_shape=like(32, 256), name="down2")(w2, *parts, m2)


def down1_kernel(g1, e1, m1, w1, v1):
    g = g1[...].reshape(128, 256)
    lifted = dot3(g, e1[...], NT)
    v1[...] = w1[...] - dot3(m1[0], lifted, NT)


def down1_call(g1, e1, node_inverse, w1):
    return pl.pallas_call(
        down1_kernel,
        grid=(1,),
        in_specs=[whole(4, 32, 256), whole(1024, 256), whole(1, 256, 1024), whole(256, 128)],
        out_specs=whole(256, 128),
        out_shape=like(256, 128),
        name="down1",
    )(g1, e1, node_inverse, w1)


def residual_kernel(order, parts, res, ordered, picks):
    res_sum = parts[0] + parts[1] + (parts[2] + parts[3])
    res[...] = res_sum
    at = lax.broadcasted_iota(jnp.int32, (1024, 1024), 1)
    picks[...] = jnp.where(order[...] == at, 1.0, 0.0).astype(BF16)
    top, low = split(res_sum)
    ordered[...] = dot(picks[...], top) + dot(picks[...], low)


def residual_call(order, parts):
    return pl.pallas_call(
        residual_kernel,
        out_shape=[like(1024, 128), like(1024, 128)],
        scratch_shapes=[pltpu.VMEM((1024, 1024), BF16)],
        name="residual",
    )(order, parts)


def finish_kernel(place, leaf_map, order, pieces, ordered, basis, solve, delta, picks, tops, lows):
    i = pl.program_id(0)

    @pl.when(i == 0)
    def _():
        base = place[3] // 4 * 4
        slot = jnp.int32(3)
        for k in range(3):
            slot = jnp.where(leaf_map[base + k] == place[3], k, slot)
        tops[...], lows[...] = split(ordered[...] - dot3(basis[0], pieces[slot]))

    a, b = split(solve[0])
    y = dot(a, tops[...]) + (dot(a, lows[...]) + dot(b, tops[...]))
    at = lax.broadcasted_iota(jnp.int32, (1024, Q), 0)
    picks[...] = jnp.where(order[...] == at, 1.0, 0.0).astype(BF16)
    top, low = split(y)
    term = dot(picks[...], top) + dot(picks[...], low)
    delta[...] = jnp.where(i == 0, term, delta[...] + term)


def finish_call(place, leaf_map, order, pieces, ordered, leaf_basis, leaf_inverse):
    return pl.pallas_call(
        finish_kernel,
        grid=(4,),
        in_specs=[
            SMEM,
            SMEM,
            pl.BlockSpec((1, Q), lambda i: (0, i)),
            whole(4, 256, 128),
            whole(1024, 128),
            whole(1, 1024, 256),
            pl.BlockSpec((1, Q, 1024), lambda i: (0, i, 0)),
        ],
        out_specs=whole(1024, 128),
        out_shape=like(1024, 128),
        scratch_shapes=[
            pltpu.VMEM((1024, Q), BF16),
            pltpu.VMEM((1024, 128), BF16),
            pltpu.VMEM((1024, 128), BF16),
        ],
        name="finish",
    )(place, leaf_map, order, pieces, ordered, leaf_basis, leaf_inverse)


def outputs_kernel(res, delta, coefs, out_res, out_new):
    for k in range(4):
        at = slice(k * 128, (k + 1) * 128)
        out_res[:, at] = res[k]
        out_new[:, at] = coefs[:, at] + delta[k]


def outputs_call(res, delta, coefs):
    return pl.pallas_call(
        outputs_kernel, out_shape=[like(Q, 512), like(Q, 512)], name="outputs"
    )(res, delta, coefs)


def swap_cols(value):
    return lax.all_to_all(value, "col", 0, 0, tiled=True)


def local(
    points,
    coefs,
    targets,
    ridge,
    tile_mask,
    cluster_perm,
    leaf_map,
    leaf_inverse,
    leaf_basis,
    node_inverse,
    node_transfer,
):
    col = lax.axis_index("col")
    leaf = lax.axis_index("leaf")
    core = leaf % 2
    place = jnp.stack([core, leaf // 2 % 2, col, leaf]).astype(jnp.int32)

    left_x, right_x = leaf_from(points, -2), leaf_from(points, 2)
    xs = [points] + [col_shift(points, d) for d in (1, 2, 3)]
    left_a, right_a = leaf_from(coefs, -2), leaf_from(coefs, 2)
    partner_x, partner_a = leaf_xor(points, 1), leaf_xor(coefs, 1)
    relay_x = leaf_xor(jnp.where(core == 0, right_x, left_x), 1)
    relay_a = leaf_xor(jnp.where(core == 0, right_a, left_a), 1)

    order = cluster_perm[0]
    at = jnp.arange(1024, dtype=jnp.int32)
    pick = (order[:, None] == at[None, :]).astype(BF16)
    lead = select(mm(leaf_basis[0], leaf_inverse[0], ((0,), (0,))), pick, NN)

    near = near_call(place, tile_mask, xs, partner_x, coefs, partner_a)
    partial, led = far_call(
        place,
        tile_mask,
        ridge,
        xs,
        (left_x, right_x, relay_x),
        (left_a, right_a, relay_a),
        near,
        targets,
        coefs,
        lead,
    )
    reduced = swap_cols(led).sum(0)

    held = lax.optimization_barrier((node_transfer[0, :320], node_inverse[0, 256:336], relay_a))
    e1, m2, e2, m3 = nodes_call(place, group(held[1]), group(held[0]))

    partial, _ = lax.optimization_barrier((partial, reduced))
    res, ordered = residual_call(order.reshape(1024, 1), swap_cols(partial))
    res_rows = swap_cols(res.reshape(4, Q, 128))

    w1, p1 = level1_call(place, leaf_map, gather4(reduced, G4), node_inverse, node_transfer)
    p1 = lax.all_to_all(p1, "leaf", 0, 0, axis_index_groups=GK, tiled=True)
    r1 = p1.reshape(4, 32, RANK).sum(0)
    w2, p2 = level2_call(siblings(r1), m2, e2)
    r2 = sum(siblings(p2))
    r2s = [r2, z_from(r2, -1, 1), z_from(r2, 2, -2), z_from(r2, -3, 3)]
    lifted = lift_call(place, siblings(root_call(r2s, m3)), e2)
    g1 = gather4(down2_call(w2, siblings(lifted), m2), GK)
    pieces = gather4(down1_call(g1, e1, node_inverse, w1), G4)

    delta = finish_call(place, leaf_map, cluster_perm, pieces, ordered, leaf_basis, leaf_inverse)
    return outputs_call(res_rows, swap_cols(delta.reshape(4, Q, 128)), coefs)


def solution(mesh):
    return jax.shard_map(
        local,
        mesh=mesh,
        in_specs=(
            P(("leaf", "col"), None),
            P(("leaf", "col"), None),
            P(("leaf", "col"), None),
            P(),
            P("leaf", None),
            P("leaf", None),
            P(),
            P("leaf", None, None),
            P("leaf", None, None),
            P("leaf", None, None),
            P("leaf", None, None),
        ),
        out_specs=(P(("leaf", "col"), None), P(("leaf", "col"), None)),
        check_vma=False,
    )
```

```python
import jax
import jax.numpy as jnp
from jax import lax
from jax.experimental import pallas as pl
from jax.experimental.pallas import tpu as pltpu
from jax.sharding import PartitionSpec as P


HIGH = lax.Precision.HIGH
F32 = jnp.float32
BF16 = jnp.bfloat16
Q = 256
RANK = 256
LEAVES = 64


def leaf_at(z, x_hi, kappa):
    x = 2 * x_hi + ((kappa >> 1) ^ x_hi)
    return z * 8 + x * 2 + (kappa & 1)


G4 = [[4 * n + k for k in range(4)] for n in range(16)]
GK = [[leaf_at(z, xh, k) for k in range(4)] for z in range(8) for xh in range(2)]


def facing(i, flip_x, flip_z):
    z, x, core = i // 8, i // 2 % 4, i % 2
    return (z ^ flip_z) * 8 + (3 - x if flip_x else x) * 2 + core


def leaf_route(value, target):
    return lax.ppermute(value, "leaf", [(i, target(i)) for i in range(LEAVES)])


def leaf_xor(value, bit):
    return leaf_route(value, lambda i: i ^ bit)


def leaf_from(value, step):
    return leaf_route(value, lambda i: (i - step) % LEAVES)


def siblings(value):
    return [value] + [
        leaf_route(value, lambda i, d=d: facing(i, d & 1, d >> 1)) for d in (1, 2, 3)
    ]


def z_from(value, even, odd):
    route = []
    for i in range(LEAVES):
        step = odd if i // 8 % 2 else even
        route.append(((i + 8 * step) % LEAVES, i))
    return lax.ppermute(value, "leaf", route)


def col_shift(value, step):
    return lax.ppermute(value, "col", [(i, (i + step) % 4) for i in range(4)])


def gather4(value, groups):
    return lax.all_gather(value, "leaf", axis=0, axis_index_groups=groups)


def mm(a, b, dims, precision=HIGH):
    return lax.dot_general(a, b, (dims, ((), ())), precision=precision, preferred_element_type=F32)


def halves(value):
    top = lax.reduce_precision(value, 8, 7)
    return top.astype(BF16), (value - top).astype(BF16)


def select(value, picks, dims):
    a, b = halves(value)
    return mm(a, picks, dims, None) + mm(b, picks, dims, None)


NN = ((1,), (0,))
NT = ((1,), (1,))


def dot(a, b, dims=NN):
    return lax.dot_general(a, b, (dims, ((), ())), preferred_element_type=F32)


def split(value):
    top = value.astype(BF16)
    return top, (value - top.astype(F32)).astype(BF16)


def dot3(a, b, dims=NN):
    at, al = split(a)
    bt, bl = split(b)
    return dot(at, bt, dims) + (dot(at, bl, dims) + dot(al, bt, dims))


SMEM = pl.BlockSpec(memory_space=pltpu.SMEM)


def whole(*shape):
    return pl.BlockSpec(shape, lambda *i: (0,) * len(shape))


def like(*shape, dtype=F32):
    return jax.ShapeDtypeStruct(shape, dtype)


CHUNK = 512


def two_part(value):
    top, low = split(value)
    return jnp.concatenate([top, low], axis=1), top.astype(F32) + low.astype(F32)


def tile_setup(place, xs, blocks, rows, norms, squares, others, tops, lows):
    for k, ref in enumerate(xs):
        at = (place[2] + 4 - k) % 4
        rows[at], exact = two_part(ref[...])
        norms[at] = jnp.sum(exact * exact, axis=1, keepdims=True)
    for k, (y, a) in enumerate(blocks):
        others[k], exact = two_part(y)
        total = jnp.sum(exact * exact, axis=1, keepdims=True)
        squares[k] = jnp.transpose(jnp.broadcast_to(total, (Q, 128)))[:8]
        tops[k], lows[k] = split(a)


def tile_sum(i, weights, rows, norms, squares, others, tops, lows):
    x = rows[pl.ds(2 * i, 2)].reshape(CHUNK, 256)
    own = norms[pl.ds(2 * i, 2)].reshape(CHUNK, 1)
    total = None
    for k, weight in enumerate(weights):
        top, low = others[k][:, :128], others[k][:, 128:]
        inner = dot(x, jnp.concatenate([top, top], axis=1), NT)
        inner = inner + dot(x, jnp.concatenate([low, low], axis=1), NT)
        distance = own + squares[k][:1] - 2.0 * inner
        top, low = split(jnp.exp(distance * (-2.0 / 128.0)) * weight)
        term = dot(top, tops[k]) + dot(top, lows[k]) + dot(low, tops[k])
        total = term if total is None else total + term
    return total


def near_kernel(place, mask, x0, x1, x2, x3, p0, p1, out, *scratch):
    i = pl.program_id(0)

    @pl.when(i == 0)
    def _():
        blocks = [(p[:, :128], p[:, 128:]) for p in (p0, p1)]
        tile_setup(place, (x0, x1, x2, x3), blocks, *scratch)

    weights = (mask[0, 2].astype(F32), mask[0, 3 - 2 * place[0]].astype(F32))
    out[...] = tile_sum(i, weights, *scratch)


def far_kernel(
    place, mask, ridge, x0, x1, x2, x3, p0, p1, p2, near, own_y, own_a, lead, out, led, *scratch
):
    i = pl.program_id(0)

    @pl.when(i == 0)
    def _():
        blocks = [(p[:, :128], p[:, 128:]) for p in (p0, p1, p2)]
        tile_setup(place, (x0, x1, x2, x3), blocks, *scratch)

    weights = (
        mask[0, 0].astype(F32),
        mask[0, 4].astype(F32),
        mask[0, 1 + 2 * place[0]].astype(F32),
    )
    total = near[...] + tile_sum(i, weights, *scratch)
    own = own_y[...] - ridge[0] * own_a[...]
    part = jnp.concatenate(
        [
            jnp.where(place[2] == 2 * i + h, own, 0.0) - total[h * Q : (h + 1) * Q]
            for h in range(2)
        ],
        axis=0,
    )
    product = dot3(lead[...], part)
    for k in range(4):
        out[k] = part[:, k * 128 : (k + 1) * 128]
        piece = product[:, k * 128 : (k + 1) * 128]
        led[k] = jnp.where(i == 0, piece, led[k] + piece)


def tile_scratch(count):
    return [
        pltpu.VMEM((4, Q, 256), BF16),
        pltpu.VMEM((4, Q, 1), F32),
        pltpu.VMEM((count, 8, Q), F32),
        pltpu.VMEM((count, Q, 256), BF16),
        pltpu.VMEM((count, Q, 512), BF16),
        pltpu.VMEM((count, Q, 512), BF16),
    ]


def near_call(place, mask, xs, blocks):
    return pl.pallas_call(
        near_kernel,
        grid=(2,),
        in_specs=[SMEM, SMEM] + [whole(Q, 128)] * 4 + [whole(Q, 640)] * 2,
        out_specs=pl.BlockSpec((CHUNK, 512), lambda i: (i, 0)),
        out_shape=like(1024, 512),
        scratch_shapes=tile_scratch(2),
        name="near",
    )(place, mask, *xs, *blocks)


def far_call(place, mask, ridge, xs, blocks, near, own_y, own_a, lead):
    return pl.pallas_call(
        far_kernel,
        grid=(2,),
        in_specs=[SMEM, SMEM, SMEM]
        + [whole(Q, 128)] * 4
        + [whole(Q, 640)] * 3
        + [pl.BlockSpec((CHUNK, 512), lambda i: (i, 0))]
        + [whole(Q, 512)] * 2
        + [pl.BlockSpec((RANK, CHUNK), lambda i: (0, i))],
        out_specs=[pl.BlockSpec((4, CHUNK, 128), lambda i: (0, i, 0)), whole(4, RANK, 128)],
        out_shape=[like(4, 1024, 128), like(4, RANK, 128)],
        scratch_shapes=tile_scratch(3),
        name="far",
    )(place, mask, ridge, *xs, *blocks, near, own_y, own_a, lead)


def pack_kernel(a, b, out):
    out[:, :128] = a[...]
    out[:, 128:] = b[...]


def pack_call(a, b):
    return pl.pallas_call(pack_kernel, out_shape=like(Q, 640), name="pack")(a, b)


def fill_slices(transfer, inverse, out, start):
    out[start : start + 64, :] = transfer[0, 256:320, :]
    for k in range(4):
        at = start + 64 + k * 16
        out[at : at + 16, :] = inverse[0, 320:336, k * 256 : (k + 1) * 256]


def slices_kernel(transfer, inverse, out):
    fill_slices(transfer, inverse, out, 0)


def pair_kernel(transfer, inverse, lower, out):
    fill_slices(transfer, inverse, out, 0)
    out[128:, :] = lower[...]


def held_kernel(transfer, inverse, lower, mirrored, out):
    out[:256, :] = transfer[0, :256, :]
    for k in range(4):
        at = 256 + k * 64
        out[at : at + 64, :] = inverse[0, 256:320, k * 256 : (k + 1) * 256]
    fill_slices(transfer, inverse, out, 512)
    out[640:768, :] = lower[...]
    out[768:, :] = mirrored[...]


def collect(body, rows, *parts):
    return pl.pallas_call(body, out_shape=like(rows, 256))(*parts)


def nodes_kernel(place, b0, b1, b2, b3, e1, m2, f2, m3, own_e2, e2):
    q = place[3] % 4
    child = place[3] // 4 % 4
    parent = place[3] // 16
    odd = place[3] // 8 % 2
    for d, block in enumerate((b0, b1, b2, b3)):
        at = q ^ d
        e1[pl.ds(pl.multiple_of(at * 256, 256), 256), :] = block[:256, :]
        rows = pl.ds(pl.multiple_of(at * 64, 64), 64)
        for k in range(4):
            source = pl.multiple_of(256 + (child ^ k) * 64, 64)
            m2[rows, k * 256 : (k + 1) * 256] = block[pl.ds(source, 64), :]
        for s, (start, flip) in enumerate(((512, 0), (768, 2), (640, 0), (896, 2))):
            held = at ^ flip
            e2[pl.ds(pl.multiple_of(s * 256 + held * 64, 64), 64), :] = block[
                start : start + 64, :
            ]
            rows = pl.ds(pl.multiple_of((child ^ s) * 64 + held * 16, 16), 16)
            for k in range(4):
                step = (0, 3, 1, 2)[k] + odd * (0, -2, 2, 0)[k]
                source = pl.multiple_of(start + 64 + (parent + step) % 4 * 16, 16)
                m3[rows, k * 256 : (k + 1) * 256] = block[pl.ds(source, 16), :]
    own_e2[...] = e2[:256, :]
    f2[...] = dot3(m2[...], e2[...])


def nodes_call(place, blocks):
    return pl.pallas_call(
        nodes_kernel,
        in_specs=[SMEM] + [whole(1024, 256)] * 4,
        out_specs=[whole(1024, 256), whole(256, 1024), whole(256, 256), whole(256, 1024), whole(256, 256)],
        out_shape=[like(1024, 256), like(256, 1024), like(256, 256), like(256, 1024), like(256, 256)],
        scratch_shapes=[pltpu.VMEM((1024, 256), F32)],
        grid=(1,),
        name="nodes",
    )(place, *blocks)


def level1_kernel(place, leaf_map, stacked, m1, e1, w1, p1):
    base = place[3] // 4 * 4
    total = None
    for k in range(4):
        term = dot3(m1[0, :, k * 256 : (k + 1) * 256], stacked[leaf_map[base + k] - base])
        total = term if total is None else total + term
    w1[...] = total
    p1[...] = dot3(jnp.transpose(total), e1[0])


def level1_call(place, leaf_map, stacked, node_inverse, node_transfer):
    return pl.pallas_call(
        level1_kernel,
        grid=(1,),
        in_specs=[SMEM, SMEM, whole(4, 256, 128), whole(1, 256, 1024), whole(1, 256, 256)],
        out_specs=[whole(256, 128), whole(128, 256)],
        out_shape=[like(256, 128), like(128, 256)],
        name="level1",
    )(place, leaf_map, stacked, node_inverse, node_transfer)


def row_blocks(parts, matrix):
    total = None
    for k, part in enumerate(parts):
        term = dot3(part[...], matrix[:, k * 256 : (k + 1) * 256], NT)
        total = term if total is None else total + term
    return total


def level2_kernel(r0, r1, r2, r3, m2, e2, w2, p2):
    total = row_blocks((r0, r1, r2, r3), m2)
    w2[...] = total
    p2[...] = dot3(total, e2[...])


def level2_call(parts, m2, e2):
    return pl.pallas_call(
        level2_kernel,
        out_shape=[like(32, 256), like(32, 256)],
        name="level2",
    )(*parts, m2, e2)


def upper_kernel(r0, r1, r2, r3, m3, f2, w2, g1):
    g2 = row_blocks((r0, r1, r2, r3), m3)
    g1[...] = w2[...] - dot3(g2, f2[...], NT)


def upper_call(parts, m3, f2, w2):
    return pl.pallas_call(upper_kernel, out_shape=like(32, 256), name="upper")(
        *parts, m3, f2, w2
    )


def down1_kernel(g1, e1, m1, w1, v1):
    g = g1[...].reshape(128, 256)
    lifted = dot3(g, e1[...], NT)
    v1[...] = w1[...] - dot3(m1[0], lifted, NT)


def down1_call(g1, e1, node_inverse, w1):
    return pl.pallas_call(
        down1_kernel,
        grid=(1,),
        in_specs=[whole(4, 32, 256), whole(1024, 256), whole(1, 256, 1024), whole(256, 128)],
        out_specs=whole(256, 128),
        out_shape=like(256, 128),
        name="down1",
    )(g1, e1, node_inverse, w1)


def residual_kernel(order, parts, res, ordered, picks):
    res_sum = parts[0] + parts[1] + (parts[2] + parts[3])
    res[...] = res_sum
    at = lax.broadcasted_iota(jnp.int32, (1024, 1024), 1)
    picks[...] = jnp.where(order[...] == at, 1.0, 0.0).astype(BF16)
    both = dot(picks[...], jnp.concatenate(split(res_sum), axis=1))
    ordered[...] = both[:, :128] + both[:, 128:]


def residual_call(order, parts):
    return pl.pallas_call(
        residual_kernel,
        out_shape=[like(1024, 128), like(1024, 128)],
        scratch_shapes=[pltpu.VMEM((1024, 1024), BF16)],
        name="residual",
    )(order, parts)


def finish_kernel(place, leaf_map, order, pieces, ordered, basis, solve, delta, picks, rhs):
    i = pl.program_id(0)

    @pl.when(i == 0)
    def _():
        base = place[3] // 4 * 4
        slot = jnp.int32(3)
        for k in range(3):
            slot = jnp.where(leaf_map[base + k] == place[3], k, slot)
        top, low = split(ordered[...] - dot3(basis[0], pieces[slot]))
        rhs[...] = jnp.concatenate([top, low], axis=1)

    a, b = split(solve[0])
    both = dot(a, rhs[...])
    y = both[:, :128] + (both[:, 128:] + dot(b, rhs[:, :128]))
    at = lax.broadcasted_iota(jnp.int32, (1024, Q), 0)
    picks[...] = jnp.where(order[...] == at, 1.0, 0.0).astype(BF16)
    both = dot(picks[...], jnp.concatenate(split(y), axis=1))
    term = both[:, :128] + both[:, 128:]
    delta[...] = jnp.where(i == 0, term, delta[...] + term)


def finish_call(place, leaf_map, order, pieces, ordered, leaf_basis, leaf_inverse):
    return pl.pallas_call(
        finish_kernel,
        grid=(4,),
        in_specs=[
            SMEM,
            SMEM,
            pl.BlockSpec((1, Q), lambda i: (0, i)),
            whole(4, 256, 128),
            whole(1024, 128),
            whole(1, 1024, 256),
            pl.BlockSpec((1, Q, 1024), lambda i: (0, i, 0)),
        ],
        out_specs=whole(1024, 128),
        out_shape=like(1024, 128),
        scratch_shapes=[
            pltpu.VMEM((1024, Q), BF16),
            pltpu.VMEM((1024, 256), BF16),
        ],
        name="finish",
    )(place, leaf_map, order, pieces, ordered, leaf_basis, leaf_inverse)


def outputs_kernel(res, delta, coefs, out_res, out_new):
    for k in range(4):
        at = slice(k * 128, (k + 1) * 128)
        out_res[:, at] = res[k]
        out_new[:, at] = coefs[:, at] + delta[k]


def outputs_call(res, delta, coefs):
    return pl.pallas_call(
        outputs_kernel, out_shape=[like(Q, 512), like(Q, 512)], name="outputs"
    )(res, delta, coefs)


def swap_cols(value):
    return lax.all_to_all(value, "col", 0, 0, tiled=True)


def step(
    points,
    coefs,
    targets,
    ridge,
    tile_mask,
    cluster_perm,
    leaf_map,
    leaf_inverse,
    leaf_basis,
    node_inverse,
    node_transfer,
):
    col = lax.axis_index("col")
    leaf = lax.axis_index("leaf")
    core = leaf % 2
    place = jnp.stack([core, leaf // 2 % 2, col, leaf]).astype(jnp.int32)

    xs = [points] + [col_shift(points, d) for d in (1, 2, 3)]
    packed = pack_call(points, coefs)
    left, right = leaf_from(packed, -2), leaf_from(packed, 2)
    partner = leaf_xor(packed, 1)
    relay = leaf_xor(jnp.where(core == 0, right, left), 1)

    nodes = (node_transfer, node_inverse)
    lower = leaf_route(collect(slices_kernel, 128, *nodes), lambda i: facing(i, 0, 1))
    mirrored = leaf_route(collect(pair_kernel, 256, *nodes, lower), lambda i: facing(i, 1, 0))
    held = collect(held_kernel, 1024, *nodes, lower, mirrored)

    order = cluster_perm[0]
    at = jnp.arange(1024, dtype=jnp.int32)
    pick = (order[:, None] == at[None, :]).astype(BF16)
    lead = select(mm(leaf_basis[0], leaf_inverse[0], ((0,), (0,))), pick, NN)

    near = near_call(place, tile_mask, xs, (packed, partner))
    near, held = lax.optimization_barrier((near, held))
    across = leaf_xor(held, 2)
    own_core = leaf_xor(held, 1)
    both_ways = leaf_xor(across, 1)
    partial, led = far_call(
        place, tile_mask, ridge, xs, (left, right, relay), near, targets, coefs, lead
    )
    reduced = swap_cols(led).sum(0)
    e1, m2, f2, m3, e2 = nodes_call(place, (held, own_core, across, both_ways))

    partial, _ = lax.optimization_barrier((partial, reduced))
    res, ordered = residual_call(order.reshape(1024, 1), swap_cols(partial))
    res_rows = swap_cols(res.reshape(4, Q, 128))

    w1, p1 = level1_call(place, leaf_map, gather4(reduced, G4), node_inverse, node_transfer)
    p1 = lax.all_to_all(p1, "leaf", 0, 0, axis_index_groups=GK, tiled=True)
    r1 = p1.reshape(4, 32, RANK).sum(0)
    w2, p2 = level2_call(siblings(r1), m2, e2)
    r2 = sum(siblings(p2))
    r2s = [r2, z_from(r2, -1, 1), z_from(r2, 2, -2), z_from(r2, -3, 3)]
    g1 = gather4(upper_call(r2s, m3, f2, w2), GK)
    pieces = gather4(down1_call(g1, e1, node_inverse, w1), G4)

    delta = finish_call(place, leaf_map, cluster_perm, pieces, ordered, leaf_basis, leaf_inverse)
    return outputs_call(res_rows, swap_cols(delta.reshape(4, Q, 128)), coefs)


def solution(mesh):
    return jax.shard_map(
        step,
        mesh=mesh,
        in_specs=(
            P(("leaf", "col"), None),
            P(("leaf", "col"), None),
            P(("leaf", "col"), None),
            P(),
            P("leaf", None),
            P("leaf", None),
            P(),
            P("leaf", None, None),
            P("leaf", None, None),
            P("leaf", None, None),
            P("leaf", None, None),
        ),
        out_specs=(P(("leaf", "col"), None), P(("leaf", "col"), None)),
        check_vma=False,
    )
```

```python
import jax
import jax.numpy as jnp
from jax import lax
from jax.experimental import pallas as pl
from jax.experimental.pallas import tpu as pltpu
from jax.sharding import PartitionSpec as P


F32 = jnp.float32
BF16 = jnp.bfloat16
Q = 256
RANK = 256
LEAVES = 64


def leaf_at(z, x_hi, kappa):
    x = 2 * x_hi + ((kappa >> 1) ^ x_hi)
    return z * 8 + x * 2 + (kappa & 1)


G4 = [[4 * n + k for k in range(4)] for n in range(16)]
GK = [[leaf_at(z, xh, k) for k in range(4)] for z in range(8) for xh in range(2)]


def facing(i, flip_x, flip_z):
    z, x, core = i // 8, i // 2 % 4, i % 2
    return (z ^ flip_z) * 8 + (3 - x if flip_x else x) * 2 + core


def leaf_route(value, target):
    return lax.ppermute(value, "leaf", [(i, target(i)) for i in range(LEAVES)])


def leaf_xor(value, bit):
    return leaf_route(value, lambda i: i ^ bit)


def leaf_from(value, step):
    return leaf_route(value, lambda i: (i - step) % LEAVES)


def siblings(value):
    return [value] + [
        leaf_route(value, lambda i, d=d: facing(i, d & 1, d >> 1)) for d in (1, 2, 3)
    ]


def z_from(value, even, odd):
    route = []
    for i in range(LEAVES):
        step = odd if i // 8 % 2 else even
        route.append(((i + 8 * step) % LEAVES, i))
    return lax.ppermute(value, "leaf", route)


def col_shift(value, step):
    return lax.ppermute(value, "col", [(i, (i + step) % 4) for i in range(4)])


def gather4(value, groups):
    return lax.all_gather(value, "leaf", axis=0, axis_index_groups=groups)


NN = ((1,), (0,))
NT = ((1,), (1,))


def dot(a, b, dims=NN):
    return lax.dot_general(a, b, (dims, ((), ())), preferred_element_type=F32)


def split(value):
    top = value.astype(BF16)
    return top, (value - top.astype(F32)).astype(BF16)


def dot3(a, b, dims=NN):
    at, al = split(a)
    bt, bl = split(b)
    return dot(at, bt, dims) + (dot(at, bl, dims) + dot(al, bt, dims))


SMEM = pl.BlockSpec(memory_space=pltpu.SMEM)
VMEM = pl.BlockSpec(memory_space=pltpu.VMEM)


def near_memory(value):
    return pltpu.with_memory_space_constraint(value, pltpu.VMEM)


def kernel(body, outs, values, scalars=(), scratch=()):
    result = pl.pallas_call(
        body,
        in_specs=[SMEM] * len(scalars) + [VMEM] * len(values),
        out_specs=[VMEM] * len(outs),
        out_shape=[pltpu.VMEM(shape, F32) for shape in outs],
        scratch_shapes=list(scratch),
        compiler_params=pltpu.CompilerParams(vmem_limit_bytes=20 << 20),
    )(*scalars, *[near_memory(value) for value in values])
    return result if len(outs) > 1 else result[0]


def like(*shape, dtype=F32):
    return jax.ShapeDtypeStruct(shape, dtype)


CHUNK = 512


def two_part(value):
    top, low = split(value)
    return jnp.concatenate([top, low], axis=1), top.astype(F32) + low.astype(F32)


def tile_setup(place, xs, blocks, rows, norms, squares, others, tops, lows):
    for k, ref in enumerate(xs):
        at = (place[2] + 4 - k) % 4
        rows[at], exact = two_part(ref[...])
        norms[at] = jnp.sum(exact * exact, axis=1, keepdims=True)
    for k, (y, a) in enumerate(blocks):
        others[k], exact = two_part(y)
        total = jnp.sum(exact * exact, axis=1, keepdims=True)
        squares[k] = jnp.transpose(jnp.broadcast_to(total, (Q, 128)))[:8]
        tops[k], lows[k] = split(a)


def tile_sum(i, weights, rows, norms, squares, others, tops, lows):
    x = rows[pl.ds(2 * i, 2)].reshape(CHUNK, 256)
    own = norms[pl.ds(2 * i, 2)].reshape(CHUNK, 1)
    total = None
    for k, weight in enumerate(weights):
        top, low = others[k][:, :128], others[k][:, 128:]
        inner = dot(x, jnp.concatenate([top, top], axis=1), NT)
        inner = inner + dot(x, jnp.concatenate([low, low], axis=1), NT)
        distance = own + squares[k][:1] - 2.0 * inner
        top, low = split(jnp.exp(distance * (-2.0 / 128.0)) * weight)
        term = dot(top, tops[k]) + dot(top, lows[k]) + dot(low, tops[k])
        total = term if total is None else total + term
    return total


def near_kernel(place, mask, x0, x1, x2, x3, p0, p1, out, *scratch):
    blocks = [(p[:, :128], p[:, 128:]) for p in (p0, p1)]
    tile_setup(place, (x0, x1, x2, x3), blocks, *scratch)
    weights = (mask[0, 2].astype(F32), mask[0, 3 - 2 * place[0]].astype(F32))

    @pl.loop(0, 2)
    def _(i):
        out[pl.ds(pl.multiple_of(i * CHUNK, CHUNK), CHUNK), :] = tile_sum(i, weights, *scratch)


def far_kernel(
    place, mask, ridge, x0, x1, x2, x3, p0, p1, p2, near, own_y, own_a, lead, out, led, *scratch
):
    blocks = [(p[:, :128], p[:, 128:]) for p in (p0, p1, p2)]
    tile_setup(place, (x0, x1, x2, x3), blocks, *scratch)
    weights = (
        mask[0, 0].astype(F32),
        mask[0, 4].astype(F32),
        mask[0, 1 + 2 * place[0]].astype(F32),
    )
    for k in range(4):
        led[k] = jnp.zeros((RANK, 128), F32)

    @pl.loop(0, 2)
    def _(i):
        rows = pl.ds(pl.multiple_of(i * CHUNK, CHUNK), CHUNK)
        total = near[rows, :] + tile_sum(i, weights, *scratch)
        own = own_y[...] - ridge[0] * own_a[...]
        part = jnp.concatenate(
            [
                jnp.where(place[2] == 2 * i + h, own, 0.0) - total[h * Q : (h + 1) * Q]
                for h in range(2)
            ],
            axis=0,
        )
        product = dot3(lead[:, rows], part)
        for k in range(4):
            out[k, rows, :] = part[:, k * 128 : (k + 1) * 128]
            led[k] += product[:, k * 128 : (k + 1) * 128]


def tile_scratch(count):
    return [
        pltpu.VMEM((4, Q, 256), BF16),
        pltpu.VMEM((4, Q, 1), F32),
        pltpu.VMEM((count, 8, Q), F32),
        pltpu.VMEM((count, Q, 256), BF16),
        pltpu.VMEM((count, Q, 512), BF16),
        pltpu.VMEM((count, Q, 512), BF16),
    ]


def near_call(place, mask, xs, blocks):
    return kernel(near_kernel, [(1024, 512)], [*xs, *blocks], (place, mask), tile_scratch(2))


def far_call(place, mask, ridge, xs, blocks, near, own_y, own_a, lead):
    return kernel(
        far_kernel,
        [(4, 1024, 128), (4, RANK, 128)],
        [*xs, *blocks, near, own_y, own_a, lead],
        (place, mask, ridge),
        tile_scratch(3),
    )


def picks_by_row(order, picks):
    at = lax.broadcasted_iota(jnp.int32, picks.shape, 0)
    picks[...] = jnp.where(order == at, 1.0, 0.0).astype(BF16)


def lead_kernel(order, basis, solve, lead, picks):
    picks_by_row(order[...], picks)
    turned = jnp.transpose(basis[0])
    both = jnp.concatenate(split(dot3(turned, solve[0])), axis=0)
    chosen = dot(both, picks[...], NT)
    lead[...] = chosen[:RANK] + chosen[RANK:]


def lead_call(order, leaf_basis, leaf_inverse):
    return kernel(
        lead_kernel,
        [(RANK, 1024)],
        [order, leaf_basis, leaf_inverse],
        scratch=[pltpu.VMEM((1024, 1024), BF16)],
    )


def pack_kernel(a, b, out):
    out[:, :128] = a[...]
    out[:, 128:] = b[...]


def pack_call(a, b):
    return kernel(pack_kernel, [(Q, 640)], [a, b])


def fill_slices(transfer, inverse, out, start):
    out[start : start + 64, :] = transfer[0, 256:320, :]
    for k in range(4):
        at = start + 64 + k * 16
        out[at : at + 16, :] = inverse[0, 320:336, k * 256 : (k + 1) * 256]


def slices_kernel(transfer, inverse, out):
    fill_slices(transfer, inverse, out, 0)


def pair_kernel(transfer, inverse, lower, out):
    fill_slices(transfer, inverse, out, 0)
    out[128:, :] = lower[...]


def held_kernel(transfer, inverse, lower, mirrored, out):
    out[:256, :] = transfer[0, :256, :]
    for k in range(4):
        at = 256 + k * 64
        out[at : at + 64, :] = inverse[0, 256:320, k * 256 : (k + 1) * 256]
    fill_slices(transfer, inverse, out, 512)
    out[640:768, :] = lower[...]
    out[768:, :] = mirrored[...]


def collect(body, rows, *parts):
    return kernel(body, [(rows, 256)], parts)


def nodes_kernel(place, b0, b1, b2, b3, e1, m2, f2, m3, own_e2, e2):
    q = place[3] % 4
    child = place[3] // 4 % 4
    parent = place[3] // 16
    odd = place[3] // 8 % 2
    for d, block in enumerate((b0, b1, b2, b3)):
        at = q ^ d
        e1[pl.ds(pl.multiple_of(at * 256, 256), 256), :] = block[:256, :]
        rows = pl.ds(pl.multiple_of(at * 64, 64), 64)
        for k in range(4):
            source = pl.multiple_of(256 + (child ^ k) * 64, 64)
            m2[rows, k * 256 : (k + 1) * 256] = block[pl.ds(source, 64), :]
        for s, (start, flip) in enumerate(((512, 0), (768, 2), (640, 0), (896, 2))):
            held = at ^ flip
            e2[pl.ds(pl.multiple_of(s * 256 + held * 64, 64), 64), :] = block[
                start : start + 64, :
            ]
            rows = pl.ds(pl.multiple_of((child ^ s) * 64 + held * 16, 16), 16)
            for k in range(4):
                step = (0, 3, 1, 2)[k] + odd * (0, -2, 2, 0)[k]
                source = pl.multiple_of(start + 64 + (parent + step) % 4 * 16, 16)
                m3[rows, k * 256 : (k + 1) * 256] = block[pl.ds(source, 16), :]
    own_e2[...] = e2[:256, :]
    f2[...] = dot3(m2[...], e2[...])


def nodes_call(place, blocks):
    return kernel(
        nodes_kernel,
        [(1024, 256), (256, 1024), (256, 256), (256, 1024), (256, 256)],
        blocks,
        (place,),
        [pltpu.VMEM((1024, 256), F32)],
    )


def level1_kernel(place, leaf_map, stacked, m1, e1, w1, p1):
    base = place[3] // 4 * 4
    total = None
    for k in range(4):
        term = dot3(m1[0, :256, k * 256 : (k + 1) * 256], stacked[leaf_map[base + k] - base])
        total = term if total is None else total + term
    w1[...] = total
    p1[...] = dot3(jnp.transpose(total), e1[0, :256, :])


def level1_call(place, leaf_map, stacked, node_inverse, node_transfer):
    return kernel(
        level1_kernel,
        [(256, 128), (128, 256)],
        [stacked, node_inverse, node_transfer],
        (place, leaf_map),
    )


def row_blocks(parts, matrix):
    total = None
    for k, part in enumerate(parts):
        term = dot3(part[...], matrix[:, k * 256 : (k + 1) * 256], NT)
        total = term if total is None else total + term
    return total


def level2_kernel(r0, r1, r2, r3, m2, e2, w2, p2):
    total = row_blocks((r0, r1, r2, r3), m2)
    w2[...] = total
    p2[...] = dot3(total, e2[...])


def level2_call(parts, m2, e2):
    return kernel(level2_kernel, [(32, 256), (32, 256)], [*parts, m2, e2])


def upper_kernel(r0, r1, r2, r3, m3, f2, w2, g1):
    g2 = row_blocks((r0, r1, r2, r3), m3)
    g1[...] = w2[...] - dot3(g2, f2[...], NT)


def upper_call(parts, m3, f2, w2):
    return kernel(upper_kernel, [(32, 256)], [*parts, m3, f2, w2])


def down1_kernel(g1, e1, m1, w1, v1):
    g = g1[...].reshape(128, 256)
    lifted = dot3(g, e1[...], NT)
    v1[...] = w1[...] - dot3(m1[0, :256, :], lifted, NT)


def down1_call(g1, e1, node_inverse, w1):
    return kernel(down1_kernel, [(256, 128)], [g1, e1, node_inverse, w1])


def residual_kernel(order, parts, res, ordered, picks):
    res_sum = parts[0] + parts[1] + (parts[2] + parts[3])
    res[...] = res_sum
    rows = jnp.broadcast_to(order[...].astype(F32), (128, 1024))
    holds = jnp.transpose(rows)[:, :1].astype(jnp.int32)
    at = lax.broadcasted_iota(jnp.int32, (1024, 1024), 1)
    picks[...] = jnp.where(holds == at, 1.0, 0.0).astype(BF16)
    both = dot(picks[...], jnp.concatenate(split(res_sum), axis=1))
    ordered[...] = both[:, :128] + both[:, 128:]


def residual_call(order, parts):
    return kernel(
        residual_kernel,
        [(1024, 128), (1024, 128)],
        [order, parts],
        scratch=[pltpu.VMEM((1024, 1024), BF16)],
    )


def finish_kernel(place, leaf_map, order, pieces, ordered, basis, solve, delta, picks, rhs, sides):
    base = place[3] // 4 * 4
    slot = jnp.int32(3)
    for k in range(3):
        slot = jnp.where(leaf_map[base + k] == place[3], k, slot)
    rhs[...] = jnp.concatenate(
        split(ordered[...] - dot3(basis[0], pieces[slot])), axis=1
    )
    picks_by_row(order[...], picks)

    @pl.loop(0, 2)
    def _(i):
        rows = pl.ds(pl.multiple_of(i * CHUNK, CHUNK), CHUNK)
        a, b = split(solve[0, rows, :])
        both = dot(a, rhs[...])
        y = both[:, :128] + (both[:, 128:] + dot(b, rhs[:, :128]))
        sides[rows, :] = jnp.concatenate(split(y), axis=1)

    @pl.loop(0, 2)
    def _(i):
        rows = pl.ds(pl.multiple_of(i * CHUNK, CHUNK), CHUNK)
        both = dot(picks[rows, :], sides[...])
        delta[rows, :] = both[:, :128] + both[:, 128:]


def finish_call(place, leaf_map, order, pieces, ordered, leaf_basis, leaf_inverse):
    return kernel(
        finish_kernel,
        [(1024, 128)],
        [order, pieces, ordered, leaf_basis, leaf_inverse],
        (place, leaf_map),
        [
            pltpu.VMEM((1024, 1024), BF16),
            pltpu.VMEM((1024, 256), BF16),
            pltpu.VMEM((1024, 256), BF16),
        ],
    )


def outputs_kernel(res, delta, coefs, out_res, out_new):
    for k in range(4):
        at = slice(k * 128, (k + 1) * 128)
        out_res[:, at] = res[k]
        out_new[:, at] = coefs[:, at] + delta[k]


def outputs_call(res, delta, coefs):
    return pl.pallas_call(
        outputs_kernel,
        in_specs=[VMEM] * 3,
        out_shape=[like(Q, 512), like(Q, 512)],
        compiler_params=pltpu.CompilerParams(vmem_limit_bytes=8 << 20),
        name="outputs",
    )(*[near_memory(value) for value in (res, delta, coefs)])


def swap_cols(value):
    return lax.all_to_all(value, "col", 0, 0, tiled=True)


def step(
    points,
    coefs,
    targets,
    ridge,
    tile_mask,
    cluster_perm,
    leaf_map,
    leaf_inverse,
    leaf_basis,
    node_inverse,
    node_transfer,
):
    col = lax.axis_index("col")
    leaf = lax.axis_index("leaf")
    core = leaf % 2
    place = jnp.stack([core, leaf // 2 % 2, col, leaf]).astype(jnp.int32)

    xs = [points] + [col_shift(points, d) for d in (1, 2, 3)]
    packed = pack_call(points, coefs)
    left, right = leaf_from(packed, -2), leaf_from(packed, 2)
    partner = leaf_xor(packed, 1)
    relay = leaf_xor(jnp.where(core == 0, right, left), 1)

    nodes = (node_transfer, node_inverse)
    lower = leaf_route(collect(slices_kernel, 128, *nodes), lambda i: facing(i, 0, 1))
    mirrored = leaf_route(collect(pair_kernel, 256, *nodes, lower), lambda i: facing(i, 1, 0))
    held = collect(held_kernel, 1024, *nodes, lower, mirrored)

    lead = lead_call(cluster_perm, leaf_basis, leaf_inverse)

    near = near_call(place, tile_mask, xs, (packed, partner))
    near, held = lax.optimization_barrier((near, held))
    across = leaf_xor(held, 2)
    own_core = leaf_xor(held, 1)
    both_ways = leaf_xor(across, 1)
    partial, led = far_call(
        place, tile_mask, ridge, xs, (left, right, relay), near, targets, coefs, lead
    )
    reduced = swap_cols(led).sum(0)
    e1, m2, f2, m3, e2 = nodes_call(place, (held, own_core, across, both_ways))

    partial, _ = lax.optimization_barrier((partial, reduced))
    columns = swap_cols(partial)

    w1, p1 = level1_call(place, leaf_map, gather4(reduced, G4), node_inverse, node_transfer)
    p1 = lax.all_to_all(p1, "leaf", 0, 0, axis_index_groups=GK, tiled=True)
    r1 = p1.reshape(4, 32, RANK).sum(0)
    w2, p2 = level2_call(siblings(r1), m2, e2)
    r2 = sum(siblings(p2))
    r2s = [r2, z_from(r2, -1, 1), z_from(r2, 2, -2), z_from(r2, -3, 3)]
    g1 = upper_call(r2s, m3, f2, w2)
    columns, g1 = lax.optimization_barrier((columns, g1))
    res, ordered = residual_call(cluster_perm, columns)
    res_rows = swap_cols(res.reshape(4, Q, 128))
    g1 = gather4(g1, GK)
    pieces = gather4(down1_call(g1, e1, node_inverse, w1), G4)

    delta = finish_call(place, leaf_map, cluster_perm, pieces, ordered, leaf_basis, leaf_inverse)
    return outputs_call(res_rows, swap_cols(delta.reshape(4, Q, 128)), coefs)


def solution(mesh):
    return jax.shard_map(
        step,
        mesh=mesh,
        in_specs=(
            P(("leaf", "col"), None),
            P(("leaf", "col"), None),
            P(("leaf", "col"), None),
            P(),
            P("leaf", None),
            P("leaf", None),
            P(),
            P("leaf", None, None),
            P("leaf", None, None),
            P("leaf", None, None),
            P("leaf", None, None),
        ),
        out_specs=(P(("leaf", "col"), None), P(("leaf", "col"), None)),
        check_vma=False,
    )
```

```python
import jax
import jax.numpy as jnp
from jax import lax
from jax.experimental import pallas as pl
from jax.experimental.pallas import tpu as pltpu
from jax.sharding import PartitionSpec as P


F32 = jnp.float32
BF16 = jnp.bfloat16
Q = 256
RANK = 256
LEAVES = 64


def leaf_at(z, x_hi, kappa):
    x = 2 * x_hi + ((kappa >> 1) ^ x_hi)
    return z * 8 + x * 2 + (kappa & 1)


G4 = [[4 * n + k for k in range(4)] for n in range(16)]
GK = [[leaf_at(z, xh, k) for k in range(4)] for z in range(8) for xh in range(2)]


def facing(i, flip_x, flip_z):
    z, x, core = i // 8, i // 2 % 4, i % 2
    return (z ^ flip_z) * 8 + (3 - x if flip_x else x) * 2 + core


def leaf_route(value, target):
    return lax.ppermute(value, "leaf", [(i, target(i)) for i in range(LEAVES)])


def leaf_xor(value, bit):
    return leaf_route(value, lambda i: i ^ bit)


def leaf_from(value, step):
    return leaf_route(value, lambda i: (i - step) % LEAVES)


def siblings(value):
    return [value] + [
        leaf_route(value, lambda i, d=d: facing(i, d & 1, d >> 1)) for d in (1, 2, 3)
    ]


def z_from(value, even, odd):
    route = []
    for i in range(LEAVES):
        step = odd if i // 8 % 2 else even
        route.append(((i + 8 * step) % LEAVES, i))
    return lax.ppermute(value, "leaf", route)


def col_shift(value, step):
    return lax.ppermute(value, "col", [(i, (i + step) % 4) for i in range(4)])


def gather4(value, groups):
    return lax.all_gather(value, "leaf", axis=0, axis_index_groups=groups)


NN = ((1,), (0,))
NT = ((1,), (1,))


def dot(a, b, dims=NN):
    return lax.dot_general(a, b, (dims, ((), ())), preferred_element_type=F32)


def split(value):
    top = value.astype(BF16)
    return top, (value - top.astype(F32)).astype(BF16)


def dot3(a, b, dims=NN):
    at, al = split(a)
    bt, bl = split(b)
    return dot(at, bt, dims) + (dot(at, bl, dims) + dot(al, bt, dims))


SMEM = pl.BlockSpec(memory_space=pltpu.SMEM)
VMEM = pl.BlockSpec(memory_space=pltpu.VMEM)
HBM = pl.BlockSpec(memory_space=pltpu.HBM)


def near_memory(value):
    return pltpu.with_memory_space_constraint(value, pltpu.VMEM)


def far_memory(value):
    return pltpu.with_memory_space_constraint(value, pltpu.HBM)


def kernel(body, outs, values, scalars=(), scratch=(), far_values=(), far_outs=()):
    result = pl.pallas_call(
        body,
        in_specs=[SMEM] * len(scalars) + [VMEM] * len(values) + [HBM] * len(far_values),
        out_specs=[VMEM] * len(outs) + [HBM] * len(far_outs),
        out_shape=[pltpu.VMEM(shape, F32) for shape in outs]
        + [pltpu.HBM(shape, F32) for shape in far_outs],
        scratch_shapes=list(scratch),
        compiler_params=pltpu.CompilerParams(vmem_limit_bytes=20 << 20),
    )(*scalars, *[near_memory(value) for value in values], *[far_memory(value) for value in far_values])
    return result if len(outs) + len(far_outs) > 1 else result[0]


def like(*shape, dtype=F32):
    return jax.ShapeDtypeStruct(shape, dtype)


CHUNK = 512


def two_part(value):
    top, low = split(value)
    return jnp.concatenate([top, low], axis=1), top.astype(F32) + low.astype(F32)


def tile_setup(place, xs, blocks, rows, norms, squares, others, tops, lows):
    for k, ref in enumerate(xs):
        at = (place[2] + 4 - k) % 4
        rows[at], exact = two_part(ref[...])
        norms[at] = jnp.sum(exact * exact, axis=1, keepdims=True)
    for k, (y, a) in enumerate(blocks):
        others[k], exact = two_part(y)
        total = jnp.sum(exact * exact, axis=1, keepdims=True)
        squares[k] = jnp.transpose(jnp.broadcast_to(total, (Q, 128)))[:8]
        tops[k], lows[k] = split(a)


def tile_sum(i, weights, rows, norms, squares, others, tops, lows):
    x = rows[pl.ds(2 * i, 2)].reshape(CHUNK, 256)
    own = norms[pl.ds(2 * i, 2)].reshape(CHUNK, 1)
    total = None
    for k, weight in enumerate(weights):
        top, low = others[k][:, :128], others[k][:, 128:]
        inner = dot(x, jnp.concatenate([top, top], axis=1), NT)
        inner = inner + dot(x, jnp.concatenate([low, low], axis=1), NT)
        distance = own + squares[k][:1] - 2.0 * inner
        top, low = split(jnp.exp(distance * (-2.0 / 128.0)) * weight)
        term = dot(top, tops[k]) + dot(top, lows[k]) + dot(low, tops[k])
        total = term if total is None else total + term
    return total


def near_kernel(place, mask, x0, x1, x2, x3, p0, p1, out, *scratch):
    blocks = [(p[:, :128], p[:, 128:]) for p in (p0, p1)]
    tile_setup(place, (x0, x1, x2, x3), blocks, *scratch)
    weights = (mask[0, 2].astype(F32), mask[0, 3 - 2 * place[0]].astype(F32))

    @pl.loop(0, 2)
    def _(i):
        out[pl.ds(pl.multiple_of(i * CHUNK, CHUNK), CHUNK), :] = tile_sum(i, weights, *scratch)


def far_kernel(
    place, mask, ridge, x0, x1, x2, x3, p0, p1, p2, near, own_y, own_a, lead,
    led, out, parts, sems, *scratch
):
    blocks = [(p[:, :128], p[:, 128:]) for p in (p0, p1, p2)]
    tile_setup(place, (x0, x1, x2, x3), blocks, *scratch)
    weights = (
        mask[0, 0].astype(F32),
        mask[0, 4].astype(F32),
        mask[0, 1 + 2 * place[0]].astype(F32),
    )
    for k in range(4):
        led[k] = jnp.zeros((RANK, 128), F32)

    def sent(i):
        rows = pl.ds(pl.multiple_of(i * CHUNK, CHUNK), CHUNK)
        return pltpu.make_async_copy(parts.at[i], out.at[:, rows, :], sems.at[i])

    @pl.loop(0, 2)
    def _(i):
        rows = pl.ds(pl.multiple_of(i * CHUNK, CHUNK), CHUNK)
        total = near[rows, :] + tile_sum(i, weights, *scratch)
        own = own_y[...] - ridge[0] * own_a[...]
        part = jnp.concatenate(
            [
                jnp.where(place[2] == 2 * i + h, own, 0.0) - total[h * Q : (h + 1) * Q]
                for h in range(2)
            ],
            axis=0,
        )
        product = dot3(lead[:, rows], part)
        for k in range(4):
            parts[i, k] = part[:, k * 128 : (k + 1) * 128]
            led[k] += product[:, k * 128 : (k + 1) * 128]
        sent(i).start()

    for i in range(2):
        sent(i).wait()


def tile_scratch(count):
    return [
        pltpu.VMEM((4, Q, 256), BF16),
        pltpu.VMEM((4, Q, 1), F32),
        pltpu.VMEM((count, 8, Q), F32),
        pltpu.VMEM((count, Q, 256), BF16),
        pltpu.VMEM((count, Q, 512), BF16),
        pltpu.VMEM((count, Q, 512), BF16),
    ]


def near_call(place, mask, xs, blocks):
    return kernel(near_kernel, [(1024, 512)], [*xs, *blocks], (place, mask), tile_scratch(2))


def far_call(place, mask, ridge, xs, blocks, near, own_y, own_a, lead):
    return kernel(
        far_kernel,
        [(4, RANK, 128)],
        [*xs, *blocks, near, own_y, own_a, lead],
        (place, mask, ridge),
        [pltpu.VMEM((2, 4, CHUNK, 128), F32), pltpu.SemaphoreType.DMA((2,))] + tile_scratch(3),
        far_outs=[(4, 1024, 128)],
    )


def picks_by_row(order, picks):
    at = lax.broadcasted_iota(jnp.int32, picks.shape, 0)
    picks[...] = jnp.where(order == at, 1.0, 0.0).astype(BF16)


def load_solve(basis, solve, basis_in, solve_in, sems):
    copies = [pltpu.make_async_copy(basis.at[0], basis_in, sems.at[4])]
    for k in range(4):
        rows = pl.ds(k * Q, Q)
        copies.append(
            pltpu.make_async_copy(solve.at[0, rows, :], solve_in.at[rows, :], sems.at[k])
        )
    for copy in copies:
        copy.start()
    return copies


SOLVE_SCRATCH = [
    pltpu.VMEM((1024, RANK), F32),
    pltpu.VMEM((1024, 1024), F32),
    pltpu.SemaphoreType.DMA((5,)),
]


def lead_kernel(order, basis, solve, lead, basis_in, solve_in, sems, picks, turned):
    first, *rest = load_solve(basis, solve, basis_in, solve_in, sems)
    picks_by_row(order[...], picks)
    first.wait()
    turned[...] = jnp.transpose(basis_in[...])
    for k in range(4):
        rest[k].wait()
        rows = slice(k * Q, (k + 1) * Q)
        term = dot3(turned[:, rows], solve_in[rows, :])
        if k:
            lead[...] += term
        else:
            lead[...] = term
    both = jnp.concatenate(split(lead[...]), axis=0)
    chosen = dot(both, picks[...], NT)
    lead[...] = chosen[:RANK] + chosen[RANK:]


def lead_call(order, leaf_basis, leaf_inverse):
    return kernel(
        lead_kernel,
        [(RANK, 1024)],
        [order],
        scratch=SOLVE_SCRATCH
        + [pltpu.VMEM((1024, 1024), BF16), pltpu.VMEM((RANK, 1024), F32)],
        far_values=[leaf_basis, leaf_inverse],
    )


def run_copies(sems, moves):
    copies = [
        pltpu.make_async_copy(source, target, sems.at[k])
        for k, (source, target) in enumerate(moves)
    ]
    for copy in copies:
        copy.start()
    for copy in copies:
        copy.wait()


def mover(body, shape, count, *parts):
    return pl.pallas_call(
        body,
        in_specs=[HBM] * len(parts),
        out_specs=HBM,
        out_shape=like(*shape),
        scratch_shapes=[pltpu.SemaphoreType.DMA((count,))],
        compiler_params=pltpu.CompilerParams(vmem_limit_bytes=4 << 20),
    )(*[far_memory(part) for part in parts])


def pack_kernel(a, b, out, sems):
    run_copies(sems, [(a, out.at[:, pl.ds(0, 128)]), (b, out.at[:, pl.ds(128, 512)])])


def slice_moves(transfer, inverse, out, start):
    moves = [(transfer.at[0, pl.ds(256, 64), :], out.at[pl.ds(start, 64), :])]
    for k in range(4):
        source = inverse.at[0, pl.ds(320, 16), pl.ds(k * 256, 256)]
        moves.append((source, out.at[pl.ds(start + 64 + k * 16, 16), :]))
    return moves


def slices_kernel(transfer, inverse, out, sems):
    run_copies(sems, slice_moves(transfer, inverse, out, 0))


def pair_kernel(slices, lower, out, sems):
    run_copies(sems, [(slices, out.at[pl.ds(0, 128), :]), (lower, out.at[pl.ds(128, 128), :])])


def held_kernel(transfer, inverse, pair, mirrored, out, sems):
    moves = [
        (transfer.at[0, pl.ds(0, 256), :], out.at[pl.ds(0, 256), :]),
        (pair, out.at[pl.ds(512, 256), :]),
        (mirrored, out.at[pl.ds(768, 256), :]),
    ]
    for k in range(4):
        source = inverse.at[0, pl.ds(256, 64), pl.ds(k * 256, 256)]
        moves.append((source, out.at[pl.ds(256 + k * 64, 64), :]))
    run_copies(sems, moves)


def nodes_kernel(place, b0, b1, b2, b3, e1, m2, f2, m3, own_e2, e2):
    q = place[3] % 4
    child = place[3] // 4 % 4
    parent = place[3] // 16
    odd = place[3] // 8 % 2
    for d, block in enumerate((b0, b1, b2, b3)):
        at = q ^ d
        e1[pl.ds(pl.multiple_of(at * 256, 256), 256), :] = block[:256, :]
        rows = pl.ds(pl.multiple_of(at * 64, 64), 64)
        for k in range(4):
            source = pl.multiple_of(256 + (child ^ k) * 64, 64)
            m2[rows, k * 256 : (k + 1) * 256] = block[pl.ds(source, 64), :]
        for s, (start, flip) in enumerate(((512, 0), (768, 2), (640, 0), (896, 2))):
            held = at ^ flip
            e2[pl.ds(pl.multiple_of(s * 256 + held * 64, 64), 64), :] = block[
                start : start + 64, :
            ]
            rows = pl.ds(pl.multiple_of((child ^ s) * 64 + held * 16, 16), 16)
            for k in range(4):
                step = (0, 3, 1, 2)[k] + odd * (0, -2, 2, 0)[k]
                source = pl.multiple_of(start + 64 + (parent + step) % 4 * 16, 16)
                m3[rows, k * 256 : (k + 1) * 256] = block[pl.ds(source, 16), :]
    own_e2[...] = e2[:256, :]
    f2[...] = dot3(m2[...], e2[...])


def nodes_call(place, blocks):
    return kernel(
        nodes_kernel,
        [(1024, 256), (256, 1024), (256, 256), (256, 1024), (256, 256)],
        blocks,
        (place,),
        [pltpu.VMEM((1024, 256), F32)],
    )


def level1_kernel(place, leaf_map, stacked, m1, e1, w1, p1):
    base = place[3] // 4 * 4
    total = None
    for k in range(4):
        term = dot3(m1[0, :256, k * 256 : (k + 1) * 256], stacked[leaf_map[base + k] - base])
        total = term if total is None else total + term
    w1[...] = total
    p1[...] = dot3(jnp.transpose(total), e1[0, :256, :])


def level1_call(place, leaf_map, stacked, node_inverse, node_transfer):
    return kernel(
        level1_kernel,
        [(256, 128), (128, 256)],
        [stacked, node_inverse, node_transfer],
        (place, leaf_map),
    )


def row_blocks(parts, matrix):
    total = None
    for k, part in enumerate(parts):
        term = dot3(part[...], matrix[:, k * 256 : (k + 1) * 256], NT)
        total = term if total is None else total + term
    return total


def level2_kernel(r0, r1, r2, r3, m2, e2, w2, p2):
    total = row_blocks((r0, r1, r2, r3), m2)
    w2[...] = total
    p2[...] = dot3(total, e2[...])


def level2_call(parts, m2, e2):
    return kernel(level2_kernel, [(32, 256), (32, 256)], [*parts, m2, e2])


def upper_kernel(r0, r1, r2, r3, m3, f2, w2, g1):
    g2 = row_blocks((r0, r1, r2, r3), m3)
    g1[...] = w2[...] - dot3(g2, f2[...], NT)


def upper_call(parts, m3, f2, w2):
    return kernel(upper_kernel, [(32, 256)], [*parts, m3, f2, w2])


def down1_kernel(g1, e1, m1, w1, v1):
    g = g1[...].reshape(128, 256)
    lifted = dot3(g, e1[...], NT)
    v1[...] = w1[...] - dot3(m1[0, :256, :], lifted, NT)


def down1_call(g1, e1, node_inverse, w1):
    return kernel(down1_kernel, [(256, 128)], [g1, e1, node_inverse, w1])


def residual_kernel(order, parts, res_out, ordered_out, picks, res, ordered, sems):
    res_sum = parts[0] + parts[1] + (parts[2] + parts[3])
    res[...] = res_sum
    rows = jnp.broadcast_to(order[...].astype(F32), (128, 1024))
    holds = jnp.transpose(rows)[:, :1].astype(jnp.int32)
    at = lax.broadcasted_iota(jnp.int32, (1024, 1024), 1)
    picks[...] = jnp.where(holds == at, 1.0, 0.0).astype(BF16)
    both = dot(picks[...], jnp.concatenate(split(res_sum), axis=1))
    ordered[...] = both[:, :128] + both[:, 128:]
    run_copies(sems, [(res, res_out), (ordered, ordered_out)])


def residual_call(order, parts):
    return kernel(
        residual_kernel,
        [],
        [order, parts],
        scratch=[
            pltpu.VMEM((1024, 1024), BF16),
            pltpu.VMEM((1024, 128), F32),
            pltpu.VMEM((1024, 128), F32),
            pltpu.SemaphoreType.DMA((2,)),
        ],
        far_outs=[(1024, 128), (1024, 128)],
    )


def finish_kernel(
    place, leaf_map, order, pieces, ordered, basis, solve, delta,
    basis_in, solve_in, sems, picks, rhs, sides,
):
    first, *rest = load_solve(basis, solve, basis_in, solve_in, sems)
    base = place[3] // 4 * 4
    slot = jnp.int32(3)
    for k in range(3):
        slot = jnp.where(leaf_map[base + k] == place[3], k, slot)
    picks_by_row(order[...], picks)
    first.wait()
    rhs[...] = jnp.concatenate(
        split(ordered[...] - dot3(basis_in[...], pieces[slot])), axis=1
    )
    for k in range(4):
        rest[k].wait()
        rows = slice(k * Q, (k + 1) * Q)
        a, b = split(solve_in[rows, :])
        both = dot(a, rhs[...])
        y = both[:, :128] + (both[:, 128:] + dot(b, rhs[:, :128]))
        sides[rows, :] = jnp.concatenate(split(y), axis=1)

    @pl.loop(0, 2)
    def _(i):
        rows = pl.ds(pl.multiple_of(i * CHUNK, CHUNK), CHUNK)
        both = dot(picks[rows, :], sides[...])
        delta[rows, :] = both[:, :128] + both[:, 128:]


def finish_call(place, leaf_map, order, pieces, ordered, leaf_basis, leaf_inverse):
    return kernel(
        finish_kernel,
        [(1024, 128)],
        [order, pieces, ordered],
        (place, leaf_map),
        SOLVE_SCRATCH
        + [
            pltpu.VMEM((1024, 1024), BF16),
            pltpu.VMEM((1024, 256), BF16),
            pltpu.VMEM((1024, 256), BF16),
        ],
        [leaf_basis, leaf_inverse],
    )


def outputs_kernel(res, delta, coefs, out_res, out_new):
    for k in range(4):
        at = slice(k * 128, (k + 1) * 128)
        out_res[:, at] = res[k]
        out_new[:, at] = coefs[:, at] + delta[k]


def outputs_call(res, delta, coefs):
    return pl.pallas_call(
        outputs_kernel,
        in_specs=[VMEM] * 3,
        out_shape=[like(Q, 512), like(Q, 512)],
        compiler_params=pltpu.CompilerParams(vmem_limit_bytes=8 << 20),
        name="outputs",
    )(*[near_memory(value) for value in (res, delta, coefs)])


def swap_cols(value):
    return lax.all_to_all(value, "col", 0, 0, tiled=True)


def step(
    points,
    coefs,
    targets,
    ridge,
    tile_mask,
    cluster_perm,
    leaf_map,
    leaf_inverse,
    leaf_basis,
    node_inverse,
    node_transfer,
):
    col = lax.axis_index("col")
    leaf = lax.axis_index("leaf")
    core = leaf % 2
    place = jnp.stack([core, leaf // 2 % 2, col, leaf]).astype(jnp.int32)

    xs = [points] + [col_shift(points, d) for d in (1, 2, 3)]
    packed = mover(pack_kernel, (Q, 640), 2, points, coefs)
    left, right = leaf_from(packed, -2), leaf_from(packed, 2)
    partner = leaf_xor(packed, 1)
    relay = leaf_xor(jnp.where(core == 0, right, left), 1)

    nodes = (node_transfer, node_inverse)
    slices = mover(slices_kernel, (128, 256), 5, *nodes)
    lower = leaf_route(slices, lambda i: facing(i, 0, 1))
    pair = mover(pair_kernel, (256, 256), 2, slices, lower)
    mirrored = leaf_route(pair, lambda i: facing(i, 1, 0))
    held = mover(held_kernel, (1024, 256), 7, *nodes, pair, mirrored)

    lead = lead_call(cluster_perm, leaf_basis, leaf_inverse)

    near = near_call(place, tile_mask, xs, (packed, partner))
    near, held = lax.optimization_barrier((near, held))
    across = leaf_xor(held, 2)
    own_core = leaf_xor(held, 1)
    both_ways = leaf_xor(across, 1)
    led, partial = far_call(
        place, tile_mask, ridge, xs, (left, right, relay), near, targets, coefs, lead
    )
    led = swap_cols(led)
    reduced = led.sum(0)
    e1, m2, f2, m3, e2 = nodes_call(place, (held, own_core, across, both_ways))

    columns = swap_cols(partial)

    w1, p1 = level1_call(place, leaf_map, gather4(reduced, G4), node_inverse, node_transfer)
    p1 = lax.all_to_all(p1, "leaf", 0, 0, axis_index_groups=GK, tiled=True)
    r1 = p1.reshape(4, 32, RANK).sum(0)
    w2, p2 = level2_call(siblings(r1), m2, e2)
    r2 = sum(siblings(p2))
    r2s = [r2, z_from(r2, -1, 1), z_from(r2, 2, -2), z_from(r2, -3, 3)]
    g1 = upper_call(r2s, m3, f2, w2)
    columns, g1 = lax.optimization_barrier((columns, g1))
    res, ordered = residual_call(cluster_perm, columns)
    res_rows = swap_cols(res.reshape(4, Q, 128))
    g1 = gather4(g1, GK)
    pieces = gather4(down1_call(g1, e1, node_inverse, w1), G4)

    delta = finish_call(place, leaf_map, cluster_perm, pieces, ordered, leaf_basis, leaf_inverse)
    return outputs_call(res_rows, swap_cols(delta.reshape(4, Q, 128)), coefs)


def solution(mesh):
    return jax.shard_map(
        step,
        mesh=mesh,
        in_specs=(
            P(("leaf", "col"), None),
            P(("leaf", "col"), None),
            P(("leaf", "col"), None),
            P(),
            P("leaf", None),
            P("leaf", None),
            P(),
            P("leaf", None, None),
            P("leaf", None, None),
            P("leaf", None, None),
            P("leaf", None, None),
        ),
        out_specs=(P(("leaf", "col"), None), P(("leaf", "col"), None)),
        check_vma=False,
    )
```

```python
import jax
import jax.numpy as jnp
from jax import lax
from jax.experimental import pallas as pl
from jax.experimental.pallas import tpu as pltpu
from jax.sharding import PartitionSpec as P


F32 = jnp.float32
BF16 = jnp.bfloat16
Q = 256
RANK = 256
LEAVES = 64


def leaf_at(z, x_hi, kappa):
    x = 2 * x_hi + ((kappa >> 1) ^ x_hi)
    return z * 8 + x * 2 + (kappa & 1)


G4 = [[4 * n + k for k in range(4)] for n in range(16)]
GK = [[leaf_at(z, xh, k) for k in range(4)] for z in range(8) for xh in range(2)]


def facing(i, flip_x, flip_z):
    z, x, core = i // 8, i // 2 % 4, i % 2
    return (z ^ flip_z) * 8 + (3 - x if flip_x else x) * 2 + core


def leaf_route(value, target):
    return lax.ppermute(value, "leaf", [(i, target(i)) for i in range(LEAVES)])


def leaf_xor(value, bit):
    return leaf_route(value, lambda i: i ^ bit)


def leaf_from(value, step):
    return leaf_route(value, lambda i: (i - step) % LEAVES)


def siblings(value):
    return [value] + [
        leaf_route(value, lambda i, d=d: facing(i, d & 1, d >> 1)) for d in (1, 2, 3)
    ]


def z_from(value, even, odd):
    route = []
    for i in range(LEAVES):
        step = odd if i // 8 % 2 else even
        route.append(((i + 8 * step) % LEAVES, i))
    return lax.ppermute(value, "leaf", route)


def col_shift(value, step):
    return lax.ppermute(value, "col", [(i, (i + step) % 4) for i in range(4)])


def gather4(value, groups):
    return lax.all_gather(value, "leaf", axis=0, axis_index_groups=groups)


NN = ((1,), (0,))
NT = ((1,), (1,))


def dot(a, b, dims=NN):
    return lax.dot_general(a, b, (dims, ((), ())), preferred_element_type=F32)


def split(value):
    top = value.astype(BF16)
    return top, (value - top.astype(F32)).astype(BF16)


def dot3(a, b, dims=NN):
    at, al = split(a)
    bt, bl = split(b)
    return dot(at, bt, dims) + (dot(at, bl, dims) + dot(al, bt, dims))


SMEM = pl.BlockSpec(memory_space=pltpu.SMEM)
VMEM = pl.BlockSpec(memory_space=pltpu.VMEM)
HBM = pl.BlockSpec(memory_space=pltpu.HBM)


def near_memory(value):
    return pltpu.with_memory_space_constraint(value, pltpu.VMEM)


def far_memory(value):
    return pltpu.with_memory_space_constraint(value, pltpu.HBM)


def kernel(body, outs, values, scalars=(), scratch=(), far_values=(), far_outs=()):
    result = pl.pallas_call(
        body,
        in_specs=[SMEM] * len(scalars) + [VMEM] * len(values) + [HBM] * len(far_values),
        out_specs=[VMEM] * len(outs) + [HBM] * len(far_outs),
        out_shape=[pltpu.VMEM(shape, F32) for shape in outs]
        + [pltpu.HBM(shape, F32) for shape in far_outs],
        scratch_shapes=list(scratch),
        compiler_params=pltpu.CompilerParams(vmem_limit_bytes=20 << 20),
    )(*scalars, *[near_memory(value) for value in values], *[far_memory(value) for value in far_values])
    return result if len(outs) + len(far_outs) > 1 else result[0]


def like(*shape, dtype=F32):
    return jax.ShapeDtypeStruct(shape, dtype)


CHUNK = 512


def two_part(value):
    top, low = split(value)
    return jnp.concatenate([top, low], axis=1), top.astype(F32) + low.astype(F32)


def tile_setup(place, xs, blocks, rows, norms, squares, others, tops, lows):
    for k, ref in enumerate(xs):
        at = (place[2] + 4 - k) % 4
        rows[at], exact = two_part(ref[...])
        norms[at] = jnp.sum(exact * exact, axis=1, keepdims=True)
    for k, (y, a) in enumerate(blocks):
        others[k], exact = two_part(y)
        total = jnp.sum(exact * exact, axis=1, keepdims=True)
        squares[k] = jnp.transpose(jnp.broadcast_to(total, (Q, 128)))[:8]
        tops[k], lows[k] = split(a)


def tile_sum(i, weights, rows, norms, squares, others, tops, lows):
    x = rows[pl.ds(2 * i, 2)].reshape(CHUNK, 256)
    own = norms[pl.ds(2 * i, 2)].reshape(CHUNK, 1)
    total = None
    for k, weight in enumerate(weights):
        top, low = others[k][:, :128], others[k][:, 128:]
        inner = dot(x, jnp.concatenate([top, top], axis=1), NT)
        inner = inner + dot(x, jnp.concatenate([low, low], axis=1), NT)
        distance = own + squares[k][:1] - 2.0 * inner
        top, low = split(jnp.exp(distance * (-2.0 / 128.0)) * weight)
        term = dot(top, tops[k]) + dot(top, lows[k]) + dot(low, tops[k])
        total = term if total is None else total + term
    return total


def near_kernel(place, mask, x0, x1, x2, x3, p0, p1, out, *scratch):
    blocks = [(p[:, :128], p[:, 128:]) for p in (p0, p1)]
    tile_setup(place, (x0, x1, x2, x3), blocks, *scratch)
    weights = (mask[0, 2].astype(F32), mask[0, 3 - 2 * place[0]].astype(F32))

    @pl.loop(0, 2)
    def _(i):
        out[pl.ds(pl.multiple_of(i * CHUNK, CHUNK), CHUNK), :] = tile_sum(i, weights, *scratch)


def far_kernel(
    place, mask, ridge, x0, x1, x2, x3, p0, p1, p2, near, own_y, own_a, lead,
    led, out0, out1, out2, out3, parts, sems, *scratch
):
    blocks = [(p[:, :128], p[:, 128:]) for p in (p0, p1, p2)]
    tile_setup(place, (x0, x1, x2, x3), blocks, *scratch)
    weights = (
        mask[0, 0].astype(F32),
        mask[0, 4].astype(F32),
        mask[0, 1 + 2 * place[0]].astype(F32),
    )
    for k in range(4):
        led[k] = jnp.zeros((RANK, 128), F32)

    def sent(i):
        rows = pl.ds(pl.multiple_of(i * CHUNK, CHUNK), CHUNK)
        return [
            pltpu.make_async_copy(
                parts.at[i, (place[2] + d) % 4], out.at[rows, :], sems.at[i, d]
            )
            for d, out in enumerate((out0, out1, out2, out3))
        ]

    @pl.loop(0, 2)
    def _(i):
        rows = pl.ds(pl.multiple_of(i * CHUNK, CHUNK), CHUNK)
        total = near[rows, :] + tile_sum(i, weights, *scratch)
        own = own_y[...] - ridge[0] * own_a[...]
        part = jnp.concatenate(
            [
                jnp.where(place[2] == 2 * i + h, own, 0.0) - total[h * Q : (h + 1) * Q]
                for h in range(2)
            ],
            axis=0,
        )
        product = dot3(lead[:, rows], part)
        for k in range(4):
            parts[i, k] = part[:, k * 128 : (k + 1) * 128]
            led[k] += product[:, k * 128 : (k + 1) * 128]
        for copy in sent(i):
            copy.start()

    for i in range(2):
        for copy in sent(i):
            copy.wait()


def tile_scratch(count):
    return [
        pltpu.VMEM((4, Q, 256), BF16),
        pltpu.VMEM((4, Q, 1), F32),
        pltpu.VMEM((count, 8, Q), F32),
        pltpu.VMEM((count, Q, 256), BF16),
        pltpu.VMEM((count, Q, 512), BF16),
        pltpu.VMEM((count, Q, 512), BF16),
    ]


def near_call(place, mask, xs, blocks):
    return kernel(
        near_kernel, [(1024, 512)], [*xs, *blocks], (place, mask), tile_scratch(2)
    )


def far_call(place, mask, ridge, xs, blocks, near, own_y, own_a, lead):
    return kernel(
        far_kernel,
        [(4, RANK, 128)],
        [*xs, *blocks, near, own_y, own_a, lead],
        (place, mask, ridge),
        [pltpu.VMEM((2, 4, CHUNK, 128), F32), pltpu.SemaphoreType.DMA((2, 4))] + tile_scratch(3),
        far_outs=[(1024, 128)] * 4,
    )


def picks_by_row(order, picks):
    at = lax.broadcasted_iota(jnp.int32, picks.shape, 0)
    picks[...] = jnp.where(order == at, 1.0, 0.0).astype(BF16)


def load_solve(basis, solve, basis_in, solve_in, sems):
    copies = [pltpu.make_async_copy(basis.at[0], basis_in, sems.at[4])]
    for k in range(4):
        rows = pl.ds(k * Q, Q)
        copies.append(
            pltpu.make_async_copy(solve.at[0, rows, :], solve_in.at[rows, :], sems.at[k])
        )
    for copy in copies:
        copy.start()
    return copies


SOLVE_SCRATCH = [
    pltpu.VMEM((1024, RANK), F32),
    pltpu.VMEM((1024, 1024), F32),
    pltpu.SemaphoreType.DMA((5,)),
]


def lead_kernel(order, basis, solve, lead, basis_in, solve_in, sems, picks, turned):
    first, *rest = load_solve(basis, solve, basis_in, solve_in, sems)
    picks_by_row(order[...], picks)
    first.wait()
    turned[...] = jnp.transpose(basis_in[...])
    for k in range(4):
        rest[k].wait()
        rows = slice(k * Q, (k + 1) * Q)
        term = dot3(turned[:, rows], solve_in[rows, :])
        if k:
            lead[...] += term
        else:
            lead[...] = term
    both = jnp.concatenate(split(lead[...]), axis=0)
    chosen = dot(both, picks[...], NT)
    lead[...] = chosen[:RANK] + chosen[RANK:]


def lead_call(order, leaf_basis, leaf_inverse):
    return kernel(
        lead_kernel,
        [(RANK, 1024)],
        [order],
        scratch=SOLVE_SCRATCH
        + [pltpu.VMEM((1024, 1024), BF16), pltpu.VMEM((RANK, 1024), F32)],
        far_values=[leaf_basis, leaf_inverse],
    )


def run_copies(sems, moves):
    copies = [
        pltpu.make_async_copy(source, target, sems.at[k])
        for k, (source, target) in enumerate(moves)
    ]
    for copy in copies:
        copy.start()
    for copy in copies:
        copy.wait()


def mover(body, shape, count, *parts):
    return pl.pallas_call(
        body,
        in_specs=[HBM] * len(parts),
        out_specs=HBM,
        out_shape=like(*shape),
        scratch_shapes=[pltpu.SemaphoreType.DMA((count,))],
        compiler_params=pltpu.CompilerParams(vmem_limit_bytes=4 << 20),
    )(*[far_memory(part) for part in parts])


def pack_kernel(a, b, out, sems):
    run_copies(sems, [(a, out.at[:, pl.ds(0, 128)]), (b, out.at[:, pl.ds(128, 512)])])


def slice_moves(transfer, inverse, out, start):
    moves = [(transfer.at[0, pl.ds(256, 64), :], out.at[pl.ds(start, 64), :])]
    for k in range(4):
        source = inverse.at[0, pl.ds(320, 16), pl.ds(k * 256, 256)]
        moves.append((source, out.at[pl.ds(start + 64 + k * 16, 16), :]))
    return moves


def slices_kernel(transfer, inverse, out, sems):
    run_copies(sems, slice_moves(transfer, inverse, out, 0))


def pair_kernel(slices, lower, out, sems):
    run_copies(sems, [(slices, out.at[pl.ds(0, 128), :]), (lower, out.at[pl.ds(128, 128), :])])


def held_kernel(transfer, inverse, pair, mirrored, out, buffer, sems):
    moves = [
        (transfer.at[0, pl.ds(0, 256), :], buffer.at[pl.ds(0, 256), :]),
        (pair, buffer.at[pl.ds(512, 256), :]),
        (mirrored, buffer.at[pl.ds(768, 256), :]),
    ]
    for k in range(4):
        source = inverse.at[0, pl.ds(256, 64), pl.ds(k * 256, 256)]
        moves.append((source, buffer.at[pl.ds(256 + k * 64, 64), :]))
    run_copies(sems, moves)
    run_copies(sems, [(buffer, out)])


def held_call(*parts):
    return kernel(
        held_kernel,
        [],
        [],
        scratch=[pltpu.VMEM((1024, 256), F32), pltpu.SemaphoreType.DMA((7,))],
        far_values=parts,
        far_outs=[(1024, 256)],
    )


def nodes_kernel(place, b0, b1, b2, b3, e1, m2, f2, m3, own_e2, e2):
    q = place[3] % 4
    child = place[3] // 4 % 4
    parent = place[3] // 16
    odd = place[3] // 8 % 2
    for d, block in enumerate((b0, b1, b2, b3)):
        at = q ^ d
        e1[pl.ds(pl.multiple_of(at * 256, 256), 256), :] = block[:256, :]
        rows = pl.ds(pl.multiple_of(at * 64, 64), 64)
        for k in range(4):
            source = pl.multiple_of(256 + (child ^ k) * 64, 64)
            m2[rows, k * 256 : (k + 1) * 256] = block[pl.ds(source, 64), :]
        for s, (start, flip) in enumerate(((512, 0), (768, 2), (640, 0), (896, 2))):
            held = at ^ flip
            e2[pl.ds(pl.multiple_of(s * 256 + held * 64, 64), 64), :] = block[
                start : start + 64, :
            ]
            rows = pl.ds(pl.multiple_of((child ^ s) * 64 + held * 16, 16), 16)
            for k in range(4):
                step = (0, 3, 1, 2)[k] + odd * (0, -2, 2, 0)[k]
                source = pl.multiple_of(start + 64 + (parent + step) % 4 * 16, 16)
                m3[rows, k * 256 : (k + 1) * 256] = block[pl.ds(source, 16), :]
    own_e2[...] = e2[:256, :]
    f2[...] = dot3(m2[...], e2[...])


def nodes_call(place, blocks):
    return kernel(
        nodes_kernel,
        [(1024, 256), (256, 1024), (256, 256), (256, 1024), (256, 256)],
        blocks,
        (place,),
        [pltpu.VMEM((1024, 256), F32)],
    )


def level1_kernel(place, leaf_map, stacked, m1, e1, w1, p1):
    base = place[3] // 4 * 4
    total = None
    for k in range(4):
        term = dot3(m1[0, :256, k * 256 : (k + 1) * 256], stacked[leaf_map[base + k] - base])
        total = term if total is None else total + term
    w1[...] = total
    p1[...] = dot3(jnp.transpose(total), e1[0, :256, :])


def level1_call(place, leaf_map, stacked, node_inverse, node_transfer):
    return kernel(
        level1_kernel,
        [(256, 128), (128, 256)],
        [stacked, node_inverse, node_transfer],
        (place, leaf_map),
    )


def row_blocks(parts, matrix):
    total = None
    for k, part in enumerate(parts):
        term = dot3(part[...], matrix[:, k * 256 : (k + 1) * 256], NT)
        total = term if total is None else total + term
    return total


def level2_kernel(r0, r1, r2, r3, m2, e2, w2, p2):
    total = row_blocks((r0, r1, r2, r3), m2)
    w2[...] = total
    p2[...] = dot3(total, e2[...])


def level2_call(parts, m2, e2):
    return kernel(level2_kernel, [(32, 256), (32, 256)], [*parts, m2, e2])


def upper_kernel(r0, r1, r2, r3, m3, f2, w2, g1):
    g2 = row_blocks((r0, r1, r2, r3), m3)
    g1[...] = w2[...] - dot3(g2, f2[...], NT)


def upper_call(parts, m3, f2, w2):
    return kernel(upper_kernel, [(32, 256)], [*parts, m3, f2, w2])


def down1_kernel(g1, e1, m1, w1, v1, e1_in, m1_in, w1_in, sems):
    copies = [
        pltpu.make_async_copy(e1, e1_in, sems.at[0]),
        pltpu.make_async_copy(m1.at[0, pl.ds(0, 256), :], m1_in, sems.at[1]),
        pltpu.make_async_copy(w1, w1_in, sems.at[2]),
    ]
    for copy in copies:
        copy.start()
    g = g1[...].reshape(128, 256)
    copies[0].wait()
    lifted = dot3(g, e1_in[...], NT)
    copies[1].wait()
    copies[2].wait()
    v1[...] = w1_in[...] - dot3(m1_in[...], lifted, NT)


def down1_call(g1, e1, node_inverse, w1):
    return kernel(
        down1_kernel,
        [(256, 128)],
        [g1],
        scratch=[
            pltpu.VMEM((1024, 256), F32),
            pltpu.VMEM((256, 1024), F32),
            pltpu.VMEM((256, 128), F32),
            pltpu.SemaphoreType.DMA((3,)),
        ],
        far_values=[e1, node_inverse, w1],
    )


def residual_kernel(
    place, order, p0, p1, p2, p3, ordered_out, out0, out1, out2, out3, picks, res, ordered, sems
):
    res_sum = p0[...] + p1[...] + (p2[...] + p3[...])
    res[...] = res_sum
    rows = jnp.broadcast_to(order[...].astype(F32), (128, 1024))
    holds = jnp.transpose(rows)[:, :1].astype(jnp.int32)
    at = lax.broadcasted_iota(jnp.int32, (1024, 1024), 1)
    picks[...] = jnp.where(holds == at, 1.0, 0.0).astype(BF16)
    both = dot(picks[...], jnp.concatenate(split(res_sum), axis=1))
    ordered[...] = both[:, :128] + both[:, 128:]
    moves = [(ordered, ordered_out)]
    for k, out in enumerate((out0, out1, out2, out3)):
        rows = pl.ds(pl.multiple_of((place[2] + k) % 4 * Q, Q), Q)
        moves.append((res.at[rows, :], out))
    run_copies(sems, moves)


def residual_call(place, order, parts):
    return kernel(
        residual_kernel,
        [],
        [order, *parts],
        (place,),
        [
            pltpu.VMEM((1024, 1024), BF16),
            pltpu.VMEM((1024, 128), F32),
            pltpu.VMEM((1024, 128), F32),
            pltpu.SemaphoreType.DMA((5,)),
        ],
        far_outs=[(1024, 128)] + [(Q, 128)] * 4,
    )


def finish_kernel(
    place, leaf_map, order, pieces, ordered, basis, solve, delta,
    basis_in, solve_in, sems, picks, rhs, sides,
):
    first, *rest = load_solve(basis, solve, basis_in, solve_in, sems)
    base = place[3] // 4 * 4
    slot = jnp.int32(3)
    for k in range(3):
        slot = jnp.where(leaf_map[base + k] == place[3], k, slot)
    picks_by_row(order[...], picks)
    first.wait()
    rhs[...] = jnp.concatenate(
        split(ordered[...] - dot3(basis_in[...], pieces[slot])), axis=1
    )
    for k in range(4):
        rest[k].wait()
        rows = slice(k * Q, (k + 1) * Q)
        a, b = split(solve_in[rows, :])
        both = dot(a, rhs[...])
        y = both[:, :128] + (both[:, 128:] + dot(b, rhs[:, :128]))
        sides[rows, :] = jnp.concatenate(split(y), axis=1)

    @pl.loop(0, 2)
    def _(i):
        rows = pl.ds(pl.multiple_of(i * CHUNK, CHUNK), CHUNK)
        both = dot(picks[rows, :], sides[...])
        delta[rows, :] = both[:, :128] + both[:, 128:]


def finish_call(place, leaf_map, order, pieces, ordered, leaf_basis, leaf_inverse):
    return kernel(
        finish_kernel,
        [(1024, 128)],
        [order, pieces, ordered],
        (place, leaf_map),
        SOLVE_SCRATCH
        + [
            pltpu.VMEM((1024, 1024), BF16),
            pltpu.VMEM((1024, 256), BF16),
            pltpu.VMEM((1024, 256), BF16),
        ],
        [leaf_basis, leaf_inverse],
    )


def outputs_kernel(place, r0, r1, r2, r3, delta, coefs, out_res, out_new):
    for k, res in enumerate((r0, r1, r2, r3)):
        at = slice(k * 128, (k + 1) * 128)
        out_new[:, at] = coefs[:, at] + delta[k]
        source = pl.multiple_of((place[2] + 4 - k) % 4 * 128, 128)
        out_res[:, pl.ds(source, 128)] = res[...]


def outputs_call(place, res, delta, coefs):
    return pl.pallas_call(
        outputs_kernel,
        in_specs=[SMEM] + [VMEM] * 6,
        out_shape=[like(Q, 512), like(Q, 512)],
        compiler_params=pltpu.CompilerParams(vmem_limit_bytes=8 << 20),
        name="outputs",
    )(place, *[near_memory(value) for value in (*res, delta, coefs)])


def swap_cols(value):
    return lax.all_to_all(value, "col", 0, 0, tiled=True)


def step(
    points,
    coefs,
    targets,
    ridge,
    tile_mask,
    cluster_perm,
    leaf_map,
    leaf_inverse,
    leaf_basis,
    node_inverse,
    node_transfer,
):
    col = lax.axis_index("col")
    leaf = lax.axis_index("leaf")
    core = leaf % 2
    place = jnp.stack([core, leaf // 2 % 2, col, leaf]).astype(jnp.int32)

    xs = [points] + [col_shift(points, d) for d in (1, 2, 3)]
    packed = mover(pack_kernel, (Q, 640), 2, points, coefs)
    left, right = leaf_from(packed, -2), leaf_from(packed, 2)
    partner = leaf_xor(packed, 1)
    relay = leaf_xor(jnp.where(core == 0, right, left), 1)

    nodes = (node_transfer, node_inverse)
    slices = mover(slices_kernel, (128, 256), 5, *nodes)
    lower = leaf_route(slices, lambda i: facing(i, 0, 1))
    pair = mover(pair_kernel, (256, 256), 2, slices, lower)
    mirrored = leaf_route(pair, lambda i: facing(i, 1, 0))
    held = held_call(*nodes, pair, mirrored)

    lead = lead_call(cluster_perm, leaf_basis, leaf_inverse)

    near = near_call(place, tile_mask, xs, (packed, partner))
    near, held = lax.optimization_barrier((near, held))
    across = leaf_xor(held, 2)
    own_core = leaf_xor(held, 1)
    both_ways = leaf_xor(across, 1)
    led, *partial = far_call(
        place, tile_mask, ridge, xs, (left, right, relay), near, targets, coefs, lead
    )
    led = swap_cols(led)
    reduced = led[0] + led[1] + (led[2] + led[3])
    e1, m2, f2, m3, e2 = nodes_call(place, (held, own_core, across, both_ways))

    columns = [partial[0]] + [col_shift(partial[d], d) for d in (1, 2, 3)]

    w1, p1 = level1_call(place, leaf_map, gather4(reduced, G4), node_inverse, node_transfer)
    p1 = lax.all_to_all(p1, "leaf", 0, 0, axis_index_groups=GK, tiled=True)
    p1 = p1.reshape(4, 32, RANK)
    r1 = p1[0] + p1[1] + (p1[2] + p1[3])
    w2, p2 = level2_call(siblings(r1), m2, e2)
    r2 = sum(siblings(p2))
    r2s = [r2, z_from(r2, -1, 1), z_from(r2, 2, -2), z_from(r2, -3, 3)]
    g1 = upper_call(r2s, m3, f2, w2)
    columns, g1 = lax.optimization_barrier((columns, g1))
    ordered, *pieces = residual_call(place, cluster_perm, columns)
    res_rows = [pieces[0]] + [col_shift(pieces[k], k) for k in (1, 2, 3)]
    g1 = gather4(g1, GK)
    pieces = gather4(down1_call(g1, e1, node_inverse, w1), G4)

    delta = finish_call(place, leaf_map, cluster_perm, pieces, ordered, leaf_basis, leaf_inverse)
    return outputs_call(place, res_rows, swap_cols(delta.reshape(4, Q, 128)), coefs)


def solution(mesh):
    return jax.shard_map(
        step,
        mesh=mesh,
        in_specs=(
            P(("leaf", "col"), None),
            P(("leaf", "col"), None),
            P(("leaf", "col"), None),
            P(),
            P("leaf", None),
            P("leaf", None),
            P(),
            P("leaf", None, None),
            P("leaf", None, None),
            P("leaf", None, None),
            P("leaf", None, None),
        ),
        out_specs=(P(("leaf", "col"), None), P(("leaf", "col"), None)),
        check_vma=False,
    )
```

```python
import jax
import jax.numpy as jnp
from jax import lax
from jax.experimental import pallas as pl
from jax.experimental.pallas import tpu as pltpu
from jax.sharding import PartitionSpec as P


F32 = jnp.float32
BF16 = jnp.bfloat16
Q = 256
RANK = 256
LEAVES = 64


def leaf_at(z, x_hi, kappa):
    x = 2 * x_hi + ((kappa >> 1) ^ x_hi)
    return z * 8 + x * 2 + (kappa & 1)


G4 = [[4 * n + k for k in range(4)] for n in range(16)]
GK = [[leaf_at(z, xh, k) for k in range(4)] for z in range(8) for xh in range(2)]


def facing(i, flip_x, flip_z):
    z, x, core = i // 8, i // 2 % 4, i % 2
    return (z ^ flip_z) * 8 + (3 - x if flip_x else x) * 2 + core


def leaf_route(value, target):
    return lax.ppermute(value, "leaf", [(i, target(i)) for i in range(LEAVES)])


def leaf_xor(value, bit):
    return leaf_route(value, lambda i: i ^ bit)


def leaf_from(value, step):
    return leaf_route(value, lambda i: (i - step) % LEAVES)


def siblings(value):
    return [value] + [
        leaf_route(value, lambda i, d=d: facing(i, d & 1, d >> 1)) for d in (1, 2, 3)
    ]


def z_from(value, even, odd):
    route = []
    for i in range(LEAVES):
        step = odd if i // 8 % 2 else even
        route.append(((i + 8 * step) % LEAVES, i))
    return lax.ppermute(value, "leaf", route)


def col_shift(value, step):
    return lax.ppermute(value, "col", [(i, (i + step) % 4) for i in range(4)])


def gather4(value, groups):
    return lax.all_gather(value, "leaf", axis=0, axis_index_groups=groups)


NN = ((1,), (0,))
NT = ((1,), (1,))


def dot(a, b, dims=NN):
    return lax.dot_general(a, b, (dims, ((), ())), preferred_element_type=F32)


def split(value):
    top = value.astype(BF16)
    return top, (value - top.astype(F32)).astype(BF16)


def dot3(a, b, dims=NN):
    at, al = split(a)
    bt, bl = split(b)
    return dot(at, bt, dims) + (dot(at, bl, dims) + dot(al, bt, dims))


SMEM = pl.BlockSpec(memory_space=pltpu.SMEM)
VMEM = pl.BlockSpec(memory_space=pltpu.VMEM)
HBM = pl.BlockSpec(memory_space=pltpu.HBM)


def near_memory(value):
    return pltpu.with_memory_space_constraint(value, pltpu.VMEM)


def far_memory(value):
    return pltpu.with_memory_space_constraint(value, pltpu.HBM)


def kernel(body, outs, values, scalars=(), scratch=(), far_values=(), far_outs=()):
    result = pl.pallas_call(
        body,
        in_specs=[SMEM] * len(scalars) + [VMEM] * len(values) + [HBM] * len(far_values),
        out_specs=[VMEM] * len(outs) + [HBM] * len(far_outs),
        out_shape=[pltpu.VMEM(shape, F32) for shape in outs]
        + [pltpu.HBM(shape, F32) for shape in far_outs],
        scratch_shapes=list(scratch),
        compiler_params=pltpu.CompilerParams(vmem_limit_bytes=20 << 20),
    )(*scalars, *[near_memory(value) for value in values], *[far_memory(value) for value in far_values])
    return result if len(outs) + len(far_outs) > 1 else result[0]


def like(*shape, dtype=F32):
    return jax.ShapeDtypeStruct(shape, dtype)


CHUNK = 512


def two_part(value):
    top, low = split(value)
    return jnp.concatenate([top, low], axis=1), top.astype(F32) + low.astype(F32)


def tile_setup(place, xs, blocks, loaded, arrived, rows, norms, squares, others, tops, lows):
    copies = [
        pltpu.make_async_copy(ref, loaded.at[k], arrived.at[k]) for k, ref in enumerate(xs)
    ]
    for copy in copies:
        copy.start()
    for k, (y, a) in enumerate(blocks):
        others[k], exact = two_part(y)
        total = jnp.sum(exact * exact, axis=1, keepdims=True)
        squares[k] = jnp.transpose(jnp.broadcast_to(total, (Q, 128)))[:8]
        tops[k], lows[k] = split(a)
    for k, copy in enumerate(copies):
        copy.wait()
        at = (place[2] + 4 - k) % 4
        rows[at], exact = two_part(loaded[k])
        norms[at] = jnp.sum(exact * exact, axis=1, keepdims=True)


def tile_sum(i, weights, loaded, arrived, rows, norms, squares, others, tops, lows):
    x = rows[pl.ds(2 * i, 2)].reshape(CHUNK, 256)
    own = norms[pl.ds(2 * i, 2)].reshape(CHUNK, 1)
    total = None
    for k, weight in enumerate(weights):
        top, low = others[k][:, :128], others[k][:, 128:]
        inner = dot(x, jnp.concatenate([top, top], axis=1), NT)
        inner = inner + dot(x, jnp.concatenate([low, low], axis=1), NT)
        distance = own + squares[k][:1] - 2.0 * inner
        top, low = split(jnp.exp(distance * (-2.0 / 128.0)) * weight)
        term = dot(top, tops[k]) + dot(top, lows[k]) + dot(low, tops[k])
        total = term if total is None else total + term
    return total


def near_kernel(place, mask, p0, p1, x0, x1, x2, x3, out, *scratch):
    blocks = [(p[:, :128], p[:, 128:]) for p in (p0, p1)]
    tile_setup(place, (x0, x1, x2, x3), blocks, *scratch)
    weights = (mask[0, 2].astype(F32), mask[0, 3 - 2 * place[0]].astype(F32))

    @pl.loop(0, 2)
    def _(i):
        out[pl.ds(pl.multiple_of(i * CHUNK, CHUNK), CHUNK), :] = tile_sum(i, weights, *scratch)


def far_kernel(
    place, mask, ridge, p0, p1, p2, near, own_y, own_a, lead, x0, x1, x2, x3,
    led, out0, out1, out2, out3, parts, sems, *scratch
):
    blocks = [(p[:, :128], p[:, 128:]) for p in (p0, p1, p2)]
    tile_setup(place, (x0, x1, x2, x3), blocks, *scratch)
    weights = (
        mask[0, 0].astype(F32),
        mask[0, 4].astype(F32),
        mask[0, 1 + 2 * place[0]].astype(F32),
    )
    for k in range(4):
        led[k] = jnp.zeros((RANK, 128), F32)

    def sent(i):
        rows = pl.ds(pl.multiple_of(i * CHUNK, CHUNK), CHUNK)
        return [
            pltpu.make_async_copy(
                parts.at[i, (place[2] + d) % 4], out.at[rows, :], sems.at[i, d]
            )
            for d, out in enumerate((out0, out1, out2, out3))
        ]

    @pl.loop(0, 2)
    def _(i):
        rows = pl.ds(pl.multiple_of(i * CHUNK, CHUNK), CHUNK)
        total = near[rows, :] + tile_sum(i, weights, *scratch)
        own = own_y[...] - ridge[0] * own_a[...]
        part = jnp.concatenate(
            [
                jnp.where(place[2] == 2 * i + h, own, 0.0) - total[h * Q : (h + 1) * Q]
                for h in range(2)
            ],
            axis=0,
        )
        product = dot3(lead[:, rows], part)
        for k in range(4):
            parts[i, k] = part[:, k * 128 : (k + 1) * 128]
            led[k] += product[:, k * 128 : (k + 1) * 128]
        for copy in sent(i):
            copy.start()

    for i in range(2):
        for copy in sent(i):
            copy.wait()


def tile_scratch(count):
    return [
        pltpu.VMEM((4, Q, 128), F32),
        pltpu.SemaphoreType.DMA((4,)),
        pltpu.VMEM((4, Q, 256), BF16),
        pltpu.VMEM((4, Q, 1), F32),
        pltpu.VMEM((count, 8, Q), F32),
        pltpu.VMEM((count, Q, 256), BF16),
        pltpu.VMEM((count, Q, 512), BF16),
        pltpu.VMEM((count, Q, 512), BF16),
    ]


def near_call(place, mask, xs, blocks):
    return kernel(near_kernel, [(1024, 512)], blocks, (place, mask), tile_scratch(2), xs)


def far_call(place, mask, ridge, xs, blocks, near, own_y, own_a, lead):
    return kernel(
        far_kernel,
        [(4, RANK, 128)],
        [*blocks, near, own_y, own_a, lead],
        (place, mask, ridge),
        [pltpu.VMEM((2, 4, CHUNK, 128), F32), pltpu.SemaphoreType.DMA((2, 4))] + tile_scratch(3),
        xs,
        [(1024, 128)] * 4,
    )


def picks_by_row(order, picks):
    at = lax.broadcasted_iota(jnp.int32, picks.shape, 0)
    picks[...] = jnp.where(order == at, 1.0, 0.0).astype(BF16)


def load_solve(basis, solve, basis_in, solve_in, sems):
    copies = [pltpu.make_async_copy(basis.at[0], basis_in, sems.at[4])]
    for k in range(4):
        rows = pl.ds(k * Q, Q)
        copies.append(
            pltpu.make_async_copy(solve.at[0, rows, :], solve_in.at[rows, :], sems.at[k])
        )
    for copy in copies:
        copy.start()
    return copies


SOLVE_SCRATCH = [
    pltpu.VMEM((1024, RANK), F32),
    pltpu.VMEM((1024, 1024), F32),
    pltpu.SemaphoreType.DMA((5,)),
]


def lead_kernel(order, basis, solve, lead, basis_in, solve_in, sems, picks, turned):
    first, *rest = load_solve(basis, solve, basis_in, solve_in, sems)
    picks_by_row(order[...], picks)
    first.wait()
    turned[...] = jnp.transpose(basis_in[...])
    for k in range(4):
        rest[k].wait()
        rows = slice(k * Q, (k + 1) * Q)
        term = dot3(turned[:, rows], solve_in[rows, :])
        if k:
            lead[...] += term
        else:
            lead[...] = term
    both = jnp.concatenate(split(lead[...]), axis=0)
    chosen = dot(both, picks[...], NT)
    lead[...] = chosen[:RANK] + chosen[RANK:]


def lead_call(order, leaf_basis, leaf_inverse):
    return kernel(
        lead_kernel,
        [(RANK, 1024)],
        [order],
        scratch=SOLVE_SCRATCH
        + [pltpu.VMEM((1024, 1024), BF16), pltpu.VMEM((RANK, 1024), F32)],
        far_values=[leaf_basis, leaf_inverse],
    )


def run_copies(sems, moves):
    copies = [
        pltpu.make_async_copy(source, target, sems.at[k])
        for k, (source, target) in enumerate(moves)
    ]
    for copy in copies:
        copy.start()
    for copy in copies:
        copy.wait()


def mover(body, shape, count, *parts):
    return pl.pallas_call(
        body,
        in_specs=[HBM] * len(parts),
        out_specs=HBM,
        out_shape=like(*shape),
        scratch_shapes=[pltpu.SemaphoreType.DMA((count,))],
        compiler_params=pltpu.CompilerParams(vmem_limit_bytes=4 << 20),
    )(*[far_memory(part) for part in parts])


def pack_kernel(a, b, out, sems):
    run_copies(sems, [(a, out.at[:, pl.ds(0, 128)]), (b, out.at[:, pl.ds(128, 512)])])


def slice_moves(transfer, inverse, out, start):
    moves = [(transfer.at[0, pl.ds(256, 64), :], out.at[pl.ds(start, 64), :])]
    for k in range(4):
        source = inverse.at[0, pl.ds(320, 16), pl.ds(k * 256, 256)]
        moves.append((source, out.at[pl.ds(start + 64 + k * 16, 16), :]))
    return moves


def slices_kernel(transfer, inverse, out, sems):
    run_copies(sems, slice_moves(transfer, inverse, out, 0))


def pair_kernel(slices, lower, out):
    out[:128, :] = slices[...]
    out[128:, :] = lower[...]


def held_kernel(transfer, inverse, pair, mirrored, out, buffer, sems):
    moves = [
        (transfer.at[0, pl.ds(0, 256), :], buffer.at[pl.ds(0, 256), :]),
        (pair, buffer.at[pl.ds(512, 256), :]),
        (mirrored, buffer.at[pl.ds(768, 256), :]),
    ]
    for k in range(4):
        source = inverse.at[0, pl.ds(256, 64), pl.ds(k * 256, 256)]
        moves.append((source, buffer.at[pl.ds(256 + k * 64, 64), :]))
    run_copies(sems, moves)
    run_copies(sems, [(buffer, out)])


def held_call(*parts):
    return kernel(
        held_kernel,
        [],
        [],
        scratch=[pltpu.VMEM((1024, 256), F32), pltpu.SemaphoreType.DMA((7,))],
        far_values=parts,
        far_outs=[(1024, 256)],
    )


def nodes_kernel(place, b0, b1, b2, b3, e1, m2, f2, m3, own_e2, e2):
    q = place[3] % 4
    child = place[3] // 4 % 4
    parent = place[3] // 16
    odd = place[3] // 8 % 2
    for d, block in enumerate((b0, b1, b2, b3)):
        at = q ^ d
        e1[pl.ds(pl.multiple_of(at * 256, 256), 256), :] = block[:256, :]
        rows = pl.ds(pl.multiple_of(at * 64, 64), 64)
        for k in range(4):
            source = pl.multiple_of(256 + (child ^ k) * 64, 64)
            m2[rows, k * 256 : (k + 1) * 256] = block[pl.ds(source, 64), :]
        for s, (start, flip) in enumerate(((512, 0), (768, 2), (640, 0), (896, 2))):
            held = at ^ flip
            e2[pl.ds(pl.multiple_of(s * 256 + held * 64, 64), 64), :] = block[
                start : start + 64, :
            ]
            rows = pl.ds(pl.multiple_of((child ^ s) * 64 + held * 16, 16), 16)
            for k in range(4):
                step = (0, 3, 1, 2)[k] + odd * (0, -2, 2, 0)[k]
                source = pl.multiple_of(start + 64 + (parent + step) % 4 * 16, 16)
                m3[rows, k * 256 : (k + 1) * 256] = block[pl.ds(source, 16), :]
    own_e2[...] = e2[:256, :]
    f2[...] = dot3(m2[...], e2[...])


def nodes_call(place, blocks):
    return kernel(
        nodes_kernel,
        [(1024, 256), (256, 1024), (256, 256), (256, 1024), (256, 256)],
        blocks,
        (place,),
        [pltpu.VMEM((1024, 256), F32)],
    )


def level1_kernel(place, leaf_map, stacked, m1, e1, w1, p1):
    base = place[3] // 4 * 4
    total = None
    for k in range(4):
        term = dot3(m1[0, :256, k * 256 : (k + 1) * 256], stacked[leaf_map[base + k] - base])
        total = term if total is None else total + term
    w1[...] = total
    p1[...] = dot3(jnp.transpose(total), e1[0, :256, :])


def level1_call(place, leaf_map, stacked, node_inverse, node_transfer):
    return kernel(
        level1_kernel,
        [(256, 128), (128, 256)],
        [stacked, node_inverse, node_transfer],
        (place, leaf_map),
    )


def row_blocks(parts, matrix):
    total = None
    for k, part in enumerate(parts):
        term = dot3(part[...], matrix[:, k * 256 : (k + 1) * 256], NT)
        total = term if total is None else total + term
    return total


def level2_kernel(r0, r1, r2, r3, m2, e2, w2, p2):
    total = row_blocks((r0, r1, r2, r3), m2)
    w2[...] = total
    p2[...] = dot3(total, e2[...])


def level2_call(parts, m2, e2):
    return kernel(level2_kernel, [(32, 256), (32, 256)], [*parts, m2, e2])


def upper_kernel(r0, r1, r2, r3, m3, f2, w2, g1):
    g2 = row_blocks((r0, r1, r2, r3), m3)
    g1[...] = w2[...] - dot3(g2, f2[...], NT)


def upper_call(parts, m3, f2, w2):
    return kernel(upper_kernel, [(32, 256)], [*parts, m3, f2, w2])


def down1_kernel(g1, e1, m1, w1, v1, e1_in, m1_in, w1_in, sems):
    copies = [
        pltpu.make_async_copy(e1, e1_in, sems.at[0]),
        pltpu.make_async_copy(m1.at[0, pl.ds(0, 256), :], m1_in, sems.at[1]),
        pltpu.make_async_copy(w1, w1_in, sems.at[2]),
    ]
    for copy in copies:
        copy.start()
    g = g1[...].reshape(128, 256)
    copies[0].wait()
    lifted = dot3(g, e1_in[...], NT)
    copies[1].wait()
    copies[2].wait()
    v1[...] = w1_in[...] - dot3(m1_in[...], lifted, NT)


def down1_call(g1, e1, node_inverse, w1):
    return kernel(
        down1_kernel,
        [(256, 128)],
        [g1],
        scratch=[
            pltpu.VMEM((1024, 256), F32),
            pltpu.VMEM((256, 1024), F32),
            pltpu.VMEM((256, 128), F32),
            pltpu.SemaphoreType.DMA((3,)),
        ],
        far_values=[e1, node_inverse, w1],
    )


def residual_kernel(
    place, order, p0, p1, p2, p3, ordered_out, out0, out1, out2, out3, picks, res, ordered, sems
):
    res_sum = p0[...] + p1[...] + (p2[...] + p3[...])
    res[...] = res_sum
    rows = jnp.broadcast_to(order[...].astype(F32), (128, 1024))
    holds = jnp.transpose(rows)[:, :1].astype(jnp.int32)
    at = lax.broadcasted_iota(jnp.int32, (1024, 1024), 1)
    picks[...] = jnp.where(holds == at, 1.0, 0.0).astype(BF16)
    both = dot(picks[...], jnp.concatenate(split(res_sum), axis=1))
    ordered[...] = both[:, :128] + both[:, 128:]
    moves = [(ordered, ordered_out)]
    for k, out in enumerate((out0, out1, out2, out3)):
        rows = pl.ds(pl.multiple_of((place[2] + k) % 4 * Q, Q), Q)
        moves.append((res.at[rows, :], out))
    run_copies(sems, moves)


def residual_call(place, order, parts):
    return kernel(
        residual_kernel,
        [],
        [order, *parts],
        (place,),
        [
            pltpu.VMEM((1024, 1024), BF16),
            pltpu.VMEM((1024, 128), F32),
            pltpu.VMEM((1024, 128), F32),
            pltpu.SemaphoreType.DMA((5,)),
        ],
        far_outs=[(1024, 128)] + [(Q, 128)] * 4,
    )


def finish_kernel(
    place, leaf_map, order, pieces, ordered, basis, solve, delta,
    basis_in, solve_in, sems, picks, rhs, sides,
):
    first, *rest = load_solve(basis, solve, basis_in, solve_in, sems)
    base = place[3] // 4 * 4
    slot = jnp.int32(3)
    for k in range(3):
        slot = jnp.where(leaf_map[base + k] == place[3], k, slot)
    picks_by_row(order[...], picks)
    first.wait()
    rhs[...] = jnp.concatenate(
        split(ordered[...] - dot3(basis_in[...], pieces[slot])), axis=1
    )
    for k in range(4):
        rest[k].wait()
        rows = slice(k * Q, (k + 1) * Q)
        a, b = split(solve_in[rows, :])
        both = dot(a, rhs[...])
        y = both[:, :128] + (both[:, 128:] + dot(b, rhs[:, :128]))
        sides[rows, :] = jnp.concatenate(split(y), axis=1)

    @pl.loop(0, 2)
    def _(i):
        rows = pl.ds(pl.multiple_of(i * CHUNK, CHUNK), CHUNK)
        both = dot(picks[rows, :], sides[...])
        delta[rows, :] = both[:, :128] + both[:, 128:]


def finish_call(place, leaf_map, order, pieces, ordered, leaf_basis, leaf_inverse):
    return kernel(
        finish_kernel,
        [(1024, 128)],
        [order, pieces, ordered],
        (place, leaf_map),
        SOLVE_SCRATCH
        + [
            pltpu.VMEM((1024, 1024), BF16),
            pltpu.VMEM((1024, 256), BF16),
            pltpu.VMEM((1024, 256), BF16),
        ],
        [leaf_basis, leaf_inverse],
    )


def outputs_kernel(place, r0, r1, r2, r3, delta, coefs, out_res, out_new):
    for k, res in enumerate((r0, r1, r2, r3)):
        at = slice(k * 128, (k + 1) * 128)
        out_new[:, at] = coefs[:, at] + delta[k]
        source = pl.multiple_of((place[2] + 4 - k) % 4 * 128, 128)
        out_res[:, pl.ds(source, 128)] = res[...]


def outputs_call(place, res, delta, coefs):
    return pl.pallas_call(
        outputs_kernel,
        in_specs=[SMEM] + [VMEM] * 6,
        out_shape=[like(Q, 512), like(Q, 512)],
        compiler_params=pltpu.CompilerParams(vmem_limit_bytes=8 << 20),
        name="outputs",
    )(place, *[near_memory(value) for value in (*res, delta, coefs)])


def swap_cols(value):
    return lax.all_to_all(value, "col", 0, 0, tiled=True)


def step(
    points,
    coefs,
    targets,
    ridge,
    tile_mask,
    cluster_perm,
    leaf_map,
    leaf_inverse,
    leaf_basis,
    node_inverse,
    node_transfer,
):
    col = lax.axis_index("col")
    leaf = lax.axis_index("leaf")
    core = leaf % 2
    place = jnp.stack([core, leaf // 2 % 2, col, leaf]).astype(jnp.int32)

    xs = [points] + [col_shift(points, d) for d in (1, 2, 3)]
    packed = mover(pack_kernel, (Q, 640), 2, points, coefs)
    left, right = leaf_from(packed, -2), leaf_from(packed, 2)
    partner = leaf_xor(packed, 1)
    relay = leaf_xor(jnp.where(core == 0, right, left), 1)

    nodes = (node_transfer, node_inverse)
    slices = mover(slices_kernel, (128, 256), 5, *nodes)
    lower = leaf_route(slices, lambda i: facing(i, 0, 1))
    pair = kernel(pair_kernel, [(256, 256)], [slices, lower])
    mirrored = leaf_route(pair, lambda i: facing(i, 1, 0))
    held = held_call(*nodes, pair, mirrored)

    lead = lead_call(cluster_perm, leaf_basis, leaf_inverse)

    near = near_call(place, tile_mask, xs, (packed, partner))
    near, held = lax.optimization_barrier((near, held))
    across = leaf_xor(held, 2)
    own_core = leaf_xor(held, 1)
    both_ways = leaf_xor(across, 1)
    led, *partial = far_call(
        place, tile_mask, ridge, xs, (left, right, relay), near, targets, coefs, lead
    )
    led = swap_cols(led)
    reduced = led.sum(0)
    e1, m2, f2, m3, e2 = nodes_call(place, (held, own_core, across, both_ways))

    columns = [partial[0]] + [col_shift(partial[d], d) for d in (1, 2, 3)]

    w1, p1 = level1_call(place, leaf_map, gather4(reduced, G4), node_inverse, node_transfer)
    p1 = lax.all_to_all(p1, "leaf", 0, 0, axis_index_groups=GK, tiled=True)
    p1 = p1.reshape(4, 32, RANK)
    r1 = p1[0] + p1[1] + (p1[2] + p1[3])
    w2, p2 = level2_call(siblings(r1), m2, e2)
    r2 = sum(siblings(p2))
    r2s = [r2, z_from(r2, -1, 1), z_from(r2, 2, -2), z_from(r2, -3, 3)]
    g1 = upper_call(r2s, m3, f2, w2)
    columns, g1 = lax.optimization_barrier((columns, g1))
    ordered, *pieces = residual_call(place, cluster_perm, columns)
    res_rows = [pieces[0]] + [col_shift(pieces[k], k) for k in (1, 2, 3)]
    g1 = gather4(g1, GK)
    pieces = gather4(down1_call(g1, e1, node_inverse, w1), G4)

    delta = finish_call(place, leaf_map, cluster_perm, pieces, ordered, leaf_basis, leaf_inverse)
    return outputs_call(place, res_rows, swap_cols(delta.reshape(4, Q, 128)), coefs)


def solution(mesh):
    return jax.shard_map(
        step,
        mesh=mesh,
        in_specs=(
            P(("leaf", "col"), None),
            P(("leaf", "col"), None),
            P(("leaf", "col"), None),
            P(),
            P("leaf", None),
            P("leaf", None),
            P(),
            P("leaf", None, None),
            P("leaf", None, None),
            P("leaf", None, None),
            P("leaf", None, None),
        ),
        out_specs=(P(("leaf", "col"), None), P(("leaf", "col"), None)),
        check_vma=False,
    )
```

```python
import jax
import jax.numpy as jnp
from jax import lax
from jax.experimental import pallas as pl
from jax.experimental.pallas import tpu as pltpu
from jax.sharding import PartitionSpec as P


F32 = jnp.float32
BF16 = jnp.bfloat16
Q = 256
RANK = 256
LEAVES = 64


def leaf_at(z, x_hi, kappa):
    x = 2 * x_hi + ((kappa >> 1) ^ x_hi)
    return z * 8 + x * 2 + (kappa & 1)


G4 = [[4 * n + k for k in range(4)] for n in range(16)]
GK = [[leaf_at(z, xh, k) for k in range(4)] for z in range(8) for xh in range(2)]


def facing(i, flip_x, flip_z):
    z, x, core = i // 8, i // 2 % 4, i % 2
    return (z ^ flip_z) * 8 + (3 - x if flip_x else x) * 2 + core


def leaf_route(value, target):
    return lax.ppermute(value, "leaf", [(i, target(i)) for i in range(LEAVES)])


def leaf_xor(value, bit):
    return leaf_route(value, lambda i: i ^ bit)


def leaf_from(value, step):
    return leaf_route(value, lambda i: (i - step) % LEAVES)


def siblings(value):
    return [value] + [
        leaf_route(value, lambda i, d=d: facing(i, d & 1, d >> 1)) for d in (1, 2, 3)
    ]


def z_from(value, even, odd):
    route = []
    for i in range(LEAVES):
        step = odd if i // 8 % 2 else even
        route.append(((i + 8 * step) % LEAVES, i))
    return lax.ppermute(value, "leaf", route)


def col_shift(value, step):
    return lax.ppermute(value, "col", [(i, (i + step) % 4) for i in range(4)])


def gather4(value, groups):
    return lax.all_gather(value, "leaf", axis=0, axis_index_groups=groups)


NN = ((1,), (0,))
NT = ((1,), (1,))


def dot(a, b, dims=NN):
    return lax.dot_general(a, b, (dims, ((), ())), preferred_element_type=F32)


def split(value):
    top = value.astype(BF16)
    return top, (value - top.astype(F32)).astype(BF16)


def dot3(a, b, dims=NN):
    at, al = split(a)
    bt, bl = split(b)
    return dot(at, bt, dims) + (dot(at, bl, dims) + dot(al, bt, dims))


SMEM = pl.BlockSpec(memory_space=pltpu.SMEM)
VMEM = pl.BlockSpec(memory_space=pltpu.VMEM)
HBM = pl.BlockSpec(memory_space=pltpu.HBM)


def near_memory(value):
    return pltpu.with_memory_space_constraint(value, pltpu.VMEM)


def far_memory(value):
    return pltpu.with_memory_space_constraint(value, pltpu.HBM)


def kernel(body, outs, values, scalars=(), scratch=(), far_values=(), far_outs=()):
    result = pl.pallas_call(
        body,
        in_specs=[SMEM] * len(scalars) + [VMEM] * len(values) + [HBM] * len(far_values),
        out_specs=[VMEM] * len(outs) + [HBM] * len(far_outs),
        out_shape=[pltpu.VMEM(shape, F32) for shape in outs]
        + [
            pltpu.HBM(*shape) if isinstance(shape[0], tuple) else pltpu.HBM(shape, F32)
            for shape in far_outs
        ],
        scratch_shapes=list(scratch),
        compiler_params=pltpu.CompilerParams(vmem_limit_bytes=20 << 20),
    )(*scalars, *[near_memory(value) for value in values], *[far_memory(value) for value in far_values])
    return result if len(outs) + len(far_outs) > 1 else result[0]


def like(*shape, dtype=F32):
    return jax.ShapeDtypeStruct(shape, dtype)


CHUNK = 512


def two_part(value):
    top, low = split(value)
    return jnp.concatenate([top, low], axis=1), top.astype(F32) + low.astype(F32)


def row_setup(place, xs, loaded, arrived, rows, norms):
    for k, ref in enumerate(xs):
        pltpu.make_async_copy(ref, loaded.at[k], arrived.at[k]).wait()
        at = (place[2] + 4 - k) % 4
        rows[at], exact = two_part(loaded[k])
        norms[at] = jnp.sum(exact * exact, axis=1, keepdims=True)


def block_setup(blocks, squares, others, tops, lows):
    for k, (y, a) in enumerate(blocks):
        others[k], exact = two_part(y)
        total = jnp.sum(exact * exact, axis=1, keepdims=True)
        squares[k] = jnp.transpose(jnp.broadcast_to(total, (Q, 128)))[:8]
        tops[k], lows[k] = split(a)


def tile_sum(i, weights, rows, norms, squares, others, tops, lows):
    x = rows[pl.ds(2 * i, 2)].reshape(CHUNK, 256)
    own = norms[pl.ds(2 * i, 2)].reshape(CHUNK, 1)
    total = None
    for k, weight in enumerate(weights):
        top, low = others[k][:, :128], others[k][:, 128:]
        inner = dot(x, jnp.concatenate([top, top], axis=1), NT)
        inner = inner + dot(x, jnp.concatenate([low, low], axis=1), NT)
        distance = own + squares[k][:1] - 2.0 * inner
        top, low = split(jnp.exp(distance * (-2.0 / 128.0)) * weight)
        term = dot(top, tops[k]) + dot(top, lows[k]) + dot(low, tops[k])
        total = term if total is None else total + term
    return total


def near_kernel(
    place, mask, p0, p1, x0, x1, x2, x3, out, rows_out, norms_out, loaded, arrived, rows, norms, *scratch
):
    xs = (x0, x1, x2, x3)
    for k, ref in enumerate(xs):
        pltpu.make_async_copy(ref, loaded.at[k], arrived.at[k]).start()
    block_setup([(p[:, :128], p[:, 128:]) for p in (p0, p1)], *scratch)
    row_setup(place, xs, loaded, arrived, rows, norms)
    copies = [
        pltpu.make_async_copy(rows, rows_out, arrived.at[4]),
        pltpu.make_async_copy(norms, norms_out, arrived.at[5]),
    ]
    for copy in copies:
        copy.start()
    weights = (mask[0, 2].astype(F32), mask[0, 3 - 2 * place[0]].astype(F32))

    @pl.loop(0, 2)
    def _(i):
        at = pl.ds(pl.multiple_of(i * CHUNK, CHUNK), CHUNK)
        out[at, :] = tile_sum(i, weights, rows, norms, *scratch)

    for copy in copies:
        copy.wait()


def far_kernel(
    place, mask, ridge, p0, p1, p2, near, own_y, own_a, lead, split_rows, norms,
    led, out0, out1, out2, out3, parts, sems, *scratch
):
    block_setup([(p[:, :128], p[:, 128:]) for p in (p0, p1, p2)], *scratch)
    weights = (
        mask[0, 0].astype(F32),
        mask[0, 4].astype(F32),
        mask[0, 1 + 2 * place[0]].astype(F32),
    )
    for k in range(4):
        led[k] = jnp.zeros((RANK, 128), F32)

    def sent(i):
        rows = pl.ds(pl.multiple_of(i * CHUNK, CHUNK), CHUNK)
        return [
            pltpu.make_async_copy(
                parts.at[i, (place[2] + d) % 4], out.at[rows, :], sems.at[i, d]
            )
            for d, out in enumerate((out0, out1, out2, out3))
        ]

    @pl.loop(0, 2)
    def _(i):
        rows = pl.ds(pl.multiple_of(i * CHUNK, CHUNK), CHUNK)
        total = near[rows, :] + tile_sum(i, weights, split_rows, norms, *scratch)
        own = own_y[...] - ridge[0] * own_a[...]
        part = jnp.concatenate(
            [
                jnp.where(place[2] == 2 * i + h, own, 0.0) - total[h * Q : (h + 1) * Q]
                for h in range(2)
            ],
            axis=0,
        )
        product = dot3(lead[:, rows], part)
        for k in range(4):
            parts[i, k] = part[:, k * 128 : (k + 1) * 128]
            led[k] += product[:, k * 128 : (k + 1) * 128]
        for copy in sent(i):
            copy.start()

    for i in range(2):
        for copy in sent(i):
            copy.wait()


def block_scratch(count):
    return [
        pltpu.VMEM((count, 8, Q), F32),
        pltpu.VMEM((count, Q, 256), BF16),
        pltpu.VMEM((count, Q, 512), BF16),
        pltpu.VMEM((count, Q, 512), BF16),
    ]


def near_call(place, mask, xs, blocks):
    return kernel(
        near_kernel,
        [(1024, 512)],
        blocks,
        (place, mask),
        [
            pltpu.VMEM((4, Q, 128), F32),
            pltpu.SemaphoreType.DMA((6,)),
            pltpu.VMEM((4, Q, 256), BF16),
            pltpu.VMEM((4, Q, 1), F32),
        ]
        + block_scratch(2),
        xs,
        [((4, Q, 256), BF16), (4, Q, 1)],
    )


def far_call(place, mask, ridge, blocks, near, own_y, own_a, lead):
    near, rows, norms = near
    return kernel(
        far_kernel,
        [(4, RANK, 128)],
        [*blocks, near, own_y, own_a, lead, rows, norms],
        (place, mask, ridge),
        [pltpu.VMEM((2, 4, CHUNK, 128), F32), pltpu.SemaphoreType.DMA((2, 4))]
        + block_scratch(3),
        far_outs=[(1024, 128)] * 4,
    )


def picks_by_row(order, picks):
    at = lax.broadcasted_iota(jnp.int32, picks.shape, 0)
    picks[...] = jnp.where(order == at, 1.0, 0.0).astype(BF16)


def load_solve(basis, solve, basis_in, solve_in, sems):
    copies = [pltpu.make_async_copy(basis.at[0], basis_in, sems.at[4])]
    for k in range(4):
        rows = pl.ds(k * Q, Q)
        copies.append(
            pltpu.make_async_copy(solve.at[0, rows, :], solve_in.at[rows, :], sems.at[k])
        )
    for copy in copies:
        copy.start()
    return copies


SOLVE_SCRATCH = [
    pltpu.VMEM((1024, RANK), F32),
    pltpu.VMEM((1024, 1024), F32),
    pltpu.SemaphoreType.DMA((5,)),
]


def lead_kernel(order, basis, solve, lead, basis_in, solve_in, sems, picks, turned):
    first, *rest = load_solve(basis, solve, basis_in, solve_in, sems)
    picks_by_row(order[...], picks)
    first.wait()
    turned[...] = jnp.transpose(basis_in[...])
    for k in range(4):
        rest[k].wait()
        rows = slice(k * Q, (k + 1) * Q)
        term = dot3(turned[:, rows], solve_in[rows, :])
        if k:
            lead[...] += term
        else:
            lead[...] = term
    both = jnp.concatenate(split(lead[...]), axis=0)
    chosen = dot(both, picks[...], NT)
    lead[...] = chosen[:RANK] + chosen[RANK:]


def lead_call(order, leaf_basis, leaf_inverse):
    return kernel(
        lead_kernel,
        [(RANK, 1024)],
        [order],
        scratch=SOLVE_SCRATCH
        + [pltpu.VMEM((1024, 1024), BF16), pltpu.VMEM((RANK, 1024), F32)],
        far_values=[leaf_basis, leaf_inverse],
    )


def run_copies(sems, moves):
    copies = [
        pltpu.make_async_copy(source, target, sems.at[k])
        for k, (source, target) in enumerate(moves)
    ]
    for copy in copies:
        copy.start()
    for copy in copies:
        copy.wait()


def pack_kernel(a, b, out, buffer, sems):
    run_copies(sems, [(a, buffer.at[:, pl.ds(0, 128)]), (b, buffer.at[:, pl.ds(128, 512)])])
    run_copies(sems, [(buffer, out)])


def slices_kernel(transfer, inverse, out, buffer, sems):
    moves = [(transfer.at[0, pl.ds(256, 64), :], buffer.at[pl.ds(0, 64), :])]
    for k in range(4):
        source = inverse.at[0, pl.ds(320, 16), pl.ds(k * 256, 256)]
        moves.append((source, buffer.at[pl.ds(64 + k * 16, 16), :]))
    run_copies(sems, moves)
    run_copies(sems, [(buffer, out)])


def assemble(body, shape, count, *parts):
    return kernel(
        body,
        [],
        [],
        scratch=[pltpu.VMEM(shape, F32), pltpu.SemaphoreType.DMA((count,))],
        far_values=parts,
        far_outs=[shape],
    )


def pair_kernel(slices, lower, out):
    out[:128, :] = slices[...]
    out[128:, :] = lower[...]


def held_kernel(transfer, inverse, pair, mirrored, out, buffer, sems):
    moves = [
        (transfer.at[0, pl.ds(0, 256), :], buffer.at[pl.ds(0, 256), :]),
        (pair, buffer.at[pl.ds(512, 256), :]),
        (mirrored, buffer.at[pl.ds(768, 256), :]),
    ]
    for k in range(4):
        source = inverse.at[0, pl.ds(256, 64), pl.ds(k * 256, 256)]
        moves.append((source, buffer.at[pl.ds(256 + k * 64, 64), :]))
    run_copies(sems, moves)
    run_copies(sems, [(buffer, out)])


def nodes_kernel(place, b0, b1, b2, b3, e1, m2, f2, m3, own_e2, e2):
    q = place[3] % 4
    child = place[3] // 4 % 4
    parent = place[3] // 16
    odd = place[3] // 8 % 2
    for d, block in enumerate((b0, b1, b2, b3)):
        at = q ^ d
        e1[pl.ds(pl.multiple_of(at * 256, 256), 256), :] = block[:256, :]
        rows = pl.ds(pl.multiple_of(at * 64, 64), 64)
        for k in range(4):
            source = pl.multiple_of(256 + (child ^ k) * 64, 64)
            m2[rows, k * 256 : (k + 1) * 256] = block[pl.ds(source, 64), :]
        for s, (start, flip) in enumerate(((512, 0), (768, 2), (640, 0), (896, 2))):
            held = at ^ flip
            e2[pl.ds(pl.multiple_of(s * 256 + held * 64, 64), 64), :] = block[
                start : start + 64, :
            ]
            rows = pl.ds(pl.multiple_of((child ^ s) * 64 + held * 16, 16), 16)
            for k in range(4):
                step = (0, 3, 1, 2)[k] + odd * (0, -2, 2, 0)[k]
                source = pl.multiple_of(start + 64 + (parent + step) % 4 * 16, 16)
                m3[rows, k * 256 : (k + 1) * 256] = block[pl.ds(source, 16), :]
    own_e2[...] = e2[:256, :]
    f2[...] = dot3(m2[...], e2[...])


def nodes_call(place, blocks):
    return kernel(
        nodes_kernel,
        [(1024, 256), (256, 1024), (256, 256), (256, 1024), (256, 256)],
        blocks,
        (place,),
        [pltpu.VMEM((1024, 256), F32)],
    )


def level1_kernel(place, leaf_map, stacked, m1, e1, w1, p1):
    base = place[3] // 4 * 4
    total = None
    for k in range(4):
        term = dot3(m1[0, :256, k * 256 : (k + 1) * 256], stacked[leaf_map[base + k] - base])
        total = term if total is None else total + term
    w1[...] = total
    p1[...] = dot3(jnp.transpose(total), e1[0, :256, :])


def level1_call(place, leaf_map, stacked, node_inverse, node_transfer):
    return kernel(
        level1_kernel,
        [(256, 128), (128, 256)],
        [stacked, node_inverse, node_transfer],
        (place, leaf_map),
    )


def row_blocks(parts, matrix):
    total = None
    for k, part in enumerate(parts):
        term = dot3(part[...], matrix[:, k * 256 : (k + 1) * 256], NT)
        total = term if total is None else total + term
    return total


def level2_kernel(r0, r1, r2, r3, m2, e2, w2, p2):
    total = row_blocks((r0, r1, r2, r3), m2)
    w2[...] = total
    p2[...] = dot3(total, e2[...])


def level2_call(parts, m2, e2):
    return kernel(level2_kernel, [(32, 256), (32, 256)], [*parts, m2, e2])


def upper_kernel(r0, r1, r2, r3, m3, f2, w2, g1):
    g2 = row_blocks((r0, r1, r2, r3), m3)
    g1[...] = w2[...] - dot3(g2, f2[...], NT)


def upper_call(parts, m3, f2, w2):
    return kernel(upper_kernel, [(32, 256)], [*parts, m3, f2, w2])


def down1_kernel(g1, e1, m1, w1, v1, e1_in, m1_in, w1_in, sems):
    copies = [
        pltpu.make_async_copy(e1, e1_in, sems.at[0]),
        pltpu.make_async_copy(m1.at[0, pl.ds(0, 256), :], m1_in, sems.at[1]),
        pltpu.make_async_copy(w1, w1_in, sems.at[2]),
    ]
    for copy in copies:
        copy.start()
    g = g1[...].reshape(128, 256)
    copies[0].wait()
    lifted = dot3(g, e1_in[...], NT)
    copies[1].wait()
    copies[2].wait()
    v1[...] = w1_in[...] - dot3(m1_in[...], lifted, NT)


def down1_call(g1, e1, node_inverse, w1):
    return kernel(
        down1_kernel,
        [(256, 128)],
        [g1],
        scratch=[
            pltpu.VMEM((1024, 256), F32),
            pltpu.VMEM((256, 1024), F32),
            pltpu.VMEM((256, 128), F32),
            pltpu.SemaphoreType.DMA((3,)),
        ],
        far_values=[e1, node_inverse, w1],
    )


def residual_kernel(
    place, order, p0, p1, p2, p3, ordered_out, out0, out1, out2, out3, picks, res, ordered, sems
):
    res_sum = p0[...] + p1[...] + (p2[...] + p3[...])
    res[...] = res_sum
    rows = jnp.broadcast_to(order[...].astype(F32), (128, 1024))
    holds = jnp.transpose(rows)[:, :1].astype(jnp.int32)
    at = lax.broadcasted_iota(jnp.int32, (1024, 1024), 1)
    picks[...] = jnp.where(holds == at, 1.0, 0.0).astype(BF16)
    both = dot(picks[...], jnp.concatenate(split(res_sum), axis=1))
    ordered[...] = both[:, :128] + both[:, 128:]
    moves = [(ordered, ordered_out)]
    for k, out in enumerate((out0, out1, out2, out3)):
        rows = pl.ds(pl.multiple_of((place[2] + k) % 4 * Q, Q), Q)
        moves.append((res.at[rows, :], out))
    run_copies(sems, moves)


def residual_call(place, order, parts):
    return kernel(
        residual_kernel,
        [],
        [order, *parts],
        (place,),
        [
            pltpu.VMEM((1024, 1024), BF16),
            pltpu.VMEM((1024, 128), F32),
            pltpu.VMEM((1024, 128), F32),
            pltpu.SemaphoreType.DMA((5,)),
        ],
        far_outs=[(1024, 128)] + [(Q, 128)] * 4,
    )


def finish_kernel(
    place, leaf_map, order, pieces, ordered, basis, solve, delta,
    basis_in, solve_in, sems, picks, rhs, sides,
):
    first, *rest = load_solve(basis, solve, basis_in, solve_in, sems)
    base = place[3] // 4 * 4
    slot = jnp.int32(3)
    for k in range(3):
        slot = jnp.where(leaf_map[base + k] == place[3], k, slot)
    picks_by_row(order[...], picks)
    first.wait()
    rhs[...] = jnp.concatenate(
        split(ordered[...] - dot3(basis_in[...], pieces[slot])), axis=1
    )
    for k in range(4):
        rest[k].wait()
        rows = slice(k * Q, (k + 1) * Q)
        a, b = split(solve_in[rows, :])
        both = dot(a, rhs[...])
        y = both[:, :128] + (both[:, 128:] + dot(b, rhs[:, :128]))
        sides[rows, :] = jnp.concatenate(split(y), axis=1)

    @pl.loop(0, 2)
    def _(i):
        rows = pl.ds(pl.multiple_of(i * CHUNK, CHUNK), CHUNK)
        both = dot(picks[rows, :], sides[...])
        delta[rows, :] = both[:, :128] + both[:, 128:]


def finish_call(place, leaf_map, order, pieces, ordered, leaf_basis, leaf_inverse):
    return kernel(
        finish_kernel,
        [(1024, 128)],
        [order, pieces, ordered],
        (place, leaf_map),
        SOLVE_SCRATCH
        + [
            pltpu.VMEM((1024, 1024), BF16),
            pltpu.VMEM((1024, 256), BF16),
            pltpu.VMEM((1024, 256), BF16),
        ],
        [leaf_basis, leaf_inverse],
    )


def outputs_kernel(place, r0, r1, r2, r3, delta, coefs, out_res, out_new):
    for k, res in enumerate((r0, r1, r2, r3)):
        at = slice(k * 128, (k + 1) * 128)
        out_new[:, at] = coefs[:, at] + delta[k]
        source = pl.multiple_of((place[2] + 4 - k) % 4 * 128, 128)
        out_res[:, pl.ds(source, 128)] = res[...]


def outputs_call(place, res, delta, coefs):
    return pl.pallas_call(
        outputs_kernel,
        in_specs=[SMEM] + [VMEM] * 6,
        out_shape=[like(Q, 512), like(Q, 512)],
        compiler_params=pltpu.CompilerParams(vmem_limit_bytes=8 << 20),
        name="outputs",
    )(place, *[near_memory(value) for value in (*res, delta, coefs)])


def swap_cols(value):
    return lax.all_to_all(value, "col", 0, 0, tiled=True)


def step(
    points,
    coefs,
    targets,
    ridge,
    tile_mask,
    cluster_perm,
    leaf_map,
    leaf_inverse,
    leaf_basis,
    node_inverse,
    node_transfer,
):
    col = lax.axis_index("col")
    leaf = lax.axis_index("leaf")
    core = leaf % 2
    place = jnp.stack([core, leaf // 2 % 2, col, leaf]).astype(jnp.int32)

    xs = [points] + [col_shift(points, d) for d in (1, 2, 3)]
    packed = assemble(pack_kernel, (Q, 640), 2, points, coefs)
    left, right = leaf_from(packed, -2), leaf_from(packed, 2)
    partner = leaf_xor(packed, 1)
    relay = leaf_xor(jnp.where(core == 0, right, left), 1)

    nodes = (node_transfer, node_inverse)
    slices = assemble(slices_kernel, (128, 256), 5, *nodes)
    lower = leaf_route(slices, lambda i: facing(i, 0, 1))
    pair = kernel(pair_kernel, [(256, 256)], [slices, lower])
    mirrored = leaf_route(pair, lambda i: facing(i, 1, 0))
    held = assemble(held_kernel, (1024, 256), 7, *nodes, pair, mirrored)

    lead = lead_call(cluster_perm, leaf_basis, leaf_inverse)

    near = near_call(place, tile_mask, xs, (packed, partner))
    near, held = lax.optimization_barrier((near, held))
    across = leaf_xor(held, 2)
    own_core = leaf_xor(held, 1)
    both_ways = leaf_xor(across, 1)
    led, *partial = far_call(
        place, tile_mask, ridge, (left, right, relay), near, targets, coefs, lead
    )
    led = swap_cols(led)
    reduced = led.sum(0)
    e1, m2, f2, m3, e2 = nodes_call(place, (held, own_core, across, both_ways))

    columns = [partial[0]] + [col_shift(partial[d], d) for d in (1, 2, 3)]

    w1, p1 = level1_call(place, leaf_map, gather4(reduced, G4), node_inverse, node_transfer)
    p1 = lax.all_to_all(p1, "leaf", 0, 0, axis_index_groups=GK, tiled=True)
    p1 = p1.reshape(4, 32, RANK)
    r1 = p1[0] + p1[1] + (p1[2] + p1[3])
    w2, p2 = level2_call(siblings(r1), m2, e2)
    r2 = sum(siblings(p2))
    r2s = [r2, z_from(r2, -1, 1), z_from(r2, 2, -2), z_from(r2, -3, 3)]
    g1 = upper_call(r2s, m3, f2, w2)
    columns, g1 = lax.optimization_barrier((columns, g1))
    ordered, *pieces = residual_call(place, cluster_perm, columns)
    res_rows = [pieces[0]] + [col_shift(pieces[k], k) for k in (1, 2, 3)]
    g1 = gather4(g1, GK)
    pieces = gather4(down1_call(g1, e1, node_inverse, w1), G4)

    delta = finish_call(place, leaf_map, cluster_perm, pieces, ordered, leaf_basis, leaf_inverse)
    return outputs_call(place, res_rows, swap_cols(delta.reshape(4, Q, 128)), coefs)


def solution(mesh):
    return jax.shard_map(
        step,
        mesh=mesh,
        in_specs=(
            P(("leaf", "col"), None),
            P(("leaf", "col"), None),
            P(("leaf", "col"), None),
            P(),
            P("leaf", None),
            P("leaf", None),
            P(),
            P("leaf", None, None),
            P("leaf", None, None),
            P("leaf", None, None),
            P("leaf", None, None),
        ),
        out_specs=(P(("leaf", "col"), None), P(("leaf", "col"), None)),
        check_vma=False,
    )
```

```python
import jax
import jax.numpy as jnp
from jax import lax
from jax.experimental import pallas as pl
from jax.experimental.pallas import tpu as pltpu
from jax.sharding import PartitionSpec as P


F32 = jnp.float32
BF16 = jnp.bfloat16
Q = 256
RANK = 256
LEAVES = 64


def leaf_at(z, x_hi, kappa):
    x = 2 * x_hi + ((kappa >> 1) ^ x_hi)
    return z * 8 + x * 2 + (kappa & 1)


G4 = [[4 * n + k for k in range(4)] for n in range(16)]
GK = [[leaf_at(z, xh, k) for k in range(4)] for z in range(8) for xh in range(2)]


def facing(i, flip_x, flip_z):
    z, x, core = i // 8, i // 2 % 4, i % 2
    return (z ^ flip_z) * 8 + (3 - x if flip_x else x) * 2 + core


def leaf_route(value, target):
    return lax.ppermute(value, "leaf", [(i, target(i)) for i in range(LEAVES)])


def leaf_xor(value, bit):
    return leaf_route(value, lambda i: i ^ bit)


def leaf_from(value, step):
    return leaf_route(value, lambda i: (i - step) % LEAVES)


def siblings(value):
    return [value] + [
        leaf_route(value, lambda i, d=d: facing(i, d & 1, d >> 1)) for d in (1, 2, 3)
    ]


def z_from(value, even, odd):
    route = []
    for i in range(LEAVES):
        step = odd if i // 8 % 2 else even
        route.append(((i + 8 * step) % LEAVES, i))
    return lax.ppermute(value, "leaf", route)


def col_shift(value, step):
    return lax.ppermute(value, "col", [(i, (i + step) % 4) for i in range(4)])


def gather4(value, groups):
    return lax.all_gather(value, "leaf", axis=0, axis_index_groups=groups)


NN = ((1,), (0,))
NT = ((1,), (1,))


def dot(a, b, dims=NN):
    return lax.dot_general(a, b, (dims, ((), ())), preferred_element_type=F32)


def split(value):
    top = value.astype(BF16)
    return top, (value - top.astype(F32)).astype(BF16)


def dot3(a, b, dims=NN):
    at, al = split(a)
    bt, bl = split(b)
    return dot(at, bt, dims) + (dot(at, bl, dims) + dot(al, bt, dims))


SMEM = pl.BlockSpec(memory_space=pltpu.SMEM)
VMEM = pl.BlockSpec(memory_space=pltpu.VMEM)
HBM = pl.BlockSpec(memory_space=pltpu.HBM)


def near_memory(value):
    return pltpu.with_memory_space_constraint(value, pltpu.VMEM)


def far_memory(value):
    return pltpu.with_memory_space_constraint(value, pltpu.HBM)


def kernel(body, outs, values, scalars=(), scratch=(), far_values=(), far_outs=()):
    result = pl.pallas_call(
        body,
        in_specs=[SMEM] * len(scalars) + [VMEM] * len(values) + [HBM] * len(far_values),
        out_specs=[VMEM] * len(outs) + [HBM] * len(far_outs),
        out_shape=[pltpu.VMEM(shape, F32) for shape in outs]
        + [
            pltpu.HBM(*shape) if isinstance(shape[0], tuple) else pltpu.HBM(shape, F32)
            for shape in far_outs
        ],
        scratch_shapes=list(scratch),
        compiler_params=pltpu.CompilerParams(vmem_limit_bytes=20 << 20),
    )(*scalars, *[near_memory(value) for value in values], *[far_memory(value) for value in far_values])
    return result if len(outs) + len(far_outs) > 1 else result[0]


def like(*shape, dtype=F32):
    return jax.ShapeDtypeStruct(shape, dtype)


CHUNK = 512


def two_part(value):
    top, low = split(value)
    return jnp.concatenate([top, low], axis=1), top.astype(F32) + low.astype(F32)


def row_setup(place, xs, loaded, arrived, rows, norms):
    for k, ref in enumerate(xs):
        pltpu.make_async_copy(ref, loaded.at[k], arrived.at[k]).wait()
        at = (place[2] + 4 - k) % 4
        rows[at], exact = two_part(loaded[k])
        norms[at] = jnp.sum(exact * exact, axis=1, keepdims=True)


def block_setup(blocks, squares, others, tops, lows):
    for k, (y, a) in enumerate(blocks):
        others[k], exact = two_part(y)
        total = jnp.sum(exact * exact, axis=1, keepdims=True)
        squares[k] = jnp.transpose(jnp.broadcast_to(total, (Q, 128)))[:8]
        tops[k], lows[k] = split(a)


def tile_sum(i, weights, rows, norms, squares, others, tops, lows):
    x = rows[pl.ds(2 * i, 2)].reshape(CHUNK, 256)
    own = norms[pl.ds(2 * i, 2)].reshape(CHUNK, 1)
    total = None
    for k, weight in enumerate(weights):
        top, low = others[k][:, :128], others[k][:, 128:]
        inner = dot(x, jnp.concatenate([top, top], axis=1), NT)
        inner = inner + dot(x, jnp.concatenate([low, low], axis=1), NT)
        distance = own + squares[k][:1] - 2.0 * inner
        top, low = split(jnp.exp(distance * (-2.0 / 128.0)) * weight)
        term = dot(top, tops[k]) + dot(top, lows[k]) + dot(low, tops[k])
        total = term if total is None else total + term
    return total


def near_kernel(
    place, mask, p0, p1, x0, x1, x2, x3, out, rows_out, norms_out, loaded, arrived, rows, norms, *scratch
):
    xs = (x0, x1, x2, x3)
    for k, ref in enumerate(xs):
        pltpu.make_async_copy(ref, loaded.at[k], arrived.at[k]).start()
    block_setup([(p[:, :128], p[:, 128:]) for p in (p0, p1)], *scratch)
    row_setup(place, xs, loaded, arrived, rows, norms)
    copies = [
        pltpu.make_async_copy(rows, rows_out, arrived.at[4]),
        pltpu.make_async_copy(norms, norms_out, arrived.at[5]),
    ]
    for copy in copies:
        copy.start()
    weights = (mask[0, 2].astype(F32), mask[0, 3 - 2 * place[0]].astype(F32))

    @pl.loop(0, 2)
    def _(i):
        at = pl.ds(pl.multiple_of(i * CHUNK, CHUNK), CHUNK)
        out[at, :] = tile_sum(i, weights, rows, norms, *scratch)

    for copy in copies:
        copy.wait()


def far_kernel(
    place, mask, ridge, p0, p1, p2, near, own_y, own_a, lead, split_rows, norms,
    led, out0, out1, out2, out3, parts, sems, *scratch
):
    block_setup([(p[:, :128], p[:, 128:]) for p in (p0, p1, p2)], *scratch)
    weights = (
        mask[0, 0].astype(F32),
        mask[0, 4].astype(F32),
        mask[0, 1 + 2 * place[0]].astype(F32),
    )
    for k in range(4):
        led[k] = jnp.zeros((RANK, 128), F32)

    def sent(i):
        rows = pl.ds(pl.multiple_of(i * CHUNK, CHUNK), CHUNK)
        return [
            pltpu.make_async_copy(
                parts.at[i, (place[2] + d) % 4], out.at[rows, :], sems.at[i, d]
            )
            for d, out in enumerate((out0, out1, out2, out3))
        ]

    @pl.loop(0, 2)
    def _(i):
        rows = pl.ds(pl.multiple_of(i * CHUNK, CHUNK), CHUNK)
        total = near[rows, :] + tile_sum(i, weights, split_rows, norms, *scratch)
        own = own_y[...] - ridge[0] * own_a[...]
        part = jnp.concatenate(
            [
                jnp.where(place[2] == 2 * i + h, own, 0.0) - total[h * Q : (h + 1) * Q]
                for h in range(2)
            ],
            axis=0,
        )
        product = dot3(lead[:, rows], part)
        for k in range(4):
            parts[i, k] = part[:, k * 128 : (k + 1) * 128]
            led[k] += product[:, k * 128 : (k + 1) * 128]
        for copy in sent(i):
            copy.start()

    for i in range(2):
        for copy in sent(i):
            copy.wait()


def block_scratch(count):
    return [
        pltpu.VMEM((count, 8, Q), F32),
        pltpu.VMEM((count, Q, 256), BF16),
        pltpu.VMEM((count, Q, 512), BF16),
        pltpu.VMEM((count, Q, 512), BF16),
    ]


def near_call(place, mask, xs, blocks):
    return kernel(
        near_kernel,
        [(1024, 512)],
        blocks,
        (place, mask),
        [
            pltpu.VMEM((4, Q, 128), F32),
            pltpu.SemaphoreType.DMA((6,)),
            pltpu.VMEM((4, Q, 256), BF16),
            pltpu.VMEM((4, Q, 1), F32),
        ]
        + block_scratch(2),
        xs,
        [((4, Q, 256), BF16), (4, Q, 1)],
    )


def far_call(place, mask, ridge, blocks, near, own_y, own_a, lead):
    near, rows, norms = near
    return kernel(
        far_kernel,
        [(4, RANK, 128)],
        [*blocks, near, own_y, own_a, lead, rows, norms],
        (place, mask, ridge),
        [pltpu.VMEM((2, 4, CHUNK, 128), F32), pltpu.SemaphoreType.DMA((2, 4))]
        + block_scratch(3),
        far_outs=[(1024, 128)] * 4,
    )


def picks_by_row(order, picks):
    at = lax.broadcasted_iota(jnp.int32, picks.shape, 0)
    picks[...] = jnp.where(order == at, 1.0, 0.0).astype(BF16)


def load_solve(basis, solve, basis_in, solve_in, sems):
    copies = [pltpu.make_async_copy(basis.at[0], basis_in, sems.at[4])]
    for k in range(4):
        rows = pl.ds(k * Q, Q)
        copies.append(
            pltpu.make_async_copy(solve.at[0, rows, :], solve_in.at[rows, :], sems.at[k])
        )
    for copy in copies:
        copy.start()
    return copies


SOLVE_SCRATCH = [
    pltpu.VMEM((1024, RANK), F32),
    pltpu.VMEM((1024, 1024), F32),
    pltpu.SemaphoreType.DMA((5,)),
]


def lead_kernel(order, basis, solve, lead, basis_in, solve_in, sems, picks, turned):
    first, *rest = load_solve(basis, solve, basis_in, solve_in, sems)
    picks_by_row(order[...], picks)
    first.wait()
    turned[...] = jnp.transpose(basis_in[...])
    for k in range(4):
        rest[k].wait()
        rows = slice(k * Q, (k + 1) * Q)
        term = dot3(turned[:, rows], solve_in[rows, :])
        if k:
            lead[...] += term
        else:
            lead[...] = term
    both = jnp.concatenate(split(lead[...]), axis=0)
    chosen = dot(both, picks[...], NT)
    lead[...] = chosen[:RANK] + chosen[RANK:]


def lead_call(order, leaf_basis, leaf_inverse):
    return kernel(
        lead_kernel,
        [(RANK, 1024)],
        [order],
        scratch=SOLVE_SCRATCH
        + [pltpu.VMEM((1024, 1024), BF16), pltpu.VMEM((RANK, 1024), F32)],
        far_values=[leaf_basis, leaf_inverse],
    )


def run_copies(sems, moves):
    copies = [
        pltpu.make_async_copy(source, target, sems.at[k])
        for k, (source, target) in enumerate(moves)
    ]
    for copy in copies:
        copy.start()
    for copy in copies:
        copy.wait()


def pack_kernel(a, b, out, buffer, sems):
    run_copies(sems, [(a, buffer.at[:, pl.ds(0, 128)]), (b, buffer.at[:, pl.ds(128, 512)])])
    run_copies(sems, [(buffer, out)])


def slices_kernel(transfer, inverse, out, buffer, sems):
    moves = [(transfer.at[0, pl.ds(256, 64), :], buffer.at[pl.ds(0, 64), :])]
    for k in range(4):
        source = inverse.at[0, pl.ds(320, 16), pl.ds(k * 256, 256)]
        moves.append((source, buffer.at[pl.ds(64 + k * 16, 16), :]))
    run_copies(sems, moves)
    run_copies(sems, [(buffer, out)])


def sum_kernel(parts, out):
    out[...] = parts[0] + parts[1] + (parts[2] + parts[3])


def assemble(body, shape, count, *parts):
    return kernel(
        body,
        [],
        [],
        scratch=[pltpu.VMEM(shape, F32), pltpu.SemaphoreType.DMA((count,))],
        far_values=parts,
        far_outs=[shape],
    )


def pair_kernel(slices, lower, out):
    out[:128, :] = slices[...]
    out[128:, :] = lower[...]


def held_kernel(pair, mirrored, transfer, inverse, out, buffer, sems):
    moves = [(transfer.at[0, pl.ds(0, 256), :], buffer.at[pl.ds(0, 256), :])]
    for k in range(4):
        source = inverse.at[0, pl.ds(256, 64), pl.ds(k * 256, 256)]
        moves.append((source, buffer.at[pl.ds(256 + k * 64, 64), :]))
    copies = [
        pltpu.make_async_copy(source, target, sems.at[k])
        for k, (source, target) in enumerate(moves)
    ]
    for copy in copies:
        copy.start()
    buffer[512:768, :] = pair[...]
    buffer[768:, :] = mirrored[...]
    for copy in copies:
        copy.wait()
    run_copies(sems, [(buffer, out)])


def held_call(pair, mirrored, transfer, inverse):
    return kernel(
        held_kernel,
        [],
        [pair, mirrored],
        scratch=[pltpu.VMEM((1024, 256), F32), pltpu.SemaphoreType.DMA((5,))],
        far_values=[transfer, inverse],
        far_outs=[(1024, 256)],
    )


def nodes_kernel(place, b0, b1, b2, b3, e1, m2, f2, m3, own_e2, e2):
    q = place[3] % 4
    child = place[3] // 4 % 4
    parent = place[3] // 16
    odd = place[3] // 8 % 2
    for d, block in enumerate((b0, b1, b2, b3)):
        at = q ^ d
        e1[pl.ds(pl.multiple_of(at * 256, 256), 256), :] = block[:256, :]
        rows = pl.ds(pl.multiple_of(at * 64, 64), 64)
        for k in range(4):
            source = pl.multiple_of(256 + (child ^ k) * 64, 64)
            m2[rows, k * 256 : (k + 1) * 256] = block[pl.ds(source, 64), :]
        for s, (start, flip) in enumerate(((512, 0), (768, 2), (640, 0), (896, 2))):
            held = at ^ flip
            e2[pl.ds(pl.multiple_of(s * 256 + held * 64, 64), 64), :] = block[
                start : start + 64, :
            ]
            rows = pl.ds(pl.multiple_of((child ^ s) * 64 + held * 16, 16), 16)
            for k in range(4):
                step = (0, 3, 1, 2)[k] + odd * (0, -2, 2, 0)[k]
                source = pl.multiple_of(start + 64 + (parent + step) % 4 * 16, 16)
                m3[rows, k * 256 : (k + 1) * 256] = block[pl.ds(source, 16), :]
    own_e2[...] = e2[:256, :]
    f2[...] = dot3(m2[...], e2[...])


def nodes_call(place, blocks):
    return kernel(
        nodes_kernel,
        [(1024, 256), (256, 1024), (256, 256), (256, 1024), (256, 256)],
        blocks,
        (place,),
        [pltpu.VMEM((1024, 256), F32)],
    )


def level1_kernel(place, leaf_map, stacked, m1, e1, w1, p1):
    base = place[3] // 4 * 4
    total = None
    for k in range(4):
        term = dot3(m1[0, :256, k * 256 : (k + 1) * 256], stacked[leaf_map[base + k] - base])
        total = term if total is None else total + term
    w1[...] = total
    p1[...] = dot3(jnp.transpose(total), e1[0, :256, :])


def level1_call(place, leaf_map, stacked, node_inverse, node_transfer):
    return kernel(
        level1_kernel,
        [(256, 128), (128, 256)],
        [stacked, node_inverse, node_transfer],
        (place, leaf_map),
    )


def row_blocks(parts, matrix):
    total = None
    for k, part in enumerate(parts):
        term = dot3(part[...], matrix[:, k * 256 : (k + 1) * 256], NT)
        total = term if total is None else total + term
    return total


def level2_kernel(r0, r1, r2, r3, m2, e2, w2, p2):
    total = row_blocks((r0, r1, r2, r3), m2)
    w2[...] = total
    p2[...] = dot3(total, e2[...])


def level2_call(parts, m2, e2):
    return kernel(level2_kernel, [(32, 256), (32, 256)], [*parts, m2, e2])


def upper_kernel(r0, r1, r2, r3, m3, f2, w2, g1):
    g2 = row_blocks((r0, r1, r2, r3), m3)
    g1[...] = w2[...] - dot3(g2, f2[...], NT)


def upper_call(parts, m3, f2, w2):
    return kernel(upper_kernel, [(32, 256)], [*parts, m3, f2, w2])


def down1_kernel(g1, e1, m1, w1, v1, e1_in, m1_in, w1_in, sems):
    copies = [
        pltpu.make_async_copy(e1, e1_in, sems.at[0]),
        pltpu.make_async_copy(m1.at[0, pl.ds(0, 256), :], m1_in, sems.at[1]),
        pltpu.make_async_copy(w1, w1_in, sems.at[2]),
    ]
    for copy in copies:
        copy.start()
    g = g1[...].reshape(128, 256)
    copies[0].wait()
    lifted = dot3(g, e1_in[...], NT)
    copies[1].wait()
    copies[2].wait()
    v1[...] = w1_in[...] - dot3(m1_in[...], lifted, NT)


def down1_call(g1, e1, node_inverse, w1):
    return kernel(
        down1_kernel,
        [(256, 128)],
        [g1],
        scratch=[
            pltpu.VMEM((1024, 256), F32),
            pltpu.VMEM((256, 1024), F32),
            pltpu.VMEM((256, 128), F32),
            pltpu.SemaphoreType.DMA((3,)),
        ],
        far_values=[e1, node_inverse, w1],
    )


def residual_kernel(
    place, order, p0, p1, p2, p3, ordered_out, out0, out1, out2, out3, picks, res, ordered, sems
):
    res_sum = p0[...] + p1[...] + (p2[...] + p3[...])
    res[...] = res_sum
    rows = jnp.broadcast_to(order[...].astype(F32), (128, 1024))
    holds = jnp.transpose(rows)[:, :1].astype(jnp.int32)
    at = lax.broadcasted_iota(jnp.int32, (1024, 1024), 1)
    picks[...] = jnp.where(holds == at, 1.0, 0.0).astype(BF16)
    both = dot(picks[...], jnp.concatenate(split(res_sum), axis=1))
    ordered[...] = both[:, :128] + both[:, 128:]
    moves = [(ordered, ordered_out)]
    for k, out in enumerate((out0, out1, out2, out3)):
        rows = pl.ds(pl.multiple_of((place[2] + k) % 4 * Q, Q), Q)
        moves.append((res.at[rows, :], out))
    run_copies(sems, moves)


def residual_call(place, order, parts):
    return kernel(
        residual_kernel,
        [],
        [order, *parts],
        (place,),
        [
            pltpu.VMEM((1024, 1024), BF16),
            pltpu.VMEM((1024, 128), F32),
            pltpu.VMEM((1024, 128), F32),
            pltpu.SemaphoreType.DMA((5,)),
        ],
        far_outs=[(1024, 128)] + [(Q, 128)] * 4,
    )


def finish_kernel(
    place, leaf_map, order, pieces, ordered, basis, solve, delta,
    basis_in, solve_in, sems, picks, rhs, sides,
):
    first, *rest = load_solve(basis, solve, basis_in, solve_in, sems)
    base = place[3] // 4 * 4
    slot = jnp.int32(3)
    for k in range(3):
        slot = jnp.where(leaf_map[base + k] == place[3], k, slot)
    picks_by_row(order[...], picks)
    first.wait()
    rhs[...] = jnp.concatenate(
        split(ordered[...] - dot3(basis_in[...], pieces[slot])), axis=1
    )
    for k in range(4):
        rest[k].wait()
        rows = slice(k * Q, (k + 1) * Q)
        a, b = split(solve_in[rows, :])
        both = dot(a, rhs[...])
        y = both[:, :128] + (both[:, 128:] + dot(b, rhs[:, :128]))
        sides[rows, :] = jnp.concatenate(split(y), axis=1)

    @pl.loop(0, 2)
    def _(i):
        rows = pl.ds(pl.multiple_of(i * CHUNK, CHUNK), CHUNK)
        both = dot(picks[rows, :], sides[...])
        delta[rows, :] = both[:, :128] + both[:, 128:]


def finish_call(place, leaf_map, order, pieces, ordered, leaf_basis, leaf_inverse):
    return kernel(
        finish_kernel,
        [(1024, 128)],
        [order, pieces, ordered],
        (place, leaf_map),
        SOLVE_SCRATCH
        + [
            pltpu.VMEM((1024, 1024), BF16),
            pltpu.VMEM((1024, 256), BF16),
            pltpu.VMEM((1024, 256), BF16),
        ],
        [leaf_basis, leaf_inverse],
    )


def outputs_kernel(place, r0, r1, r2, r3, delta, coefs, out_res, out_new):
    for k, res in enumerate((r0, r1, r2, r3)):
        at = slice(k * 128, (k + 1) * 128)
        out_new[:, at] = coefs[:, at] + delta[k]
        source = pl.multiple_of((place[2] + 4 - k) % 4 * 128, 128)
        out_res[:, pl.ds(source, 128)] = res[...]


def outputs_call(place, res, delta, coefs):
    return pl.pallas_call(
        outputs_kernel,
        in_specs=[SMEM] + [VMEM] * 6,
        out_shape=[like(Q, 512), like(Q, 512)],
        compiler_params=pltpu.CompilerParams(vmem_limit_bytes=8 << 20),
        name="outputs",
    )(place, *[near_memory(value) for value in (*res, delta, coefs)])


def swap_cols(value):
    return lax.all_to_all(value, "col", 0, 0, tiled=True)


def step(
    points,
    coefs,
    targets,
    ridge,
    tile_mask,
    cluster_perm,
    leaf_map,
    leaf_inverse,
    leaf_basis,
    node_inverse,
    node_transfer,
):
    col = lax.axis_index("col")
    leaf = lax.axis_index("leaf")
    core = leaf % 2
    place = jnp.stack([core, leaf // 2 % 2, col, leaf]).astype(jnp.int32)

    xs = [points] + [col_shift(points, d) for d in (1, 2, 3)]
    packed = assemble(pack_kernel, (Q, 640), 2, points, coefs)
    left, right = leaf_from(packed, -2), leaf_from(packed, 2)
    partner = leaf_xor(packed, 1)
    relay = leaf_xor(jnp.where(core == 0, right, left), 1)

    nodes = (node_transfer, node_inverse)
    slices = assemble(slices_kernel, (128, 256), 5, *nodes)
    lower = leaf_route(slices, lambda i: facing(i, 0, 1))
    pair = kernel(pair_kernel, [(256, 256)], [slices, lower])
    mirrored = leaf_route(pair, lambda i: facing(i, 1, 0))
    held = held_call(pair, mirrored, *nodes)

    lead = lead_call(cluster_perm, leaf_basis, leaf_inverse)

    near = near_call(place, tile_mask, xs, (packed, partner))
    across = leaf_xor(held, 2)
    own_core = leaf_xor(held, 1)
    both_ways = leaf_xor(across, 1)
    led, *partial = far_call(
        place, tile_mask, ridge, (left, right, relay), near, targets, coefs, lead
    )
    led = swap_cols(led)
    reduced = kernel(sum_kernel, [(RANK, 128)], [led])
    e1, m2, f2, m3, e2 = nodes_call(place, (held, own_core, across, both_ways))

    columns = [partial[0]] + [col_shift(partial[d], d) for d in (1, 2, 3)]

    w1, p1 = level1_call(place, leaf_map, gather4(reduced, G4), node_inverse, node_transfer)
    p1 = lax.all_to_all(p1, "leaf", 0, 0, axis_index_groups=GK, tiled=True)
    p1 = p1.reshape(4, 32, RANK)
    r1 = p1[0] + p1[1] + (p1[2] + p1[3])
    w2, p2 = level2_call(siblings(r1), m2, e2)
    r2 = sum(siblings(p2))
    r2s = [r2, z_from(r2, -1, 1), z_from(r2, 2, -2), z_from(r2, -3, 3)]
    g1 = upper_call(r2s, m3, f2, w2)
    columns, g1 = lax.optimization_barrier((columns, g1))
    ordered, *pieces = residual_call(place, cluster_perm, columns)
    res_rows = [pieces[0]] + [col_shift(pieces[k], k) for k in (1, 2, 3)]
    g1 = gather4(g1, GK)
    pieces = gather4(down1_call(g1, e1, node_inverse, w1), G4)

    delta = finish_call(place, leaf_map, cluster_perm, pieces, ordered, leaf_basis, leaf_inverse)
    return outputs_call(place, res_rows, swap_cols(delta.reshape(4, Q, 128)), coefs)


def solution(mesh):
    return jax.shard_map(
        step,
        mesh=mesh,
        in_specs=(
            P(("leaf", "col"), None),
            P(("leaf", "col"), None),
            P(("leaf", "col"), None),
            P(),
            P("leaf", None),
            P("leaf", None),
            P(),
            P("leaf", None, None),
            P("leaf", None, None),
            P("leaf", None, None),
            P("leaf", None, None),
        ),
        out_specs=(P(("leaf", "col"), None), P(("leaf", "col"), None)),
        check_vma=False,
    )
```

```python
import jax
import jax.numpy as jnp
from jax import lax
from jax.experimental import pallas as pl
from jax.experimental.pallas import tpu as pltpu
from jax.sharding import PartitionSpec as P


F32 = jnp.float32
BF16 = jnp.bfloat16
Q = 256
RANK = 256
LEAVES = 64


def leaf_at(z, x_hi, kappa):
    x = 2 * x_hi + ((kappa >> 1) ^ x_hi)
    return z * 8 + x * 2 + (kappa & 1)


G4 = [[4 * n + k for k in range(4)] for n in range(16)]
GK = [[leaf_at(z, xh, k) for k in range(4)] for z in range(8) for xh in range(2)]


def facing(i, flip_x, flip_z):
    z, x, core = i // 8, i // 2 % 4, i % 2
    return (z ^ flip_z) * 8 + (3 - x if flip_x else x) * 2 + core


def leaf_route(value, target):
    return lax.ppermute(value, "leaf", [(i, target(i)) for i in range(LEAVES)])


def leaf_xor(value, bit):
    return leaf_route(value, lambda i: i ^ bit)


def leaf_from(value, step):
    return leaf_route(value, lambda i: (i - step) % LEAVES)


def siblings(value):
    return [value] + [
        leaf_route(value, lambda i, d=d: facing(i, d & 1, d >> 1)) for d in (1, 2, 3)
    ]


def z_from(value, even, odd):
    route = []
    for i in range(LEAVES):
        step = odd if i // 8 % 2 else even
        route.append(((i + 8 * step) % LEAVES, i))
    return lax.ppermute(value, "leaf", route)


def col_shift(value, step):
    return lax.ppermute(value, "col", [(i, (i + step) % 4) for i in range(4)])


def gather4(value, groups):
    return lax.all_gather(value, "leaf", axis=0, axis_index_groups=groups)


NN = ((1,), (0,))
NT = ((1,), (1,))


def dot(a, b, dims=NN):
    return lax.dot_general(a, b, (dims, ((), ())), preferred_element_type=F32)


def split(value):
    top = value.astype(BF16)
    return top, (value - top.astype(F32)).astype(BF16)


def dot3(a, b, dims=NN):
    at, al = split(a)
    bt, bl = split(b)
    return dot(at, bt, dims) + (dot(at, bl, dims) + dot(al, bt, dims))


SMEM = pl.BlockSpec(memory_space=pltpu.SMEM)
VMEM = pl.BlockSpec(memory_space=pltpu.VMEM)
HBM = pl.BlockSpec(memory_space=pltpu.HBM)


def near_memory(value):
    return pltpu.with_memory_space_constraint(value, pltpu.VMEM)


def far_memory(value):
    return pltpu.with_memory_space_constraint(value, pltpu.HBM)


def kernel(body, outs, values, scalars=(), scratch=(), far_values=(), far_outs=()):
    result = pl.pallas_call(
        body,
        in_specs=[SMEM] * len(scalars) + [VMEM] * len(values) + [HBM] * len(far_values),
        out_specs=[VMEM] * len(outs) + [HBM] * len(far_outs),
        out_shape=[pltpu.VMEM(shape, F32) for shape in outs]
        + [
            pltpu.HBM(*shape) if isinstance(shape[0], tuple) else pltpu.HBM(shape, F32)
            for shape in far_outs
        ],
        scratch_shapes=list(scratch),
        compiler_params=pltpu.CompilerParams(vmem_limit_bytes=20 << 20),
    )(*scalars, *[near_memory(value) for value in values], *[far_memory(value) for value in far_values])
    return result if len(outs) + len(far_outs) > 1 else result[0]


def like(*shape, dtype=F32):
    return jax.ShapeDtypeStruct(shape, dtype)


CHUNK = 512


def two_part(value):
    top, low = split(value)
    return jnp.concatenate([top, low], axis=1), top.astype(F32) + low.astype(F32)


def row_setup(place, xs, loaded, arrived, rows, norms):
    for k, ref in enumerate(xs):
        pltpu.make_async_copy(ref, loaded.at[k], arrived.at[k]).wait()
        at = (place[2] + 4 - k) % 4
        rows[at], exact = two_part(loaded[k])
        norms[at] = jnp.sum(exact * exact, axis=1, keepdims=True)


def block_setup(blocks, squares, others, tops, lows):
    for k, (y, a) in enumerate(blocks):
        others[k], exact = two_part(y)
        total = jnp.sum(exact * exact, axis=1, keepdims=True)
        squares[k] = jnp.transpose(jnp.broadcast_to(total, (Q, 128)))[:8]
        tops[k], lows[k] = split(a)


def tile_sum(i, weights, rows, norms, squares, others, tops, lows):
    x = rows[pl.ds(2 * i, 2)].reshape(CHUNK, 256)
    own = norms[pl.ds(2 * i, 2)].reshape(CHUNK, 1)
    total = None
    for k, weight in enumerate(weights):
        top, low = others[k][:, :128], others[k][:, 128:]
        inner = dot(x, jnp.concatenate([top, top], axis=1), NT)
        inner = inner + dot(x, jnp.concatenate([low, low], axis=1), NT)
        distance = own + squares[k][:1] - 2.0 * inner
        top, low = split(jnp.exp(distance * (-2.0 / 128.0)) * weight)
        term = dot(top, tops[k]) + dot(top, lows[k]) + dot(low, tops[k])
        total = term if total is None else total + term
    return total


def near_kernel(
    place, mask, p0, p1, x0, x1, x2, x3, out, rows_out, norms_out, loaded, arrived, rows, norms, *scratch
):
    xs = (x0, x1, x2, x3)
    for k, ref in enumerate(xs):
        pltpu.make_async_copy(ref, loaded.at[k], arrived.at[k]).start()
    block_setup([(p[:, :128], p[:, 128:]) for p in (p0, p1)], *scratch)
    row_setup(place, xs, loaded, arrived, rows, norms)
    copies = [
        pltpu.make_async_copy(rows, rows_out, arrived.at[4]),
        pltpu.make_async_copy(norms, norms_out, arrived.at[5]),
    ]
    for copy in copies:
        copy.start()
    weights = (mask[0, 2].astype(F32), mask[0, 3 - 2 * place[0]].astype(F32))

    @pl.loop(0, 2)
    def _(i):
        at = pl.ds(pl.multiple_of(i * CHUNK, CHUNK), CHUNK)
        out[at, :] = tile_sum(i, weights, rows, norms, *scratch)

    for copy in copies:
        copy.wait()


def far_kernel(
    place, mask, ridge, p0, p1, p2, near, own_y, own_a, lead, split_rows, norms,
    led, out0, out1, out2, out3, parts, sems, *scratch
):
    block_setup([(p[:, :128], p[:, 128:]) for p in (p0, p1, p2)], *scratch)
    weights = (
        mask[0, 0].astype(F32),
        mask[0, 4].astype(F32),
        mask[0, 1 + 2 * place[0]].astype(F32),
    )
    for k in range(4):
        led[k] = jnp.zeros((RANK, 128), F32)

    def sent(i):
        rows = pl.ds(pl.multiple_of(i * CHUNK, CHUNK), CHUNK)
        return [
            pltpu.make_async_copy(
                parts.at[i, (place[2] + d) % 4], out.at[rows, :], sems.at[i, d]
            )
            for d, out in enumerate((out0, out1, out2, out3))
        ]

    @pl.loop(0, 2)
    def _(i):
        rows = pl.ds(pl.multiple_of(i * CHUNK, CHUNK), CHUNK)
        total = near[rows, :] + tile_sum(i, weights, split_rows, norms, *scratch)
        own = own_y[...] - ridge[0] * own_a[...]
        part = jnp.concatenate(
            [
                jnp.where(place[2] == 2 * i + h, own, 0.0) - total[h * Q : (h + 1) * Q]
                for h in range(2)
            ],
            axis=0,
        )
        product = dot3(lead[:, rows], part)
        for k in range(4):
            parts[i, k] = part[:, k * 128 : (k + 1) * 128]
            led[k] += product[:, k * 128 : (k + 1) * 128]
        for copy in sent(i):
            copy.start()

    for i in range(2):
        for copy in sent(i):
            copy.wait()


def block_scratch(count):
    return [
        pltpu.VMEM((count, 8, Q), F32),
        pltpu.VMEM((count, Q, 256), BF16),
        pltpu.VMEM((count, Q, 512), BF16),
        pltpu.VMEM((count, Q, 512), BF16),
    ]


def near_call(place, mask, xs, blocks):
    return kernel(
        near_kernel,
        [(1024, 512)],
        blocks,
        (place, mask),
        [
            pltpu.VMEM((4, Q, 128), F32),
            pltpu.SemaphoreType.DMA((6,)),
            pltpu.VMEM((4, Q, 256), BF16),
            pltpu.VMEM((4, Q, 1), F32),
        ]
        + block_scratch(2),
        xs,
        [((4, Q, 256), BF16), (4, Q, 1)],
    )


def far_call(place, mask, ridge, blocks, near, own_y, own_a, lead):
    near, rows, norms = near
    return kernel(
        far_kernel,
        [(4, RANK, 128)],
        [*blocks, near, own_y, own_a, lead, rows, norms],
        (place, mask, ridge),
        [pltpu.VMEM((2, 4, CHUNK, 128), F32), pltpu.SemaphoreType.DMA((2, 4))]
        + block_scratch(3),
        far_outs=[(1024, 128)] * 4,
    )


def picks_by_row(order, picks):
    at = lax.broadcasted_iota(jnp.int32, picks.shape, 0)
    picks[...] = jnp.where(order == at, 1.0, 0.0).astype(BF16)


def load_solve(basis, solve, basis_in, solve_in, sems):
    copies = [pltpu.make_async_copy(basis.at[0], basis_in, sems.at[4])]
    for k in range(4):
        rows = pl.ds(k * Q, Q)
        copies.append(
            pltpu.make_async_copy(solve.at[0, rows, :], solve_in.at[rows, :], sems.at[k])
        )
    for copy in copies:
        copy.start()
    return copies


SOLVE_SCRATCH = [
    pltpu.VMEM((1024, RANK), F32),
    pltpu.VMEM((1024, 1024), F32),
    pltpu.SemaphoreType.DMA((5,)),
]


def lead_kernel(order, basis, solve, lead, basis_in, solve_in, sems, picks, turned):
    first, *rest = load_solve(basis, solve, basis_in, solve_in, sems)
    picks_by_row(order[...], picks)
    first.wait()
    turned[...] = jnp.transpose(basis_in[...])
    for k in range(4):
        rest[k].wait()
        rows = slice(k * Q, (k + 1) * Q)
        term = dot3(turned[:, rows], solve_in[rows, :])
        if k:
            lead[...] += term
        else:
            lead[...] = term
    both = jnp.concatenate(split(lead[...]), axis=0)
    chosen = dot(both, picks[...], NT)
    lead[...] = chosen[:RANK] + chosen[RANK:]


def lead_call(order, leaf_basis, leaf_inverse):
    return kernel(
        lead_kernel,
        [(RANK, 1024)],
        [order],
        scratch=SOLVE_SCRATCH
        + [pltpu.VMEM((1024, 1024), BF16), pltpu.VMEM((RANK, 1024), F32)],
        far_values=[leaf_basis, leaf_inverse],
    )


def run_copies(sems, moves):
    copies = [
        pltpu.make_async_copy(source, target, sems.at[k])
        for k, (source, target) in enumerate(moves)
    ]
    for copy in copies:
        copy.start()
    for copy in copies:
        copy.wait()


def pack_kernel(a, b, out, buffer, sems):
    run_copies(sems, [(a, buffer.at[:, pl.ds(0, 128)]), (b, buffer.at[:, pl.ds(128, 512)])])
    run_copies(sems, [(buffer, out)])


def slices_kernel(transfer, inverse, out, buffer, sems):
    moves = [(transfer.at[0, pl.ds(256, 64), :], buffer.at[pl.ds(0, 64), :])]
    for k in range(4):
        source = inverse.at[0, pl.ds(320, 16), pl.ds(k * 256, 256)]
        moves.append((source, buffer.at[pl.ds(64 + k * 16, 16), :]))
    run_copies(sems, moves)
    run_copies(sems, [(buffer, out)])


def assemble(body, shape, count, *parts):
    return kernel(
        body,
        [],
        [],
        scratch=[pltpu.VMEM(shape, F32), pltpu.SemaphoreType.DMA((count,))],
        far_values=parts,
        far_outs=[shape],
    )


def pair_kernel(slices, lower, out):
    out[:128, :] = slices[...]
    out[128:, :] = lower[...]


def held_kernel(pair, mirrored, transfer, inverse, out, buffer, sems):
    moves = [(transfer.at[0, pl.ds(0, 256), :], buffer.at[pl.ds(0, 256), :])]
    for k in range(4):
        source = inverse.at[0, pl.ds(256, 64), pl.ds(k * 256, 256)]
        moves.append((source, buffer.at[pl.ds(256 + k * 64, 64), :]))
    copies = [
        pltpu.make_async_copy(source, target, sems.at[k])
        for k, (source, target) in enumerate(moves)
    ]
    for copy in copies:
        copy.start()
    buffer[512:768, :] = pair[...]
    buffer[768:, :] = mirrored[...]
    for copy in copies:
        copy.wait()
    run_copies(sems, [(buffer, out)])


def held_call(pair, mirrored, transfer, inverse):
    return kernel(
        held_kernel,
        [],
        [pair, mirrored],
        scratch=[pltpu.VMEM((1024, 256), F32), pltpu.SemaphoreType.DMA((5,))],
        far_values=[transfer, inverse],
        far_outs=[(1024, 256)],
    )


def nodes_kernel(place, b0, b1, b2, b3, e1, m2, f2, m3, own_e2, e2):
    q = place[3] % 4
    child = place[3] // 4 % 4
    parent = place[3] // 16
    odd = place[3] // 8 % 2
    for d, block in enumerate((b0, b1, b2, b3)):
        at = q ^ d
        e1[pl.ds(pl.multiple_of(at * 256, 256), 256), :] = block[:256, :]
        rows = pl.ds(pl.multiple_of(at * 64, 64), 64)
        for k in range(4):
            source = pl.multiple_of(256 + (child ^ k) * 64, 64)
            m2[rows, k * 256 : (k + 1) * 256] = block[pl.ds(source, 64), :]
        for s, (start, flip) in enumerate(((512, 0), (768, 2), (640, 0), (896, 2))):
            held = at ^ flip
            e2[pl.ds(pl.multiple_of(s * 256 + held * 64, 64), 64), :] = block[
                start : start + 64, :
            ]
            rows = pl.ds(pl.multiple_of((child ^ s) * 64 + held * 16, 16), 16)
            for k in range(4):
                step = (0, 3, 1, 2)[k] + odd * (0, -2, 2, 0)[k]
                source = pl.multiple_of(start + 64 + (parent + step) % 4 * 16, 16)
                m3[rows, k * 256 : (k + 1) * 256] = block[pl.ds(source, 16), :]
    own_e2[...] = e2[:256, :]
    f2[...] = dot3(m2[...], e2[...])


def nodes_call(place, blocks):
    return kernel(
        nodes_kernel,
        [(1024, 256), (256, 1024), (256, 256), (256, 1024), (256, 256)],
        blocks,
        (place,),
        [pltpu.VMEM((1024, 256), F32)],
    )


def level1_kernel(place, leaf_map, stacked, m1, e1, w1, p1):
    base = place[3] // 4 * 4
    total = None
    for k in range(4):
        term = dot3(m1[0, :256, k * 256 : (k + 1) * 256], stacked[leaf_map[base + k] - base])
        total = term if total is None else total + term
    w1[...] = total
    p1[...] = dot3(jnp.transpose(total), e1[0, :256, :])


def level1_call(place, leaf_map, stacked, node_inverse, node_transfer):
    return kernel(
        level1_kernel,
        [(256, 128), (128, 256)],
        [stacked, node_inverse, node_transfer],
        (place, leaf_map),
    )


def row_blocks(parts, matrix):
    total = None
    for k, part in enumerate(parts):
        term = dot3(part[...], matrix[:, k * 256 : (k + 1) * 256], NT)
        total = term if total is None else total + term
    return total


def level2_kernel(r0, r1, r2, r3, m2, e2, w2, p2):
    total = row_blocks((r0, r1, r2, r3), m2)
    w2[...] = total
    p2[...] = dot3(total, e2[...])


def level2_call(parts, m2, e2):
    return kernel(level2_kernel, [(32, 256), (32, 256)], [*parts, m2, e2])


def upper_kernel(r0, r1, r2, r3, m3, f2, w2, g1):
    g2 = row_blocks((r0, r1, r2, r3), m3)
    g1[...] = w2[...] - dot3(g2, f2[...], NT)


def upper_call(parts, m3, f2, w2):
    return kernel(upper_kernel, [(32, 256)], [*parts, m3, f2, w2])


def down1_kernel(g1, e1, m1, w1, v1, e1_in, m1_in, w1_in, sems):
    copies = [
        pltpu.make_async_copy(e1, e1_in, sems.at[0]),
        pltpu.make_async_copy(m1.at[0, pl.ds(0, 256), :], m1_in, sems.at[1]),
        pltpu.make_async_copy(w1, w1_in, sems.at[2]),
    ]
    for copy in copies:
        copy.start()
    g = g1[...].reshape(128, 256)
    copies[0].wait()
    lifted = dot3(g, e1_in[...], NT)
    copies[1].wait()
    copies[2].wait()
    v1[...] = w1_in[...] - dot3(m1_in[...], lifted, NT)


def down1_call(g1, e1, node_inverse, w1):
    return kernel(
        down1_kernel,
        [(256, 128)],
        [g1],
        scratch=[
            pltpu.VMEM((1024, 256), F32),
            pltpu.VMEM((256, 1024), F32),
            pltpu.VMEM((256, 128), F32),
            pltpu.SemaphoreType.DMA((3,)),
        ],
        far_values=[e1, node_inverse, w1],
    )


def residual_kernel(
    place, order, p0, p1, p2, p3, ordered_out, out0, out1, out2, out3, picks, res, ordered, sems
):
    res_sum = p0[...] + p1[...] + (p2[...] + p3[...])
    res[...] = res_sum
    rows = jnp.broadcast_to(order[...].astype(F32), (128, 1024))
    holds = jnp.transpose(rows)[:, :1].astype(jnp.int32)
    at = lax.broadcasted_iota(jnp.int32, (1024, 1024), 1)
    picks[...] = jnp.where(holds == at, 1.0, 0.0).astype(BF16)
    both = dot(picks[...], jnp.concatenate(split(res_sum), axis=1))
    ordered[...] = both[:, :128] + both[:, 128:]
    moves = [(ordered, ordered_out)]
    for k, out in enumerate((out0, out1, out2, out3)):
        rows = pl.ds(pl.multiple_of((place[2] + k) % 4 * Q, Q), Q)
        moves.append((res.at[rows, :], out))
    run_copies(sems, moves)


def residual_call(place, order, parts):
    return kernel(
        residual_kernel,
        [],
        [order, *parts],
        (place,),
        [
            pltpu.VMEM((1024, 1024), BF16),
            pltpu.VMEM((1024, 128), F32),
            pltpu.VMEM((1024, 128), F32),
            pltpu.SemaphoreType.DMA((5,)),
        ],
        far_outs=[(1024, 128)] + [(Q, 128)] * 4,
    )


def finish_kernel(
    place, leaf_map, order, pieces, ordered, basis, solve, delta,
    basis_in, solve_in, sems, picks, rhs, sides,
):
    first, *rest = load_solve(basis, solve, basis_in, solve_in, sems)
    base = place[3] // 4 * 4
    slot = jnp.int32(3)
    for k in range(3):
        slot = jnp.where(leaf_map[base + k] == place[3], k, slot)
    picks_by_row(order[...], picks)
    first.wait()
    rhs[...] = jnp.concatenate(
        split(ordered[...] - dot3(basis_in[...], pieces[slot])), axis=1
    )
    for k in range(4):
        rest[k].wait()
        rows = slice(k * Q, (k + 1) * Q)
        a, b = split(solve_in[rows, :])
        both = dot(a, rhs[...])
        y = both[:, :128] + (both[:, 128:] + dot(b, rhs[:, :128]))
        sides[rows, :] = jnp.concatenate(split(y), axis=1)

    @pl.loop(0, 2)
    def _(i):
        rows = pl.ds(pl.multiple_of(i * CHUNK, CHUNK), CHUNK)
        both = dot(picks[rows, :], sides[...])
        delta[rows, :] = both[:, :128] + both[:, 128:]


def finish_call(place, leaf_map, order, pieces, ordered, leaf_basis, leaf_inverse):
    return kernel(
        finish_kernel,
        [(1024, 128)],
        [order, pieces, ordered],
        (place, leaf_map),
        SOLVE_SCRATCH
        + [
            pltpu.VMEM((1024, 1024), BF16),
            pltpu.VMEM((1024, 256), BF16),
            pltpu.VMEM((1024, 256), BF16),
        ],
        [leaf_basis, leaf_inverse],
    )


def outputs_kernel(place, r0, r1, r2, r3, delta, coefs, out_res, out_new):
    for k, res in enumerate((r0, r1, r2, r3)):
        at = slice(k * 128, (k + 1) * 128)
        out_new[:, at] = coefs[:, at] + delta[k]
        source = pl.multiple_of((place[2] + 4 - k) % 4 * 128, 128)
        out_res[:, pl.ds(source, 128)] = res[...]


def outputs_call(place, res, delta, coefs):
    return pl.pallas_call(
        outputs_kernel,
        in_specs=[SMEM] + [VMEM] * 6,
        out_shape=[like(Q, 512), like(Q, 512)],
        compiler_params=pltpu.CompilerParams(vmem_limit_bytes=8 << 20),
        name="outputs",
    )(place, *[near_memory(value) for value in (*res, delta, coefs)])


def swap_cols(value):
    return lax.all_to_all(value, "col", 0, 0, tiled=True)


def step(
    points,
    coefs,
    targets,
    ridge,
    tile_mask,
    cluster_perm,
    leaf_map,
    leaf_inverse,
    leaf_basis,
    node_inverse,
    node_transfer,
):
    col = lax.axis_index("col")
    leaf = lax.axis_index("leaf")
    core = leaf % 2
    place = jnp.stack([core, leaf // 2 % 2, col, leaf]).astype(jnp.int32)

    xs = [points] + [col_shift(points, d) for d in (1, 2, 3)]
    packed = assemble(pack_kernel, (Q, 640), 2, points, coefs)
    left, right = leaf_from(packed, -2), leaf_from(packed, 2)
    partner = leaf_xor(packed, 1)
    relay = leaf_xor(jnp.where(core == 0, right, left), 1)

    nodes = (node_transfer, node_inverse)
    slices = assemble(slices_kernel, (128, 256), 5, *nodes)
    lower = leaf_route(slices, lambda i: facing(i, 0, 1))
    pair = kernel(pair_kernel, [(256, 256)], [slices, lower])
    mirrored = leaf_route(pair, lambda i: facing(i, 1, 0))
    held = held_call(pair, mirrored, *nodes)

    lead = lead_call(cluster_perm, leaf_basis, leaf_inverse)

    near = near_call(place, tile_mask, xs, (packed, partner))
    near, held = lax.optimization_barrier((near, held))
    across = leaf_xor(held, 2)
    own_core = leaf_xor(held, 1)
    both_ways = leaf_xor(across, 1)
    led, *partial = far_call(
        place, tile_mask, ridge, (left, right, relay), near, targets, coefs, lead
    )
    led = swap_cols(led)
    reduced = led.sum(0)
    e1, m2, f2, m3, e2 = nodes_call(place, (held, own_core, across, both_ways))

    columns = [partial[0]] + [col_shift(partial[d], d) for d in (1, 2, 3)]

    w1, p1 = level1_call(place, leaf_map, gather4(reduced, G4), node_inverse, node_transfer)
    p1 = lax.all_to_all(p1, "leaf", 0, 0, axis_index_groups=GK, tiled=True)
    p1 = p1.reshape(4, 32, RANK)
    r1 = p1[0] + p1[1] + (p1[2] + p1[3])
    w2, p2 = level2_call(siblings(r1), m2, e2)
    r2 = sum(siblings(p2))
    r2s = [r2, z_from(r2, -1, 1), z_from(r2, 2, -2), z_from(r2, -3, 3)]
    g1 = upper_call(r2s, m3, f2, w2)
    columns, g1 = lax.optimization_barrier((columns, g1))
    ordered, *pieces = residual_call(place, cluster_perm, columns)
    res_rows = [pieces[0]] + [col_shift(pieces[k], k) for k in (1, 2, 3)]
    g1 = gather4(g1, GK)
    pieces = gather4(down1_call(g1, e1, node_inverse, w1), G4)

    delta = finish_call(place, leaf_map, cluster_perm, pieces, ordered, leaf_basis, leaf_inverse)
    return outputs_call(place, res_rows, swap_cols(delta.reshape(4, Q, 128)), coefs)


def solution(mesh):
    return jax.shard_map(
        step,
        mesh=mesh,
        in_specs=(
            P(("leaf", "col"), None),
            P(("leaf", "col"), None),
            P(("leaf", "col"), None),
            P(),
            P("leaf", None),
            P("leaf", None),
            P(),
            P("leaf", None, None),
            P("leaf", None, None),
            P("leaf", None, None),
            P("leaf", None, None),
        ),
        out_specs=(P(("leaf", "col"), None), P(("leaf", "col"), None)),
        check_vma=False,
    )
```

```python
import jax
import jax.numpy as jnp
from jax import lax
from jax.experimental import pallas as pl
from jax.experimental.pallas import tpu as pltpu
from jax.sharding import PartitionSpec as P


F32 = jnp.float32
BF16 = jnp.bfloat16
Q = 256
RANK = 256
LEAVES = 64


def leaf_at(z, x_hi, kappa):
    x = 2 * x_hi + ((kappa >> 1) ^ x_hi)
    return z * 8 + x * 2 + (kappa & 1)


G4 = [[4 * n + k for k in range(4)] for n in range(16)]
GK = [[leaf_at(z, xh, k) for k in range(4)] for z in range(8) for xh in range(2)]


def facing(i, flip_x, flip_z):
    z, x, core = i // 8, i // 2 % 4, i % 2
    return (z ^ flip_z) * 8 + (3 - x if flip_x else x) * 2 + core


def leaf_route(value, target):
    return lax.ppermute(value, "leaf", [(i, target(i)) for i in range(LEAVES)])


def leaf_xor(value, bit):
    return leaf_route(value, lambda i: i ^ bit)


def leaf_from(value, step):
    return leaf_route(value, lambda i: (i - step) % LEAVES)


def siblings(value):
    return [value] + [
        leaf_route(value, lambda i, d=d: facing(i, d & 1, d >> 1)) for d in (1, 2, 3)
    ]


def z_from(value, even, odd):
    route = []
    for i in range(LEAVES):
        step = odd if i // 8 % 2 else even
        route.append(((i + 8 * step) % LEAVES, i))
    return lax.ppermute(value, "leaf", route)


def col_shift(value, step):
    return lax.ppermute(value, "col", [(i, (i + step) % 4) for i in range(4)])


def gather4(value, groups):
    return lax.all_gather(value, "leaf", axis=0, axis_index_groups=groups)


NN = ((1,), (0,))
NT = ((1,), (1,))


def dot(a, b, dims=NN):
    return lax.dot_general(a, b, (dims, ((), ())), preferred_element_type=F32)


def split(value):
    top = value.astype(BF16)
    return top, (value - top.astype(F32)).astype(BF16)


def dot3(a, b, dims=NN):
    at, al = split(a)
    bt, bl = split(b)
    return dot(at, bt, dims) + (dot(at, bl, dims) + dot(al, bt, dims))


SMEM = pl.BlockSpec(memory_space=pltpu.SMEM)
VMEM = pl.BlockSpec(memory_space=pltpu.VMEM)
HBM = pl.BlockSpec(memory_space=pltpu.HBM)


def near_memory(value):
    return pltpu.with_memory_space_constraint(value, pltpu.VMEM)


def far_memory(value):
    return pltpu.with_memory_space_constraint(value, pltpu.HBM)


def kernel(body, outs, values, scalars=(), scratch=(), far_values=(), far_outs=()):
    result = pl.pallas_call(
        body,
        in_specs=[SMEM] * len(scalars) + [VMEM] * len(values) + [HBM] * len(far_values),
        out_specs=[VMEM] * len(outs) + [HBM] * len(far_outs),
        out_shape=[pltpu.VMEM(shape, F32) for shape in outs]
        + [
            pltpu.HBM(*shape) if isinstance(shape[0], tuple) else pltpu.HBM(shape, F32)
            for shape in far_outs
        ],
        scratch_shapes=list(scratch),
        compiler_params=pltpu.CompilerParams(vmem_limit_bytes=20 << 20),
    )(*scalars, *[near_memory(value) for value in values], *[far_memory(value) for value in far_values])
    return result if len(outs) + len(far_outs) > 1 else result[0]


def like(*shape, dtype=F32):
    return jax.ShapeDtypeStruct(shape, dtype)


CHUNK = 512


def two_part(value):
    top, low = split(value)
    return jnp.concatenate([top, low], axis=1), top.astype(F32) + low.astype(F32)


def row_setup(place, xs, loaded, arrived, rows, norms):
    for k, ref in enumerate(xs):
        pltpu.make_async_copy(ref, loaded.at[k], arrived.at[k]).wait()
        at = (place[2] + 4 - k) % 4
        rows[at], exact = two_part(loaded[k])
        norms[at] = jnp.sum(exact * exact, axis=1, keepdims=True)


def block_setup(blocks, squares, others, tops, lows):
    for k, (y, a) in enumerate(blocks):
        others[k], exact = two_part(y)
        total = jnp.sum(exact * exact, axis=1, keepdims=True)
        squares[k] = jnp.transpose(jnp.broadcast_to(total, (Q, 128)))[:8]
        tops[k], lows[k] = split(a)


def tile_sum(i, weights, rows, norms, squares, others, tops, lows):
    x = rows[pl.ds(2 * i, 2)].reshape(CHUNK, 256)
    own = norms[pl.ds(2 * i, 2)].reshape(CHUNK, 1)
    total = None
    for k, weight in enumerate(weights):
        top, low = others[k][:, :128], others[k][:, 128:]
        inner = dot(x, jnp.concatenate([top, top], axis=1), NT)
        inner = inner + dot(x, jnp.concatenate([low, low], axis=1), NT)
        distance = own + squares[k][:1] - 2.0 * inner
        top, low = split(jnp.exp(distance * (-2.0 / 128.0)) * weight)
        term = dot(top, tops[k]) + dot(top, lows[k]) + dot(low, tops[k])
        total = term if total is None else total + term
    return total


def near_kernel(
    place, mask, p0, p1, x0, x1, x2, x3, out, rows_out, norms_out, loaded, arrived, rows, norms, *scratch
):
    xs = (x0, x1, x2, x3)
    for k, ref in enumerate(xs):
        pltpu.make_async_copy(ref, loaded.at[k], arrived.at[k]).start()
    block_setup([(p[:, :128], p[:, 128:]) for p in (p0, p1)], *scratch)
    row_setup(place, xs, loaded, arrived, rows, norms)
    copies = [
        pltpu.make_async_copy(rows, rows_out, arrived.at[4]),
        pltpu.make_async_copy(norms, norms_out, arrived.at[5]),
    ]
    for copy in copies:
        copy.start()
    weights = (mask[0, 2].astype(F32), mask[0, 3 - 2 * place[0]].astype(F32))

    @pl.loop(0, 2)
    def _(i):
        at = pl.ds(pl.multiple_of(i * CHUNK, CHUNK), CHUNK)
        out[at, :] = tile_sum(i, weights, rows, norms, *scratch)

    for copy in copies:
        copy.wait()


def far_kernel(
    place, mask, ridge, p0, p1, p2, near, own_y, own_a, lead, split_rows, norms,
    led, out0, out1, out2, out3, parts, sems, *scratch
):
    block_setup([(p[:, :128], p[:, 128:]) for p in (p0, p1, p2)], *scratch)
    weights = (
        mask[0, 0].astype(F32),
        mask[0, 4].astype(F32),
        mask[0, 1 + 2 * place[0]].astype(F32),
    )
    for k in range(4):
        led[k] = jnp.zeros((RANK, 128), F32)

    def sent(i):
        rows = pl.ds(pl.multiple_of(i * CHUNK, CHUNK), CHUNK)
        return [
            pltpu.make_async_copy(
                parts.at[i, (place[2] + d) % 4], out.at[rows, :], sems.at[i, d]
            )
            for d, out in enumerate((out0, out1, out2, out3))
        ]

    @pl.loop(0, 2)
    def _(i):
        rows = pl.ds(pl.multiple_of(i * CHUNK, CHUNK), CHUNK)
        total = near[rows, :] + tile_sum(i, weights, split_rows, norms, *scratch)
        own = own_y[...] - ridge[0] * own_a[...]
        part = jnp.concatenate(
            [
                jnp.where(place[2] == 2 * i + h, own, 0.0) - total[h * Q : (h + 1) * Q]
                for h in range(2)
            ],
            axis=0,
        )
        product = dot3(lead[:, rows], part)
        for k in range(4):
            parts[i, k] = part[:, k * 128 : (k + 1) * 128]
            led[k] += product[:, k * 128 : (k + 1) * 128]
        for copy in sent(i):
            copy.start()

    for i in range(2):
        for copy in sent(i):
            copy.wait()


def block_scratch(count):
    return [
        pltpu.VMEM((count, 8, Q), F32),
        pltpu.VMEM((count, Q, 256), BF16),
        pltpu.VMEM((count, Q, 512), BF16),
        pltpu.VMEM((count, Q, 512), BF16),
    ]


def near_call(place, mask, xs, blocks):
    return kernel(
        near_kernel,
        [(1024, 512)],
        blocks,
        (place, mask),
        [
            pltpu.VMEM((4, Q, 128), F32),
            pltpu.SemaphoreType.DMA((6,)),
            pltpu.VMEM((4, Q, 256), BF16),
            pltpu.VMEM((4, Q, 1), F32),
        ]
        + block_scratch(2),
        xs,
        [((4, Q, 256), BF16), (4, Q, 1)],
    )


def far_call(place, mask, ridge, blocks, near, own_y, own_a, lead):
    near, rows, norms = near
    return kernel(
        far_kernel,
        [(4, RANK, 128)],
        [*blocks, near, own_y, own_a, lead, rows, norms],
        (place, mask, ridge),
        [pltpu.VMEM((2, 4, CHUNK, 128), F32), pltpu.SemaphoreType.DMA((2, 4))]
        + block_scratch(3),
        far_outs=[(1024, 128)] * 4,
    )


def picks_by_row(order, picks):
    at = lax.broadcasted_iota(jnp.int32, picks.shape, 0)
    picks[...] = jnp.where(order == at, 1.0, 0.0).astype(BF16)


def load_solve(basis, solve, basis_in, solve_in, sems):
    copies = [pltpu.make_async_copy(basis.at[0], basis_in, sems.at[4])]
    for k in range(4):
        rows = pl.ds(k * Q, Q)
        copies.append(
            pltpu.make_async_copy(solve.at[0, rows, :], solve_in.at[rows, :], sems.at[k])
        )
    for copy in copies:
        copy.start()
    return copies


SOLVE_SCRATCH = [
    pltpu.VMEM((1024, RANK), F32),
    pltpu.VMEM((1024, 1024), F32),
    pltpu.SemaphoreType.DMA((5,)),
]


def lead_kernel(order, basis, solve, lead, basis_in, solve_in, sems, picks, turned):
    first, *rest = load_solve(basis, solve, basis_in, solve_in, sems)
    picks_by_row(order[...], picks)
    first.wait()
    turned[...] = jnp.transpose(basis_in[...])
    for k in range(4):
        rest[k].wait()
        rows = slice(k * Q, (k + 1) * Q)
        term = dot3(turned[:, rows], solve_in[rows, :])
        if k:
            lead[...] += term
        else:
            lead[...] = term
    both = jnp.concatenate(split(lead[...]), axis=0)
    chosen = dot(both, picks[...], NT)
    lead[...] = chosen[:RANK] + chosen[RANK:]


def lead_call(order, leaf_basis, leaf_inverse):
    return kernel(
        lead_kernel,
        [(RANK, 1024)],
        [order],
        scratch=SOLVE_SCRATCH
        + [pltpu.VMEM((1024, 1024), BF16), pltpu.VMEM((RANK, 1024), F32)],
        far_values=[leaf_basis, leaf_inverse],
    )


def run_copies(sems, moves):
    copies = [
        pltpu.make_async_copy(source, target, sems.at[k])
        for k, (source, target) in enumerate(moves)
    ]
    for copy in copies:
        copy.start()
    for copy in copies:
        copy.wait()


def pack_kernel(a, b, out, buffer, sems):
    run_copies(sems, [(a, buffer.at[:, pl.ds(0, 128)]), (b, buffer.at[:, pl.ds(128, 512)])])
    run_copies(sems, [(buffer, out)])


def slices_kernel(transfer, inverse, out, buffer, sems):
    moves = [(transfer.at[0, pl.ds(256, 64), :], buffer.at[pl.ds(0, 64), :])]
    for k in range(4):
        source = inverse.at[0, pl.ds(320, 16), pl.ds(k * 256, 256)]
        moves.append((source, buffer.at[pl.ds(64 + k * 16, 16), :]))
    run_copies(sems, moves)
    run_copies(sems, [(buffer, out)])


def assemble(body, shape, count, *parts):
    return kernel(
        body,
        [],
        [],
        scratch=[pltpu.VMEM(shape, F32), pltpu.SemaphoreType.DMA((count,))],
        far_values=parts,
        far_outs=[shape],
    )


def pair_kernel(slices, lower, out):
    out[:128, :] = slices[...]
    out[128:, :] = lower[...]


def held_kernel(pair, mirrored, transfer, inverse, out, buffer, sems):
    moves = [(transfer.at[0, pl.ds(0, 256), :], buffer.at[pl.ds(0, 256), :])]
    for k in range(4):
        source = inverse.at[0, pl.ds(256, 64), pl.ds(k * 256, 256)]
        moves.append((source, buffer.at[pl.ds(256 + k * 64, 64), :]))
    copies = [
        pltpu.make_async_copy(source, target, sems.at[k])
        for k, (source, target) in enumerate(moves)
    ]
    for copy in copies:
        copy.start()
    buffer[512:768, :] = pair[...]
    buffer[768:, :] = mirrored[...]
    for copy in copies:
        copy.wait()
    run_copies(sems, [(buffer, out)])


def held_call(pair, mirrored, transfer, inverse):
    return kernel(
        held_kernel,
        [],
        [pair, mirrored],
        scratch=[pltpu.VMEM((1024, 256), F32), pltpu.SemaphoreType.DMA((5,))],
        far_values=[transfer, inverse],
        far_outs=[(1024, 256)],
    )


def nodes_kernel(place, b0, b1, b2, b3, e1, m2, f2, m3, own_e2, e2):
    q = place[3] % 4
    child = place[3] // 4 % 4
    parent = place[3] // 16
    odd = place[3] // 8 % 2
    for d, block in enumerate((b0, b1, b2, b3)):
        at = q ^ d
        e1[pl.ds(pl.multiple_of(at * 256, 256), 256), :] = block[:256, :]
        rows = pl.ds(pl.multiple_of(at * 64, 64), 64)
        for k in range(4):
            source = pl.multiple_of(256 + (child ^ k) * 64, 64)
            m2[rows, k * 256 : (k + 1) * 256] = block[pl.ds(source, 64), :]
        for s, (start, flip) in enumerate(((512, 0), (768, 2), (640, 0), (896, 2))):
            held = at ^ flip
            e2[pl.ds(pl.multiple_of(s * 256 + held * 64, 64), 64), :] = block[
                start : start + 64, :
            ]
            rows = pl.ds(pl.multiple_of((child ^ s) * 64 + held * 16, 16), 16)
            for k in range(4):
                step = (0, 3, 1, 2)[k] + odd * (0, -2, 2, 0)[k]
                source = pl.multiple_of(start + 64 + (parent + step) % 4 * 16, 16)
                m3[rows, k * 256 : (k + 1) * 256] = block[pl.ds(source, 16), :]
    own_e2[...] = e2[:256, :]
    f2[...] = dot3(m2[...], e2[...])


def nodes_call(place, blocks):
    return kernel(
        nodes_kernel,
        [(1024, 256), (256, 1024), (256, 256), (256, 1024), (256, 256)],
        blocks,
        (place,),
        [pltpu.VMEM((1024, 256), F32)],
    )


def level1_kernel(place, leaf_map, stacked, m1, e1, w1, p1):
    base = place[3] // 4 * 4
    total = None
    for k in range(4):
        term = dot3(m1[0, :256, k * 256 : (k + 1) * 256], stacked[leaf_map[base + k] - base])
        total = term if total is None else total + term
    w1[...] = total
    p1[...] = dot3(jnp.transpose(total), e1[0, :256, :])


def level1_call(place, leaf_map, stacked, node_inverse, node_transfer):
    return kernel(
        level1_kernel,
        [(256, 128), (128, 256)],
        [stacked, node_inverse, node_transfer],
        (place, leaf_map),
    )


def row_blocks(parts, matrix):
    total = None
    for k, part in enumerate(parts):
        term = dot3(part[...], matrix[:, k * 256 : (k + 1) * 256], NT)
        total = term if total is None else total + term
    return total


def level2_kernel(r0, r1, r2, r3, m2, e2, w2, p2):
    total = row_blocks((r0, r1, r2, r3), m2)
    w2[...] = total
    p2[...] = dot3(total, e2[...])


def level2_call(parts, m2, e2):
    return kernel(level2_kernel, [(32, 256), (32, 256)], [*parts, m2, e2])


def upper_kernel(r0, r1, r2, r3, m3, f2, w2, g1):
    g2 = row_blocks((r0, r1, r2, r3), m3)
    g1[...] = w2[...] - dot3(g2, f2[...], NT)


def upper_call(parts, m3, f2, w2):
    return kernel(upper_kernel, [(32, 256)], [*parts, m3, f2, w2])


def down1_kernel(g1, e1, m1, w1, v1, e1_in, m1_in, w1_in, sems):
    copies = [
        pltpu.make_async_copy(e1, e1_in, sems.at[0]),
        pltpu.make_async_copy(m1.at[0, pl.ds(0, 256), :], m1_in, sems.at[1]),
        pltpu.make_async_copy(w1, w1_in, sems.at[2]),
    ]
    for copy in copies:
        copy.start()
    g = g1[...].reshape(128, 256)
    copies[0].wait()
    lifted = dot3(g, e1_in[...], NT)
    copies[1].wait()
    copies[2].wait()
    v1[...] = w1_in[...] - dot3(m1_in[...], lifted, NT)


def down1_call(g1, e1, node_inverse, w1):
    return kernel(
        down1_kernel,
        [(256, 128)],
        [g1],
        scratch=[
            pltpu.VMEM((1024, 256), F32),
            pltpu.VMEM((256, 1024), F32),
            pltpu.VMEM((256, 128), F32),
            pltpu.SemaphoreType.DMA((3,)),
        ],
        far_values=[e1, node_inverse, w1],
    )


def residual_kernel(
    place, order, p0, p1, p2, p3, ordered_out, out0, out1, out2, out3, picks, res, ordered, sems
):
    res_sum = p0[...] + p1[...] + (p2[...] + p3[...])
    res[...] = res_sum
    rows = jnp.broadcast_to(order[...].astype(F32), (128, 1024))
    holds = jnp.transpose(rows)[:, :1].astype(jnp.int32)
    at = lax.broadcasted_iota(jnp.int32, (1024, 1024), 1)
    picks[...] = jnp.where(holds == at, 1.0, 0.0).astype(BF16)
    both = dot(picks[...], jnp.concatenate(split(res_sum), axis=1))
    ordered[...] = both[:, :128] + both[:, 128:]
    moves = [(ordered, ordered_out)]
    for k, out in enumerate((out0, out1, out2, out3)):
        rows = pl.ds(pl.multiple_of((place[2] + k) % 4 * Q, Q), Q)
        moves.append((res.at[rows, :], out))
    run_copies(sems, moves)


def residual_call(place, order, parts):
    return kernel(
        residual_kernel,
        [],
        [order, *parts],
        (place,),
        [
            pltpu.VMEM((1024, 1024), BF16),
            pltpu.VMEM((1024, 128), F32),
            pltpu.VMEM((1024, 128), F32),
            pltpu.SemaphoreType.DMA((5,)),
        ],
        far_outs=[(1024, 128)] + [(Q, 128)] * 4,
    )


def finish_kernel(
    place, leaf_map, order, pieces, ordered, basis, solve, delta, solve_in, sems, picks, rhs, sides
):
    rest = []
    for k in range(4):
        rows = pl.ds(k * Q, Q)
        rest.append(pltpu.make_async_copy(solve.at[0, rows, :], solve_in.at[rows, :], sems.at[k]))
    for copy in rest:
        copy.start()
    base = place[3] // 4 * 4
    slot = jnp.int32(3)
    for k in range(3):
        slot = jnp.where(leaf_map[base + k] == place[3], k, slot)
    picks_by_row(order[...], picks)
    rhs[...] = jnp.concatenate(split(ordered[...] - dot3(basis[0], pieces[slot])), axis=1)
    for k in range(4):
        rest[k].wait()
        rows = slice(k * Q, (k + 1) * Q)
        a, b = split(solve_in[rows, :])
        both = dot(a, rhs[...])
        y = both[:, :128] + (both[:, 128:] + dot(b, rhs[:, :128]))
        sides[rows, :] = jnp.concatenate(split(y), axis=1)

    @pl.loop(0, 2)
    def _(i):
        rows = pl.ds(pl.multiple_of(i * CHUNK, CHUNK), CHUNK)
        both = dot(picks[rows, :], sides[...])
        delta[rows, :] = both[:, :128] + both[:, 128:]


def finish_call(place, leaf_map, order, pieces, ordered, leaf_basis, leaf_inverse):
    return kernel(
        finish_kernel,
        [(1024, 128)],
        [order, pieces, ordered, leaf_basis],
        (place, leaf_map),
        SOLVE_SCRATCH[1:]
        + [
            pltpu.VMEM((1024, 1024), BF16),
            pltpu.VMEM((1024, 256), BF16),
            pltpu.VMEM((1024, 256), BF16),
        ],
        [leaf_inverse],
    )


def outputs_kernel(place, r0, r1, r2, r3, delta, coefs, out_res, out_new):
    for k, res in enumerate((r0, r1, r2, r3)):
        at = slice(k * 128, (k + 1) * 128)
        out_new[:, at] = coefs[:, at] + delta[k]
        source = pl.multiple_of((place[2] + 4 - k) % 4 * 128, 128)
        out_res[:, pl.ds(source, 128)] = res[...]


def outputs_call(place, res, delta, coefs):
    return pl.pallas_call(
        outputs_kernel,
        in_specs=[SMEM] + [VMEM] * 6,
        out_shape=[like(Q, 512), like(Q, 512)],
        compiler_params=pltpu.CompilerParams(vmem_limit_bytes=8 << 20),
        name="outputs",
    )(place, *[near_memory(value) for value in (*res, delta, coefs)])


def swap_cols(value):
    return lax.all_to_all(value, "col", 0, 0, tiled=True)


def step(
    points,
    coefs,
    targets,
    ridge,
    tile_mask,
    cluster_perm,
    leaf_map,
    leaf_inverse,
    leaf_basis,
    node_inverse,
    node_transfer,
):
    col = lax.axis_index("col")
    leaf = lax.axis_index("leaf")
    core = leaf % 2
    place = jnp.stack([core, leaf // 2 % 2, col, leaf]).astype(jnp.int32)

    xs = [points] + [col_shift(points, d) for d in (1, 2, 3)]
    packed = assemble(pack_kernel, (Q, 640), 2, points, coefs)
    left, right = leaf_from(packed, -2), leaf_from(packed, 2)
    partner = leaf_xor(packed, 1)
    relay = leaf_xor(jnp.where(core == 0, right, left), 1)

    nodes = (node_transfer, node_inverse)
    slices = assemble(slices_kernel, (128, 256), 5, *nodes)
    lower = leaf_route(slices, lambda i: facing(i, 0, 1))
    pair = kernel(pair_kernel, [(256, 256)], [slices, lower])
    mirrored = leaf_route(pair, lambda i: facing(i, 1, 0))
    held = held_call(pair, mirrored, *nodes)

    lead = lead_call(cluster_perm, leaf_basis, leaf_inverse)

    near = near_call(place, tile_mask, xs, (packed, partner))
    near, held = lax.optimization_barrier((near, held))
    across = leaf_xor(held, 2)
    own_core = leaf_xor(held, 1)
    both_ways = leaf_xor(across, 1)
    led, *partial = far_call(
        place, tile_mask, ridge, (left, right, relay), near, targets, coefs, lead
    )
    led = swap_cols(led)
    reduced = led.sum(0)
    e1, m2, f2, m3, e2 = nodes_call(place, (held, own_core, across, both_ways))

    columns = [partial[0]] + [col_shift(partial[d], d) for d in (1, 2, 3)]

    w1, p1 = level1_call(place, leaf_map, gather4(reduced, G4), node_inverse, node_transfer)
    p1 = lax.all_to_all(p1, "leaf", 0, 0, axis_index_groups=GK, tiled=True)
    p1 = p1.reshape(4, 32, RANK)
    r1 = p1[0] + p1[1] + (p1[2] + p1[3])
    w2, p2 = level2_call(siblings(r1), m2, e2)
    r2 = sum(siblings(p2))
    r2s = [r2, z_from(r2, -1, 1), z_from(r2, 2, -2), z_from(r2, -3, 3)]
    g1 = upper_call(r2s, m3, f2, w2)
    columns, g1 = lax.optimization_barrier((columns, g1))
    ordered, *pieces = residual_call(place, cluster_perm, columns)
    res_rows = [pieces[0]] + [col_shift(pieces[k], k) for k in (1, 2, 3)]
    g1 = gather4(g1, GK)
    pieces = gather4(down1_call(g1, e1, node_inverse, w1), G4)

    delta = finish_call(place, leaf_map, cluster_perm, pieces, ordered, leaf_basis, leaf_inverse)
    return outputs_call(place, res_rows, swap_cols(delta.reshape(4, Q, 128)), coefs)


def solution(mesh):
    return jax.shard_map(
        step,
        mesh=mesh,
        in_specs=(
            P(("leaf", "col"), None),
            P(("leaf", "col"), None),
            P(("leaf", "col"), None),
            P(),
            P("leaf", None),
            P("leaf", None),
            P(),
            P("leaf", None, None),
            P("leaf", None, None),
            P("leaf", None, None),
            P("leaf", None, None),
        ),
        out_specs=(P(("leaf", "col"), None), P(("leaf", "col"), None)),
        check_vma=False,
    )
```
